128 devices in a mesh: fib: 8 (over y, core), len: 4 (over x), emg: 4 (over z).
Axes of the slice: x: 4, y: 4, z: 4, core: 2. Of those that a mesh axis runs over, the one named last changes fastest.
Arguments:
- states: float32 [57, 256, 4096], P(None, 'len', ('fib', 'emg')), may hold values from -6 to 6
- voltage: float32 [256, 4096], P('len', ('fib', 'emg')), may hold values from -6 to 6
- coupling: float32 [57, 57], replicated, may hold values from -0.75 to 0.75
- decay_rates: float32 [57], replicated, may hold values from 0.05 to 1.9
- volt_gain: float32 [57], replicated, may hold values from -4 to 4
- current_weights: float32 [57], replicated, may hold values from -0.75 to 0.75
- fibre_home: int32 [4096, 1], P(('fib', 'emg')), may hold values from 0 to 31; in each aligned block of 128 rows (0 to 127, 128 to 255, ...) at most 12 rows name the same one
- cross_cell: int32 [4096], P(('fib', 'emg')), may hold values from 0 to 1023
- motor_unit: int32 [4096], P(('fib', 'emg')), may hold values from 0 to 99
- stim_step: int32 [100], replicated, may hold values from 0 to 2
- tissue: float32 [128, 64, 512], P('len', 'fib', 'emg'), may hold values from 0.5 to 2
Outputs:
- states_out: float32 [57, 256, 4096], P(None, 'len', ('fib', 'emg'))
- voltage_out: float32 [256, 4096], P('len', ('fib', 'emg'))
- potential: float32 [2, 128, 64, 512], P(None, 'len', 'fib', 'emg')
The draws below stay inside these ranges and needn't reach their ends.
Inputs may be any that keep to these rules, and one draw needn't show every extreme that they name: `fibre_home`: the fibres of one fib and emg index name any one brick column at most 12 times, and some brick column is named exactly 12 times by the fibres of some index. `stim_step`: A value of 2 means the motor unit does not fire in this window.
All inputs are finite; a program needn't handle non-finite values.
Results may differ from the reference program's by a relative error of at most 0.0003.
Values sent between devices are 32-bit elements; how exact they have to be, the bound alone decides.
A program may use at most 64 MiB of HBM per device.

```python
import math
import jax
import jax.numpy as jnp
import numpy as np
from jax import lax

STATES = 57
MU = 100
STEPS = 2
SWEEPS = 4
NPC = 2
FIB_DEV = 128
BY = 8
BZ = 128
FIBRES = 4096
NODES = 256
GX = 128
GY = 64
GZ = 512
N_FIB = 8
N_EMG = 4


def touch_ends(result, stream_key, low, largest):
    dims = result.shape
    spot = [jax.random.randint(jax.random.fold_in(stream_key, axis), (), 0, dims[axis]) for axis in range(len(dims))]
    result = result.at[tuple(spot)].set(low)
    longest = dims.index(max(dims))
    spot[longest] = (spot[longest] + 1) % dims[longest]
    return result.at[tuple(spot)].set(largest)


def shard_levels(rng, shape, pieces, smallest, high):
    loudness = 1.0
    for dim, shards_of in pieces:
        draws = jax.random.uniform(jax.random.fold_in(jax.random.fold_in(rng, 6), dim), (shards_of,), jnp.float32, smallest / len(pieces), high / len(pieces))
        loudness = loudness * jnp.repeat(jnp.exp(draws), shape[dim] // shards_of).reshape((-1,) + (1,) * (len(shape) - 1 - dim))
    return loudness


def rank_bounds(number_of, lean):
    portions = [(1 << 20) // math.isqrt(standing ** lean) + 1 for standing in range(1, number_of + 1)]
    deviation = 1 + sum(portions) // (1 << 30)
    return np.cumsum(np.array([max(1, weight // deviation) for weight in portions]))


def skewed_ids(rng, dims, amount, lean):
    table = rank_bounds(amount, lean)
    lot = jax.random.randint(jax.random.fold_in(rng, 1), dims, 0, int(table[amount - 1]))
    grade = jnp.searchsorted(jnp.asarray(table, jnp.int32), lot, side="right")
    return jax.random.permutation(jax.random.fold_in(rng, 2), amount)[grade].astype(jnp.int32)


def shared_out(rng, own, number, rows, number_of, top, reach, lean):
    order = jax.random.permutation(rng, number_of)
    heavy_load, usual = portions_of(number_of, rows * top, reach, lean, True), portions_of(number_of, rows * top, reach, lean, False)
    places = jnp.arange(number_of)

    def named(lengths, rotation):
        used = int((lengths > 0).sum())
        fixed = max(1, used // 4)
        moved = fixed + (places - fixed + rotation * (used - fixed)) % max(1, number_of - fixed)
        return jnp.zeros((number_of,), jnp.int32).at[order[jnp.where(places < fixed, places, moved)]].set(jnp.asarray(lengths, jnp.int32))

    lengths = jnp.where(number % 4 == 0, named(heavy_load, number // 4), named(usual, number - number // 4 - 1))
    mixed = jax.random.permutation(jax.random.fold_in(own, 3), number_of)
    donor, taker = mixed[0:number_of // 2 * 2:2], mixed[1:number_of // 2 * 2:2]
    room = jnp.minimum(lengths[donor] - 1, reach - lengths[taker]) // 2
    room = jnp.where((donor == order[0]) | (taker == order[0]) | (lengths[taker] == 0), 0, jnp.maximum(room, 0))
    moved = jax.random.randint(jax.random.fold_in(own, 4), (number_of // 2,), 0, 1 << 20) % (room + 1)
    lengths = lengths.at[donor].add(-moved).at[taker].add(moved)
    items = jnp.searchsorted(jnp.cumsum(lengths), jnp.arange(rows * top), side="right").astype(jnp.int32)
    listing = items.reshape(top, rows).T
    listing = listing[jax.random.permutation(jax.random.fold_in(own, 1), rows)]
    rotation = jax.random.randint(jax.random.fold_in(own, 2), (rows, 1), 0, top)
    return jnp.take_along_axis(listing, (jnp.arange(top)[None, :] + rotation) % top, axis=1)


def portions_of(count, total, bound, slope, full):
    portions = [(1 << 20) // math.isqrt(standing ** slope) + 1 for standing in range(1, count + 1)]
    largest = bound if full else min(bound, max(-(-total // count), total * portions[0] // sum(portions)))
    least = 1 if total - largest >= count - 1 else 0
    counts, spare = [largest] + [least] * (count - 1), total - largest - least * (count - 1)
    while spare > 0:
        free = [i for i in range(1, count) if counts[i] < largest] or [i for i in range(1, count) if counts[i] < bound]
        pool, remaining = sum([portions[i] for i in free]), spare
        for i in free:
            addition = min(bound - counts[i], max(1, remaining * portions[i] // pool), spare)
            counts[i] = counts[i] + addition
            spare = spare - addition
    return np.array(counts)


def scatter_about(own_key, extent, scale, bound, split=(), kind=jnp.bfloat16):
    level = shard_levels(own_key, extent, split, -0.22, 0.18) if split else 1.0
    entries = jax.random.normal(own_key, extent, jnp.float32) * scale * level
    return jnp.minimum(jnp.maximum(entries, -bound), bound).astype(kind)


def setup_inputs(seed: int = 0) -> dict:
    key_of = jax.random.split(jax.random.key(seed), 12)
    states = scatter_about(key_of[0], (STATES, NODES, FIBRES), 1.0, 6.0, ((1, 4), (2, 32)), jnp.float32)
    voltage = scatter_about(key_of[1], (NODES, FIBRES), 1.0, 6.0, ((0, 4), (1, 32)), jnp.float32)
    coupling = scatter_about(key_of[2], (STATES, STATES), STATES ** -0.5, 0.75, (), jnp.float32)
    decay_rates = jnp.clip(jnp.exp(jax.random.uniform(key_of[3], (STATES,), jnp.float32, math.log(0.05), math.log(1.9))), 0.05, 1.9)
    volt_gain = scatter_about(key_of[4], (STATES,), 1.0, 4.0, (), jnp.float32)
    current_weights = scatter_about(key_of[5], (STATES,), STATES ** -0.5, 0.75, (), jnp.float32)
    fibre_home_keys = jax.random.split(jax.random.fold_in(key_of[6], 1), FIBRES // FIB_DEV)
    fibre_home_turns = jax.random.permutation(jax.random.fold_in(key_of[6], 3), FIBRES // FIB_DEV)
    fibre_home = jax.vmap(lambda own, number: shared_out(jax.random.fold_in(key_of[6], 2), own, number, FIB_DEV, N_FIB * N_EMG, 1, 3 * FIB_DEV // (N_FIB * N_EMG), 2))(fibre_home_keys, fibre_home_turns).reshape((FIBRES, 1))
    cross_cell = touch_ends(jax.random.randint(key_of[7], (FIBRES,), 0, BY * BZ), jax.random.fold_in(key_of[7], 1), 0, (BY * BZ) - 1).astype(jnp.int32)
    motor_unit = touch_ends(skewed_ids(key_of[8], (FIBRES,), MU, 2), jax.random.fold_in(key_of[8], 3), 0, MU - 1).astype(jnp.int32)
    stim_step = touch_ends(jax.random.randint(key_of[9], (MU,), 0, STEPS + 1), jax.random.fold_in(key_of[9], 1), 0, STEPS).astype(jnp.int32)
    tissue = jnp.clip(0.5 + 1.5 * jax.random.uniform(key_of[10], (GX, GY, GZ), jnp.float32) ** shard_levels(key_of[10], (GX, GY, GZ), ((0, 4), (1, 8), (2, 4)), -0.2, 0.2), 0.5, 2.0)
    return dict(states=states, voltage=voltage, coupling=coupling, decay_rates=decay_rates, volt_gain=volt_gain, current_weights=current_weights, fibre_home=fibre_home, cross_cell=cross_cell, motor_unit=motor_unit, stim_step=stim_step, tissue=tissue)


time_step = 0.5
conductance = 2000.0
amplitude = 200.0
band_half = 4
low_bound = 0.5
high_bound = 14.0

def cable_solve(right_side):
    length_nodes = right_side.shape[0]
    node_index = jnp.arange(length_nodes)
    main_diag = jnp.where((node_index == 0) | (node_index == length_nodes - 1), 1.0 + conductance, 1.0 + 2.0 * conductance).astype(jnp.float32)
    sub_diag = jnp.where(node_index == 0, 0.0, -conductance).astype(jnp.float32)
    super_diag = jnp.where(node_index == length_nodes - 1, 0.0, -conductance).astype(jnp.float32)
    return lax.linalg.tridiagonal_solve(sub_diag, main_diag, super_diag, right_side)

def stencil(values, tissue):
    padded = jnp.pad(values, 1)
    beside = padded[2:, 1:-1, 1:-1] + padded[:-2, 1:-1, 1:-1]
    beside = beside + padded[1:-1, 2:, 1:-1] + padded[1:-1, :-2, 1:-1]
    beside = beside + padded[1:-1, 1:-1, 2:] + padded[1:-1, 1:-1, :-2]
    return (6.0 + tissue) * values - beside

def chebyshev(source, tissue):
    middle = 0.5 * (high_bound + low_bound)
    spread = 0.5 * (high_bound - low_bound)
    ratio_value = middle / spread
    weight_now = 1.0 / ratio_value
    solution = jnp.zeros_like(source)
    residual = source
    direction = source / middle
    for sweep_index in range(SWEEPS):
        solution = solution + direction
        if sweep_index + 1 < SWEEPS:
            residual = residual - stencil(direction, tissue)
            weight_next = 1.0 / (2.0 * ratio_value - weight_now)
            direction = weight_next * weight_now * direction + 2.0 * weight_next / spread * residual
            weight_now = weight_next
    return solution

def reference(states, voltage, coupling, decay_rates, volt_gain, current_weights, fibre_home, cross_cell, motor_unit, stim_step, tissue):
    node_index = jnp.arange(NODES)
    band_mask = ((node_index >= NODES // 2 - band_half) & (node_index < NODES // 2 + band_half)).astype(jnp.float32)
    fire_step = stim_step[motor_unit]
    home_brick = fibre_home[:, 0]
    grid_row = home_brick // N_EMG * BY + cross_cell // BZ
    grid_column = home_brick % N_EMG * BZ + cross_cell % BZ
    flat_cell = (grid_row * GZ + grid_column).astype(jnp.int32)
    potentials = []
    for step_index in range(STEPS):
        drive_term = jnp.einsum('ij,jnf->inf', coupling, states, precision=lax.Precision.HIGHEST) + volt_gain[:, None, None] * voltage[None]
        states = states + time_step * (jnp.tanh(drive_term) - decay_rates[:, None, None] * states)
        current = jnp.einsum('i,inf->nf', current_weights, states, precision=lax.Precision.HIGHEST)
        active = (fire_step == step_index).astype(jnp.float32)
        right_side = voltage + time_step * (amplitude * band_mask[:, None] * active[None, :] - current)
        voltage = cable_solve(right_side)
        binned = current.reshape(GX, NPC, FIBRES).sum(axis=1)
        source = jnp.zeros((GX, GY * GZ), jnp.float32).at[:, flat_cell].add(binned).reshape(GX, GY, GZ)
        potentials.append(chebyshev(source, tissue))
    return (states, voltage, jnp.stack(potentials))
```

```python
import math

import jax
import jax.numpy as jnp
import numpy as np
from jax import lax
from jax.experimental import pallas as pl
from jax.experimental.pallas import tpu as pltpu
from jax.sharding import PartitionSpec as P

STEPS = 2
SWEEPS = 4
NPC = 2

time_step = 0.5
conductance = 2000.0
amplitude = 200.0
band_half = 4
low_bound = 0.5
high_bound = 14.0

MESH = pl.DeviceIdType.MESH
HIGH = lax.Precision.HIGHEST
F32 = jnp.float32
BF16 = jnp.bfloat16

N_FIB, N_LEN, N_EMG = 8, 4, 4
GROUPS = N_FIB * N_EMG
STATES = 57
ROWS = 64
NODES = 64
FIB = 128
BINS = NODES // NPC
BY, BZ = 8, 128
SLOT_ROWS = 4
CAPACITY = 12
FACE_ROWS = 112


def cable_tables():
    total = NODES * N_LEN
    theta = math.acosh(1.0 + 0.5 / conductance)
    scale = conductance * math.sinh(theta) * math.sinh(total * theta)
    u = np.array([math.cosh((i + 0.5) * theta) for i in range(total)])
    v = np.array([math.cosh((total - 0.5 - i) * theta) / scale for i in range(total)])
    index = np.arange(NODES)
    local = np.zeros((N_LEN, NODES + 8, NODES))
    far = np.zeros((N_LEN, NODES, 8 * N_LEN))
    for shard in range(N_LEN):
        us, vs = u[shard * NODES :][:NODES], v[shard * NODES :][:NODES]
        low = index[:, None] <= index[None, :]
        local[shard, :NODES] = np.where(low, us[:, None] * vs[None, :], vs[:, None] * us[None, :])
        local[shard, NODES] = us
        local[shard, NODES + 1] = vs
        for other in range(N_LEN):
            if other < shard:
                far[shard, :, 8 * other] = vs
            if other > shard:
                far[shard, :, 8 * other + 1] = us
    return jnp.asarray(local, F32), jnp.asarray(far, F32)


def iota(shape, axis):
    return lax.broadcasted_iota(jnp.int32, shape, axis)


def split(values):
    high = values.astype(BF16)
    return high, (values - high.astype(F32)).astype(BF16)


def dot(a, b):
    return jnp.dot(a, b, preferred_element_type=F32)


def dot_high(a, b):
    return jnp.dot(a, b, preferred_element_type=F32, precision=HIGH)


def dot_t(a, b, precision=None):
    return lax.dot_general(
        a, b, (((1,), (1,)), ((), ())), preferred_element_type=F32, precision=precision
    )


def dot_tl(a, b, precision=None):
    return lax.dot_general(
        a, b, (((0,), (0,)), ((), ())), preferred_element_type=F32, precision=precision
    )


def kernel(
    states_hbm, volt_ref, coup_ref, decay_ref, gain_ref, wts_ref, home_ref, cell_ref, mu_ref,
    stim_ref, tissue_ref, local_ref, far_ref,
    states_out, volt_out, pot_out,
    s_in, s_work, s_new, lhs_ref, keep_ref, gain_b, wts_b, cur_ref, v1_ref, hot_ref, sel_ref,
    cell_send, cell_recv, row_send, row_recv, end_send, end_recv, face_send, face_recv,
    d_ref, r_ref, x_ref, hy_ref, hz_ref,
    in_sem, out_sem, a2a_send, a2a_recv, len_send, len_recv, face_ssem, face_rsem,
):
    fib, shard, emg = lax.axis_index("fib"), lax.axis_index("len"), lax.axis_index("emg")
    me = fib * N_EMG + emg

    quarter = NODES // 4
    loads = []
    for part in range(4):
        window = pl.ds(part * quarter, quarter)
        copy = pltpu.make_async_copy(
            states_hbm.at[:, window, :], s_in.at[pl.ds(0, STATES), window, :], in_sem.at[part]
        )
        copy.start()
        loads.append(copy)

    barrier = pltpu.get_barrier_semaphore()

    def peer(step):
        other = lax.rem(me + step, GROUPS)
        return {"fib": other // N_EMG, "len": shard, "emg": lax.rem(other, N_EMG)}, other

    def greet(step, _):
        device, _other = peer(step)
        pl.semaphore_signal(barrier, inc=1, device_id=device, device_id_type=MESH)
        return 0

    lax.fori_loop(1, GROUPS, greet, 0)
    for step in range(1, N_LEN):
        other = lax.rem(shard + step, N_LEN)
        pl.semaphore_signal(
            barrier, inc=1, device_id={"fib": fib, "len": other, "emg": emg}, device_id_type=MESH
        )

    def column(row):
        wide = row.shape[1]
        picked = jnp.where(iota((ROWS, wide), 0) == iota((ROWS, wide), 1), row, 0.0)
        return dot_high(picked, jnp.ones((wide, FIB), F32))

    keep_ref[...] = 1.0 - time_step * column(decay_ref[...])
    gain_b[...] = column(gain_ref[...])
    wts_b[...] = column(wts_ref[...])
    spread = (iota((STATES, 3 * ROWS), 0) == lax.rem(iota((STATES, 3 * ROWS), 1), ROWS)).astype(F32)
    tiled = dot_high(coup_ref[...], spread)
    tiled = jnp.concatenate([tiled, jnp.zeros((ROWS - STATES, 3 * ROWS), F32)], axis=0)
    weights = dot_high(wts_ref[...], spread)
    tiled = jnp.where(iota((ROWS, 3 * ROWS), 0) == STATES, weights, tiled)
    high, low = split(tiled)
    lhs_ref[...] = jnp.where(iota((ROWS, 3 * ROWS), 1) < 2 * ROWS, high.astype(F32), low.astype(F32)).astype(BF16)

    unit_hot = (iota((FIB, FIB), 0) == mu_ref[...]).astype(F32)
    stim_row = jnp.concatenate(
        [stim_ref[...].astype(F32), jnp.zeros((1, FIB - stim_ref.shape[1]), F32)], axis=1
    )
    fire = dot(stim_row.astype(BF16), unit_hot.astype(BF16))

    home = home_ref[...]
    member = (iota((GROUPS, FIB), 0) == home).astype(F32)
    before = (iota((FIB, FIB), 0) < iota((FIB, FIB), 1)).astype(BF16)
    earlier = dot(member.astype(BF16), before)
    rank = jnp.sum(earlier * member, axis=0, keepdims=True).astype(jnp.int32)
    slot = home * CAPACITY + rank
    packed = GROUPS * SLOT_ROWS
    row_id = iota((packed, FIB), 0)
    in_brick = lax.rem(row_id, SLOT_ROWS)
    first_slot = (row_id // SLOT_ROWS) * CAPACITY + 4 * in_brick
    for q in range(4):
        chosen = (slot == first_slot + q) & (in_brick < CAPACITY // 4)
        sel_ref[:, q * FIB : (q + 1) * FIB] = chosen.astype(F32).astype(BF16)

    def pack(values):
        blank = jnp.zeros((BINS, FIB), BF16)
        total = None
        for part in split(values):
            block = jnp.concatenate(
                [
                    jnp.concatenate([part if q == row else blank for q in range(4)], axis=1)
                    for row in range(4)
                ],
                axis=0,
            )
            term = dot_t(sel_ref[...], block)
            total = term if total is None else total + term
        return total.reshape(GROUPS, SLOT_ROWS, FIB)

    def exchange(source, target, slot_index):
        def send(step, _):
            device, other = peer(step)
            pltpu.make_async_remote_copy(
                source.at[other], target.at[me], a2a_send.at[slot_index], a2a_recv.at[slot_index],
                device_id=device, device_id_type=MESH,
            ).start()
            return 0

        lax.fori_loop(1, GROUPS, send, 0)
        target[me] = source[me]

    def exchange_wait(target, slot_index):
        whole = target.at[pl.ds(0, GROUPS - 1)]
        pltpu.make_async_copy(whole, whole, a2a_recv.at[slot_index]).wait()

    def exchange_sent(source, slot_index):
        whole = source.at[pl.ds(0, GROUPS - 1)]
        pltpu.make_async_copy(whole, whole, a2a_send.at[slot_index]).wait()

    cell_row = jnp.broadcast_to(cell_ref[...].astype(F32), (BINS, FIB))
    cell_send[...] = pack(cell_row)
    pl.semaphore_wait(barrier, GROUPS - 1 + N_LEN - 1)
    exchange(cell_send, cell_recv, 0)

    s_flat = s_in.reshape(ROWS * NODES, FIB)
    s_in[pl.ds(STATES, ROWS - STATES)] = jnp.zeros((ROWS - STATES, NODES, FIB), F32)

    def stacked(values):
        high, low = split(values)
        return jnp.concatenate([high, low, high], axis=0)

    def twice(values):
        return jnp.concatenate([values, values], axis=1)

    def first_pair(pair, _):
        node = 2 * pair
        old = jnp.concatenate(
            [s_flat[pl.ds(node + k, ROWS, stride=NODES), :] for k in range(2)], axis=1
        )
        volts = jnp.concatenate([volt_ref[pl.ds(node + k, 1), :] for k in range(2)], axis=1)
        gain = twice(gain_b[...])
        drive = dot(lhs_ref[...], stacked(old)) + gain * volts
        new = twice(keep_ref[...]) * old + time_step * jnp.tanh(drive)
        new = jnp.where(iota(new.shape, 0) < STATES, new, 0.0)
        after = dot(lhs_ref[...], stacked(new))
        for k in range(2):
            lanes = slice(k * FIB, (k + 1) * FIB)
            s_work[node + k] = new[:, lanes]
            s_new[node + k] = after[:, lanes]
            cur_ref[pl.ds(node + k, 1), :] = after[STATES : STATES + 1, lanes]
        return 0

    for part in range(4):
        loads[part].wait()
        lax.fori_loop(part * (quarter // 2), (part + 1) * (quarter // 2), first_pair, 0, unroll=2)

    node_id = shard * NODES + iota((NODES, FIB), 0)
    total_nodes = NODES * N_LEN
    band = (node_id >= total_nodes // 2 - band_half) & (node_id < total_nodes // 2 + band_half)

    def cable_begin(step, volts):
        active = (fire == float(step)).astype(F32)
        pulse = jnp.where(band, amplitude * active, 0.0)
        right = volts + time_step * (pulse - cur_ref[...])
        both = dot_high(local_ref[shard], right)
        end_send[step] = both[NODES:]
        for other_step in range(1, N_LEN):
            other = lax.rem(shard + other_step, N_LEN)
            pltpu.make_async_remote_copy(
                end_send.at[step], end_recv.at[step, shard], len_send.at[step], len_recv.at[step],
                device_id={"fib": fib, "len": other, "emg": emg}, device_id_type=MESH,
            ).start()
        end_recv[step, shard] = jnp.zeros((8, FIB), F32)
        return both[:NODES]

    def cable_end(step, local):
        whole = end_recv.at[step, pl.ds(0, N_LEN - 1)]
        pltpu.make_async_copy(whole, whole, len_recv.at[step]).wait()
        far = end_recv[step].reshape(8 * N_LEN, FIB)
        return local + dot_high(far_ref[shard], far)

    def binned():
        first = cur_ref[pl.ds(0, BINS, stride=2), :]
        second = cur_ref[pl.ds(1, BINS, stride=2), :]
        return first + second

    local = cable_begin(0, volt_ref[...])
    row_send[0] = pack(binned())
    exchange(row_send.at[0], row_recv.at[0], 1)

    exchange_wait(cell_recv, 0)
    cells = cell_recv[...].reshape(packed, FIB)
    for q in range(4):
        column_q = cells[:, q * BINS : q * BINS + 1].astype(jnp.int32)
        for y in range(BY):
            hot = (column_q == iota((packed, BZ), 1) + y * BZ).astype(F32).astype(BF16)
            hot_ref[q * packed : (q + 1) * packed, y * BZ : (y + 1) * BZ] = hot

    v1_ref[...] = cable_end(0, local)

    o_flat = s_in.reshape(ROWS * NODES, FIB)

    def second_pair(node, _):
        drive = s_new[node] + gain_b[...] * v1_ref[pl.ds(node, 1), :]
        new = keep_ref[...] * s_work[node] + time_step * jnp.tanh(drive)
        o_flat[pl.ds(node, ROWS, stride=NODES), :] = new
        cur_ref[pl.ds(node, 1), :] = jnp.sum(wts_b[...] * new, axis=0, keepdims=True)
        return 0

    stores = []
    for part in range(4):
        lax.fori_loop(part * quarter, (part + 1) * quarter, second_pair, 0, unroll=2)
        window = pl.ds(part * quarter, quarter)
        copy = pltpu.make_async_copy(
            s_in.at[pl.ds(0, STATES), window, :], states_out.at[:, window, :], out_sem.at[part]
        )
        copy.start()
        stores.append(copy)

    row_send[1] = pack(binned())
    exchange(row_send.at[1], row_recv.at[1], 2)
    local = cable_begin(1, v1_ref[...])

    middle = 0.5 * (high_bound + low_bound)
    spread_width = 0.5 * (high_bound - low_bound)
    ratio = middle / spread_width
    lane = iota((BY, BZ), 1)
    sub = iota((BY, BZ), 0)

    def scatter(step):
        exchange_wait(row_recv.at[step], 1 + step)
        rows = row_recv[step].reshape(packed, FIB)
        turned = rows.T
        wide = jnp.concatenate([turned[q * BINS : (q + 1) * BINS] for q in range(4)], axis=1)
        both = dot(jnp.concatenate(split(wide), axis=0), hot_ref[...])
        source = both[:BINS] + both[BINS:]
        flat = r_ref.at[step].reshape(BINS * BY, BZ)
        for y in range(BY):
            flat[pl.ds(y, BINS, stride=BY), :] = source[:, y * BZ : (y + 1) * BZ]
        first = r_ref[step] * (1.0 / middle)
        d_ref[step, pl.ds(1, BINS)] = first
        x_ref[step] = first

    def faces(step, sweep):
        send = face_send.at[step, sweep]
        recv = face_recv.at[step, sweep]
        flat = d_ref.at[step].reshape((BINS + 2) * BY, BZ)
        send[0:32, :] = flat[pl.ds(BY, BINS, stride=BY), :]
        send[32:64, :] = flat[pl.ds(2 * BY - 1, BINS, stride=BY), :]
        send[64:72, :] = flat[BY : 2 * BY, :]
        send[72:80, :] = flat[BINS * BY : (BINS + 1) * BY, :]
        pick = (iota((8, BZ), 1) == (BZ - 1) * iota((8, BZ), 0)).astype(F32)
        side = dot_t(pick, flat[BY : (BINS + 1) * BY, :], HIGH)
        send[80:88, :] = side[:, :BZ]
        send[88:96, :] = side[:, BZ:]
        up, down = lax.rem(fib + 1, N_FIB), lax.rem(fib + N_FIB - 1, N_FIB)
        right, left = lax.rem(shard + 1, N_LEN), lax.rem(shard + N_LEN - 1, N_LEN)
        front, back = lax.rem(emg + 1, N_EMG), lax.rem(emg + N_EMG - 1, N_EMG)
        plan = (
            (0, 32, 32, {"fib": down, "len": shard, "emg": emg}),
            (32, 0, 32, {"fib": up, "len": shard, "emg": emg}),
            (64, 72, 8, {"fib": fib, "len": left, "emg": emg}),
            (72, 64, 8, {"fib": fib, "len": right, "emg": emg}),
            (80, 96, 16, {"fib": fib, "len": shard, "emg": back}),
            (80, 80, 16, {"fib": fib, "len": shard, "emg": front}),
        )
        for source, target, height, device in plan:
            pltpu.make_async_remote_copy(
                send.at[pl.ds(source, height)], recv.at[pl.ds(target, height)],
                face_ssem.at[step, sweep], face_rsem.at[step, sweep],
                device_id=device, device_id_type=MESH,
            ).start()

    def sweep_on(step, sweep, weight_now, weight_next):
        recv = face_recv.at[step, sweep]
        pltpu.make_async_copy(recv, recv, face_rsem.at[step, sweep]).wait()

        def unless(edge):
            return jnp.where(edge, 0.0, 1.0).astype(F32)

        d_ref[step, 0] = recv[64:72, :] * unless(shard == 0)
        d_ref[step, BINS + 1] = recv[72:80, :] * unless(shard == N_LEN - 1)
        hy_flat = hy_ref.reshape(BINS * BY, BZ)
        hy_flat[pl.ds(0, BINS, stride=BY), :] = recv[0:32, :] * unless(fib == 0)
        hy_flat[pl.ds(BY - 1, BINS, stride=BY), :] = recv[32:64, :] * unless(fib == N_FIB - 1)
        low_side = jnp.concatenate([recv[80:88, :], recv[88:96, :]], axis=1)
        high_side = jnp.concatenate([recv[96:104, :], recv[104:112, :]], axis=1)
        row, col = iota((16, BZ), 0), iota((16, BZ), 1)
        inject = jnp.where((row == 1) & (col == 0), unless(emg == 0), 0.0)
        inject = inject + jnp.where((row == 8) & (col == BZ - 1), unless(emg == N_EMG - 1), 0.0)
        hz_ref[...] = dot_tl(jnp.concatenate([low_side, high_side], axis=0), inject, HIGH).reshape(
            BINS, BY, BZ
        )
        keep, gain = weight_next * weight_now, 2.0 * weight_next / spread_width

        def slab(x, previous):
            here = d_ref[step, x + 1]
            beside = previous + d_ref[step, x + 2] + hy_ref[x] + hz_ref[x]
            beside = beside + jnp.where(sub == 0, 0.0, pltpu.roll(here, 1, 0))
            beside = beside + jnp.where(sub == BY - 1, 0.0, pltpu.roll(here, BY - 1, 0))
            beside = beside + jnp.where(lane == 0, 0.0, pltpu.roll(here, 1, 1))
            beside = beside + jnp.where(lane == BZ - 1, 0.0, pltpu.roll(here, BZ - 1, 1))
            rest = r_ref[step, x] - ((6.0 + tissue_ref[x]) * here - beside)
            after = keep * here + gain * rest
            r_ref[step, x] = rest
            d_ref[step, x + 1] = after
            if sweep == SWEEPS - 2:
                pot_out[step, x] = x_ref[step, x] + after
            else:
                x_ref[step, x] = x_ref[step, x] + after
            return here

        lax.fori_loop(0, BINS, slab, d_ref[step, 0], unroll=4)

    weight = [1.0 / ratio]
    for _ in range(SWEEPS - 1):
        weight.append(1.0 / (2.0 * ratio - weight[-1]))

    def advance(step, sweep):
        sweep_on(step, sweep, weight[sweep], weight[sweep + 1])
        if sweep < SWEEPS - 2:
            faces(step, sweep + 1)

    scatter(0)
    faces(0, 0)
    volt_out[...] = cable_end(1, local)
    advance(0, 0)
    scatter(1)
    faces(1, 0)
    advance(0, 1)
    advance(1, 0)
    advance(0, 2)
    advance(1, 1)
    advance(1, 2)

    for copy in stores:
        copy.wait()
    exchange_sent(cell_send, 0)
    for step in range(STEPS):
        exchange_sent(row_send.at[step], 1 + step)
        whole = end_recv.at[step, pl.ds(0, N_LEN - 1)]
        pltpu.make_async_copy(whole, whole, len_send.at[step]).wait()
        for sweep in range(SWEEPS - 1):
            sent = face_send.at[step, sweep]
            pltpu.make_async_copy(sent, sent, face_ssem.at[step, sweep]).wait()


def on_device(
    states, voltage, coupling, decay_rates, volt_gain, current_weights,
    fibre_home, cross_cell, motor_unit, stim_step, tissue,
):
    local, far = cable_tables()
    vmem = pl.BlockSpec(memory_space=pltpu.VMEM)
    hbm = pl.BlockSpec(memory_space=pl.ANY)
    sweeps = SWEEPS - 1
    return pl.pallas_call(
        kernel,
        out_shape=(
            jax.ShapeDtypeStruct(states.shape, F32),
            jax.ShapeDtypeStruct(voltage.shape, F32),
            jax.ShapeDtypeStruct((STEPS, *tissue.shape), F32),
        ),
        in_specs=[hbm] + [vmem] * 12,
        out_specs=(hbm, vmem, vmem),
        scratch_shapes=[
            pltpu.VMEM((ROWS, NODES, FIB), F32),
            pltpu.VMEM((NODES, ROWS, FIB), F32),
            pltpu.VMEM((NODES, ROWS, FIB), F32),
            pltpu.VMEM((ROWS, 3 * ROWS), BF16),
            pltpu.VMEM((ROWS, FIB), F32),
            pltpu.VMEM((ROWS, FIB), F32),
            pltpu.VMEM((ROWS, FIB), F32),
            pltpu.VMEM((NODES, FIB), F32),
            pltpu.VMEM((NODES, FIB), F32),
            pltpu.VMEM((4 * GROUPS * SLOT_ROWS, BY * BZ), BF16),
            pltpu.VMEM((GROUPS * SLOT_ROWS, 4 * FIB), BF16),
            pltpu.VMEM((GROUPS, SLOT_ROWS, FIB), F32),
            pltpu.VMEM((GROUPS, SLOT_ROWS, FIB), F32),
            pltpu.VMEM((STEPS, GROUPS, SLOT_ROWS, FIB), F32),
            pltpu.VMEM((STEPS, GROUPS, SLOT_ROWS, FIB), F32),
            pltpu.VMEM((STEPS, 8, FIB), F32),
            pltpu.VMEM((STEPS, N_LEN, 8, FIB), F32),
            pltpu.VMEM((STEPS, sweeps, FACE_ROWS, FIB), F32),
            pltpu.VMEM((STEPS, sweeps, FACE_ROWS, FIB), F32),
            pltpu.VMEM((STEPS, BINS + 2, BY, BZ), F32),
            pltpu.VMEM((STEPS, BINS, BY, BZ), F32),
            pltpu.VMEM((STEPS, BINS, BY, BZ), F32),
            pltpu.VMEM((BINS, BY, BZ), F32),
            pltpu.VMEM((BINS, BY, BZ), F32),
            pltpu.SemaphoreType.DMA((4,)),
            pltpu.SemaphoreType.DMA((4,)),
            pltpu.SemaphoreType.DMA((3,)),
            pltpu.SemaphoreType.DMA((3,)),
            pltpu.SemaphoreType.DMA((STEPS,)),
            pltpu.SemaphoreType.DMA((STEPS,)),
            pltpu.SemaphoreType.DMA((STEPS, sweeps)),
            pltpu.SemaphoreType.DMA((STEPS, sweeps)),
        ],
        compiler_params=pltpu.CompilerParams(collective_id=0, has_side_effects=True),
    )(
        states, voltage, coupling, decay_rates.reshape(1, -1), volt_gain.reshape(1, -1),
        current_weights.reshape(1, -1), fibre_home.reshape(1, -1), cross_cell.reshape(1, -1),
        motor_unit.reshape(1, -1), stim_step.reshape(1, -1), tissue, local, far,
    )


def solution(mesh):
    return jax.shard_map(
        on_device,
        mesh=mesh,
        in_specs=(
            P(None, "len", ("fib", "emg")),
            P("len", ("fib", "emg")),
            P(),
            P(),
            P(),
            P(),
            P(("fib", "emg"), None),
            P(("fib", "emg")),
            P(("fib", "emg")),
            P(),
            P("len", "fib", "emg"),
        ),
        out_specs=(
            P(None, "len", ("fib", "emg")),
            P("len", ("fib", "emg")),
            P(None, "len", "fib", "emg"),
        ),
        check_vma=False,
    )
```

```python
import math

import jax
import jax.numpy as jnp
import numpy as np
from jax import lax
from jax.experimental import pallas as pl
from jax.experimental.pallas import tpu as pltpu
from jax.sharding import PartitionSpec as P

STEPS = 2
SWEEPS = 4
NPC = 2

time_step = 0.5
conductance = 2000.0
amplitude = 200.0
band_half = 4
low_bound = 0.5
high_bound = 14.0

MESH = pl.DeviceIdType.MESH
HIGH = lax.Precision.HIGHEST
F32 = jnp.float32
BF16 = jnp.bfloat16

N_FIB, N_LEN, N_EMG = 8, 4, 4
GROUPS = N_FIB * N_EMG
STATES = 57
ROWS = 64
NODES = 64
FIB = 128
BINS = NODES // NPC
BY, BZ = 8, 128
SLOT_ROWS = 4
CAPACITY = 12
FACE_ROWS = 112
VMEM_LIMIT = 24 << 20


def cable_tables():
    total = NODES * N_LEN
    theta = math.acosh(1.0 + 0.5 / conductance)
    scale = conductance * math.sinh(theta) * math.sinh(total * theta)
    u = np.array([math.cosh((i + 0.5) * theta) for i in range(total)])
    v = np.array([math.cosh((total - 0.5 - i) * theta) / scale for i in range(total)])
    index = np.arange(NODES)
    local = np.zeros((N_LEN, NODES + 8, NODES))
    far = np.zeros((N_LEN, NODES, 8 * N_LEN))
    for shard in range(N_LEN):
        us, vs = u[shard * NODES :][:NODES], v[shard * NODES :][:NODES]
        low = index[:, None] <= index[None, :]
        local[shard, :NODES] = np.where(low, us[:, None] * vs[None, :], vs[:, None] * us[None, :])
        local[shard, NODES] = us
        local[shard, NODES + 1] = vs
        for other in range(N_LEN):
            if other < shard:
                far[shard, :, 8 * other] = vs
            if other > shard:
                far[shard, :, 8 * other + 1] = us
    return jnp.asarray(local, F32), jnp.asarray(far, F32)


def iota(shape, axis):
    return lax.broadcasted_iota(jnp.int32, shape, axis)


def split(values):
    high = values.astype(BF16)
    return high, (values - high.astype(F32)).astype(BF16)


def dot(a, b):
    return jnp.dot(a, b, preferred_element_type=F32)


def dot_high(a, b):
    return jnp.dot(a, b, preferred_element_type=F32, precision=HIGH)


def dot_t(a, b, precision=None):
    return lax.dot_general(
        a, b, (((1,), (1,)), ((), ())), preferred_element_type=F32, precision=precision
    )


def dot_tl(a, b, precision=None):
    return lax.dot_general(
        a, b, (((0,), (0,)), ((), ())), preferred_element_type=F32, precision=precision
    )


def kernel(
    states_hbm, volt_hbm, coup_hbm, decay_hbm, gain_hbm, wts_hbm, home_hbm, cell_hbm, mu_hbm,
    stim_hbm, tissue_hbm, local_hbm, far_hbm,
    states_out, volt_out, pot_out,
    volt_ref, coup_ref, decay_ref, gain_ref, wts_ref, home_ref, cell_ref, mu_ref,
    stim_ref, tissue_ref, local_ref, far_ref,
    s_in, s_work, s_new, lhs_ref, keep_ref, gain_b, wts_b, cur_ref, v1_ref, hot_ref, sel_ref,
    cell_send, cell_recv, row_send, row_recv, end_send, end_recv, face_send, face_recv,
    d_ref, r_ref, x_ref, hy_ref, hz_ref,
    in_sem, small_sem, a2a_send, a2a_recv, len_send, len_recv, face_ssem, face_rsem,
):
    fib, shard, emg = lax.axis_index("fib"), lax.axis_index("len"), lax.axis_index("emg")
    me = fib * N_EMG + emg

    quarter = NODES // 4
    smalls = [
        pltpu.make_async_copy(source, target, small_sem.at[number])
        for number, (source, target) in enumerate((
            (coup_hbm, coup_ref), (decay_hbm, decay_ref), (gain_hbm, gain_ref), (wts_hbm, wts_ref),
            (home_hbm, home_ref), (cell_hbm, cell_ref), (mu_hbm, mu_ref), (stim_hbm, stim_ref),
            (volt_hbm, volt_ref), (local_hbm, local_ref), (far_hbm, far_ref),
            (tissue_hbm, tissue_ref),
        ))
    ]
    for copy in smalls:
        copy.start()
    loads = []
    for part in range(4):
        window = pl.ds(part * quarter, quarter)
        copy = pltpu.make_async_copy(
            states_hbm.at[:, window, :], s_in.at[pl.ds(0, STATES), window, :], in_sem.at[part]
        )
        copy.start()
        loads.append(copy)

    barrier = pltpu.get_barrier_semaphore()

    def peer(step):
        other = lax.rem(me + step, GROUPS)
        return {"fib": other // N_EMG, "len": shard, "emg": lax.rem(other, N_EMG)}, other

    def greet(step, _):
        device, _other = peer(step)
        pl.semaphore_signal(barrier, inc=1, device_id=device, device_id_type=MESH)
        return 0

    lax.fori_loop(1, GROUPS, greet, 0)
    for step in range(1, N_LEN):
        other = lax.rem(shard + step, N_LEN)
        pl.semaphore_signal(
            barrier, inc=1, device_id={"fib": fib, "len": other, "emg": emg}, device_id_type=MESH
        )

    def column(row):
        wide = row.shape[1]
        picked = jnp.where(iota((ROWS, wide), 0) == iota((ROWS, wide), 1), row, 0.0)
        return dot_high(picked, jnp.ones((wide, FIB), F32))

    for copy in smalls[:8]:
        copy.wait()
    keep_ref[...] = 1.0 - time_step * column(decay_ref[...])
    gain_b[...] = column(gain_ref[...])
    wts_b[...] = column(wts_ref[...])
    spread = (iota((STATES, 3 * ROWS), 0) == lax.rem(iota((STATES, 3 * ROWS), 1), ROWS)).astype(F32)
    tiled = dot_high(coup_ref[...], spread)
    tiled = jnp.concatenate([tiled, jnp.zeros((ROWS - STATES, 3 * ROWS), F32)], axis=0)
    weights = dot_high(wts_ref[...], spread)
    tiled = jnp.where(iota((ROWS, 3 * ROWS), 0) == STATES, weights, tiled)
    high, low = split(tiled)
    lhs_ref[...] = jnp.where(iota((ROWS, 3 * ROWS), 1) < 2 * ROWS, high.astype(F32), low.astype(F32)).astype(BF16)

    unit_hot = (iota((FIB, FIB), 0) == mu_ref[...]).astype(F32)
    stim_row = jnp.concatenate(
        [stim_ref[...].astype(F32), jnp.zeros((1, FIB - stim_ref.shape[1]), F32)], axis=1
    )
    fire = dot(stim_row.astype(BF16), unit_hot.astype(BF16))

    home = home_ref[...]
    member = (iota((GROUPS, FIB), 0) == home).astype(F32)
    before = (iota((FIB, FIB), 0) < iota((FIB, FIB), 1)).astype(BF16)
    earlier = dot(member.astype(BF16), before)
    rank = jnp.sum(earlier * member, axis=0, keepdims=True).astype(jnp.int32)
    slot = home * CAPACITY + rank
    packed = GROUPS * SLOT_ROWS
    row_id = iota((packed, FIB), 0)
    in_brick = lax.rem(row_id, SLOT_ROWS)
    first_slot = (row_id // SLOT_ROWS) * CAPACITY + 4 * in_brick
    for q in range(4):
        chosen = (slot == first_slot + q) & (in_brick < CAPACITY // 4)
        sel_ref[:, q * FIB : (q + 1) * FIB] = chosen.astype(F32).astype(BF16)

    def pack(values):
        blank = jnp.zeros((BINS, FIB), BF16)
        total = None
        for part in split(values):
            block = jnp.concatenate(
                [
                    jnp.concatenate([part if q == row else blank for q in range(4)], axis=1)
                    for row in range(4)
                ],
                axis=0,
            )
            term = dot_t(sel_ref[...], block)
            total = term if total is None else total + term
        return total.reshape(GROUPS, SLOT_ROWS, FIB)

    def exchange(source, target, slot_index):
        def send(step, _):
            device, other = peer(step)
            pltpu.make_async_remote_copy(
                source.at[other], target.at[me], a2a_send.at[slot_index], a2a_recv.at[slot_index],
                device_id=device, device_id_type=MESH,
            ).start()
            return 0

        lax.fori_loop(1, GROUPS, send, 0)
        target[me] = source[me]

    def exchange_wait(target, slot_index):
        whole = target.at[pl.ds(0, GROUPS - 1)]
        pltpu.make_async_copy(whole, whole, a2a_recv.at[slot_index]).wait()

    def exchange_sent(source, slot_index):
        whole = source.at[pl.ds(0, GROUPS - 1)]
        pltpu.make_async_copy(whole, whole, a2a_send.at[slot_index]).wait()

    cell_row = jnp.broadcast_to(cell_ref[...].astype(F32), (BINS, FIB))
    cell_send[...] = pack(cell_row)

    for copy in smalls[8:]:
        copy.wait()

    s_flat = s_in.reshape(ROWS * NODES, FIB)
    s_in[pl.ds(STATES, ROWS - STATES)] = jnp.zeros((ROWS - STATES, NODES, FIB), F32)

    def stacked(values):
        high, low = split(values)
        return jnp.concatenate([high, low, high], axis=0)

    def twice(values):
        return jnp.concatenate([values, values], axis=1)

    def first_pair(pair, _):
        node = 2 * pair
        old = jnp.concatenate(
            [s_flat[pl.ds(node + k, ROWS, stride=NODES), :] for k in range(2)], axis=1
        )
        volts = jnp.concatenate([volt_ref[pl.ds(node + k, 1), :] for k in range(2)], axis=1)
        gain = twice(gain_b[...])
        drive = dot(lhs_ref[...], stacked(old)) + gain * volts
        new = twice(keep_ref[...]) * old + time_step * jnp.tanh(drive)
        after = dot(lhs_ref[...], stacked(new))
        for k in range(2):
            lanes = slice(k * FIB, (k + 1) * FIB)
            s_work[node + k] = new[:, lanes]
            s_new[node + k] = after[:, lanes]
            cur_ref[pl.ds(node + k, 1), :] = after[STATES : STATES + 1, lanes]
        return 0

    for part in range(4):
        loads[part].wait()
        lax.fori_loop(part * (quarter // 2), (part + 1) * (quarter // 2), first_pair, 0, unroll=8)
        if part == 1:
            pl.semaphore_wait(barrier, GROUPS - 1 + N_LEN - 1)
            exchange(cell_send, cell_recv, 0)

    node_id = shard * NODES + iota((NODES, FIB), 0)
    total_nodes = NODES * N_LEN
    band = (node_id >= total_nodes // 2 - band_half) & (node_id < total_nodes // 2 + band_half)

    def cable_begin(step, volts):
        active = (fire == float(step)).astype(F32)
        pulse = jnp.where(band, amplitude * active, 0.0)
        right = volts + time_step * (pulse - cur_ref[...])
        both = dot_high(local_ref[shard], right)
        end_send[step] = both[NODES:]
        for other_step in range(1, N_LEN):
            other = lax.rem(shard + other_step, N_LEN)
            pltpu.make_async_remote_copy(
                end_send.at[step], end_recv.at[step, shard], len_send.at[step], len_recv.at[step],
                device_id={"fib": fib, "len": other, "emg": emg}, device_id_type=MESH,
            ).start()
        end_recv[step, shard] = jnp.zeros((8, FIB), F32)
        return both[:NODES]

    def cable_end(step, local):
        whole = end_recv.at[step, pl.ds(0, N_LEN - 1)]
        pltpu.make_async_copy(whole, whole, len_recv.at[step]).wait()
        far = end_recv[step].reshape(8 * N_LEN, FIB)
        return local + dot_high(far_ref[shard], far)

    def binned():
        first = cur_ref[pl.ds(0, BINS, stride=2), :]
        second = cur_ref[pl.ds(1, BINS, stride=2), :]
        return first + second

    local = cable_begin(0, volt_ref[...])
    row_send[0] = pack(binned())
    exchange(row_send.at[0], row_recv.at[0], 1)

    exchange_wait(cell_recv, 0)
    cells = cell_recv[...].reshape(packed, FIB)
    for q in range(4):
        column_q = cells[:, q * BINS : q * BINS + 1].astype(jnp.int32)
        for y in range(BY):
            hot = (column_q == iota((packed, BZ), 1) + y * BZ).astype(F32).astype(BF16)
            hot_ref[q * packed : (q + 1) * packed, y * BZ : (y + 1) * BZ] = hot

    middle = 0.5 * (high_bound + low_bound)
    spread_width = 0.5 * (high_bound - low_bound)
    ratio = middle / spread_width
    lane = iota((BY, BZ), 1)
    sub = iota((BY, BZ), 0)

    def scatter(step):
        exchange_wait(row_recv.at[step], 1 + step)
        rows = row_recv[step].reshape(packed, FIB)
        turned = rows.T
        wide = jnp.concatenate([turned[q * BINS : (q + 1) * BINS] for q in range(4)], axis=1)
        both = dot(jnp.concatenate(split(wide), axis=0), hot_ref[...])
        source = both[:BINS] + both[BINS:]
        flat = r_ref.at[step].reshape(BINS * BY, BZ)
        for y in range(BY):
            flat[pl.ds(y, BINS, stride=BY), :] = source[:, y * BZ : (y + 1) * BZ]
        first = r_ref[step] * (1.0 / middle)
        d_ref[step, pl.ds(1, BINS)] = first
        x_ref[step] = first

    def faces(step, sweep):
        send = face_send.at[step, sweep]
        recv = face_recv.at[step, sweep]
        flat = d_ref.at[step].reshape((BINS + 2) * BY, BZ)
        send[0:32, :] = flat[pl.ds(BY, BINS, stride=BY), :]
        send[32:64, :] = flat[pl.ds(2 * BY - 1, BINS, stride=BY), :]
        send[64:72, :] = flat[BY : 2 * BY, :]
        send[72:80, :] = flat[BINS * BY : (BINS + 1) * BY, :]
        pick = (iota((8, BZ), 1) == (BZ - 1) * iota((8, BZ), 0)).astype(F32)
        side = dot_t(pick, flat[BY : (BINS + 1) * BY, :], HIGH)
        send[80:88, :] = side[:, :BZ]
        send[88:96, :] = side[:, BZ:]
        up, down = lax.rem(fib + 1, N_FIB), lax.rem(fib + N_FIB - 1, N_FIB)
        right, left = lax.rem(shard + 1, N_LEN), lax.rem(shard + N_LEN - 1, N_LEN)
        front, back = lax.rem(emg + 1, N_EMG), lax.rem(emg + N_EMG - 1, N_EMG)
        plan = (
            (0, 32, 32, {"fib": down, "len": shard, "emg": emg}),
            (32, 0, 32, {"fib": up, "len": shard, "emg": emg}),
            (64, 72, 8, {"fib": fib, "len": left, "emg": emg}),
            (72, 64, 8, {"fib": fib, "len": right, "emg": emg}),
            (80, 96, 16, {"fib": fib, "len": shard, "emg": back}),
            (80, 80, 16, {"fib": fib, "len": shard, "emg": front}),
        )
        for source, target, height, device in plan:
            pltpu.make_async_remote_copy(
                send.at[pl.ds(source, height)], recv.at[pl.ds(target, height)],
                face_ssem.at[step, sweep], face_rsem.at[step, sweep],
                device_id=device, device_id_type=MESH,
            ).start()

    def sweep_on(step, sweep, weight_now, weight_next):
        recv = face_recv.at[step, sweep]
        pltpu.make_async_copy(recv, recv, face_rsem.at[step, sweep]).wait()

        def unless(edge):
            return jnp.where(edge, 0.0, 1.0).astype(F32)

        d_ref[step, 0] = recv[64:72, :] * unless(shard == 0)
        d_ref[step, BINS + 1] = recv[72:80, :] * unless(shard == N_LEN - 1)
        hy_flat = hy_ref.reshape(BINS * BY, BZ)
        hy_flat[pl.ds(0, BINS, stride=BY), :] = recv[0:32, :] * unless(fib == 0)
        hy_flat[pl.ds(BY - 1, BINS, stride=BY), :] = recv[32:64, :] * unless(fib == N_FIB - 1)
        low_side = jnp.concatenate([recv[80:88, :], recv[88:96, :]], axis=1)
        high_side = jnp.concatenate([recv[96:104, :], recv[104:112, :]], axis=1)
        row, col = iota((16, BZ), 0), iota((16, BZ), 1)
        inject = jnp.where((row == 1) & (col == 0), unless(emg == 0), 0.0)
        inject = inject + jnp.where((row == 8) & (col == BZ - 1), unless(emg == N_EMG - 1), 0.0)
        hz_ref[...] = dot_tl(jnp.concatenate([low_side, high_side], axis=0), inject, HIGH).reshape(
            BINS, BY, BZ
        )
        keep, gain = weight_next * weight_now, 2.0 * weight_next / spread_width

        def slab(x, previous):
            here = d_ref[step, x + 1]
            beside = previous + d_ref[step, x + 2] + hy_ref[x] + hz_ref[x]
            beside = beside + jnp.where(sub == 0, 0.0, pltpu.roll(here, 1, 0))
            beside = beside + jnp.where(sub == BY - 1, 0.0, pltpu.roll(here, BY - 1, 0))
            beside = beside + jnp.where(lane == 0, 0.0, pltpu.roll(here, 1, 1))
            beside = beside + jnp.where(lane == BZ - 1, 0.0, pltpu.roll(here, BZ - 1, 1))
            rest = r_ref[step, x] - ((6.0 + tissue_ref[x]) * here - beside)
            after = keep * here + gain * rest
            r_ref[step, x] = rest
            d_ref[step, x + 1] = after
            if sweep == SWEEPS - 2:
                pot_out[step, x] = x_ref[step, x] + after
            else:
                x_ref[step, x] = x_ref[step, x] + after
            return here

        lax.fori_loop(0, BINS, slab, d_ref[step, 0], unroll=16)

    weight = [1.0 / ratio]
    for _ in range(SWEEPS - 1):
        weight.append(1.0 / (2.0 * ratio - weight[-1]))

    def advance(step, sweep):
        sweep_on(step, sweep, weight[sweep], weight[sweep + 1])
        if sweep < SWEEPS - 2:
            faces(step, sweep + 1)

    v1_ref[...] = cable_end(0, local)

    o_flat = states_out.reshape(STATES * NODES, FIB)

    def second(node, _):
        drive = s_new[node] + gain_b[...] * v1_ref[pl.ds(node, 1), :]
        new = keep_ref[...] * s_work[node] + time_step * jnp.tanh(drive)
        o_flat[pl.ds(node, STATES, stride=NODES), :] = new[:STATES]
        cur_ref[pl.ds(node, 1), :] = jnp.sum(wts_b[...] * new, axis=0, keepdims=True)
        return 0

    lax.fori_loop(0, NODES // 2, second, 0, unroll=8)
    scatter(0)
    faces(0, 0)
    lax.fori_loop(NODES // 2, NODES, second, 0, unroll=8)

    row_send[1] = pack(binned())
    exchange(row_send.at[1], row_recv.at[1], 2)
    local = cable_begin(1, v1_ref[...])

    advance(0, 0)
    volt_out[...] = cable_end(1, local)
    scatter(1)
    faces(1, 0)
    advance(0, 1)
    advance(1, 0)
    advance(0, 2)
    advance(1, 1)
    advance(1, 2)

    exchange_sent(cell_send, 0)
    for step in range(STEPS):
        exchange_sent(row_send.at[step], 1 + step)
        whole = end_recv.at[step, pl.ds(0, N_LEN - 1)]
        pltpu.make_async_copy(whole, whole, len_send.at[step]).wait()
        for sweep in range(SWEEPS - 1):
            sent = face_send.at[step, sweep]
            pltpu.make_async_copy(sent, sent, face_ssem.at[step, sweep]).wait()


def write_out(states, voltage, potential, states_out, voltage_out, potential_out, sem):
    cuts = (0, 15, 29, 43, STATES)
    copies = [
        pltpu.make_async_copy(
            states.at[pl.ds(cuts[k], cuts[k + 1] - cuts[k])],
            states_out.at[pl.ds(cuts[k], cuts[k + 1] - cuts[k])],
            sem.at[k],
        )
        for k in range(4)
    ]
    copies.append(pltpu.make_async_copy(potential, potential_out, sem.at[4]))
    copies.append(pltpu.make_async_copy(voltage, voltage_out, sem.at[5]))
    for copy in copies:
        copy.start()
    for copy in copies:
        copy.wait()


def on_device(
    states, voltage, coupling, decay_rates, volt_gain, current_weights,
    fibre_home, cross_cell, motor_unit, stim_step, tissue,
):
    local, far = cable_tables()
    vmem = pl.BlockSpec(memory_space=pltpu.VMEM)
    hbm = pl.BlockSpec(memory_space=pltpu.HBM)
    sweeps = SWEEPS - 1
    outputs = pl.pallas_call(
        kernel,
        out_shape=(
            jax.ShapeDtypeStruct(states.shape, F32),
            jax.ShapeDtypeStruct(voltage.shape, F32),
            jax.ShapeDtypeStruct((STEPS, *tissue.shape), F32),
        ),
        in_specs=[hbm] * 13,
        out_specs=(vmem, vmem, vmem),
        scratch_shapes=[
            pltpu.VMEM(voltage.shape, F32),
            pltpu.VMEM(coupling.shape, F32),
            pltpu.VMEM((1, STATES), F32),
            pltpu.VMEM((1, STATES), F32),
            pltpu.VMEM((1, STATES), F32),
            pltpu.VMEM((1, FIB), jnp.int32),
            pltpu.VMEM((1, FIB), jnp.int32),
            pltpu.VMEM((1, FIB), jnp.int32),
            pltpu.VMEM((1, stim_step.shape[0]), jnp.int32),
            pltpu.VMEM(tissue.shape, F32),
            pltpu.VMEM(local.shape, F32),
            pltpu.VMEM(far.shape, F32),
            pltpu.VMEM((ROWS, NODES, FIB), F32),
            pltpu.VMEM((NODES, ROWS, FIB), F32),
            pltpu.VMEM((NODES, ROWS, FIB), F32),
            pltpu.VMEM((ROWS, 3 * ROWS), BF16),
            pltpu.VMEM((ROWS, FIB), F32),
            pltpu.VMEM((ROWS, FIB), F32),
            pltpu.VMEM((ROWS, FIB), F32),
            pltpu.VMEM((NODES, FIB), F32),
            pltpu.VMEM((NODES, FIB), F32),
            pltpu.VMEM((4 * GROUPS * SLOT_ROWS, BY * BZ), BF16),
            pltpu.VMEM((GROUPS * SLOT_ROWS, 4 * FIB), BF16),
            pltpu.VMEM((GROUPS, SLOT_ROWS, FIB), F32),
            pltpu.VMEM((GROUPS, SLOT_ROWS, FIB), F32),
            pltpu.VMEM((STEPS, GROUPS, SLOT_ROWS, FIB), F32),
            pltpu.VMEM((STEPS, GROUPS, SLOT_ROWS, FIB), F32),
            pltpu.VMEM((STEPS, 8, FIB), F32),
            pltpu.VMEM((STEPS, N_LEN, 8, FIB), F32),
            pltpu.VMEM((STEPS, sweeps, FACE_ROWS, FIB), F32),
            pltpu.VMEM((STEPS, sweeps, FACE_ROWS, FIB), F32),
            pltpu.VMEM((STEPS, BINS + 2, BY, BZ), F32),
            pltpu.VMEM((STEPS, BINS, BY, BZ), F32),
            pltpu.VMEM((STEPS, BINS, BY, BZ), F32),
            pltpu.VMEM((BINS, BY, BZ), F32),
            pltpu.VMEM((BINS, BY, BZ), F32),
            pltpu.SemaphoreType.DMA((4,)),
            pltpu.SemaphoreType.DMA((12,)),
            pltpu.SemaphoreType.DMA((3,)),
            pltpu.SemaphoreType.DMA((3,)),
            pltpu.SemaphoreType.DMA((STEPS,)),
            pltpu.SemaphoreType.DMA((STEPS,)),
            pltpu.SemaphoreType.DMA((STEPS, sweeps)),
            pltpu.SemaphoreType.DMA((STEPS, sweeps)),
        ],
        compiler_params=pltpu.CompilerParams(collective_id=0, has_side_effects=True, vmem_limit_bytes=VMEM_LIMIT),
    )(*(pltpu.with_memory_space_constraint(array, pltpu.HBM) for array in (
        states, voltage, coupling, decay_rates.reshape(1, -1), volt_gain.reshape(1, -1),
        current_weights.reshape(1, -1), fibre_home.reshape(1, -1), cross_cell.reshape(1, -1),
        motor_unit.reshape(1, -1), stim_step.reshape(1, -1), tissue, local, far,
    )))
    return pl.pallas_call(
        write_out,
        out_shape=tuple(jax.ShapeDtypeStruct(array.shape, F32) for array in outputs),
        in_specs=[vmem] * 3,
        out_specs=(pl.BlockSpec(memory_space=pl.ANY),) * 3,
        scratch_shapes=[pltpu.SemaphoreType.DMA((6,))],
        compiler_params=pltpu.CompilerParams(vmem_limit_bytes=VMEM_LIMIT),
    )(*(pltpu.with_memory_space_constraint(array, pltpu.VMEM) for array in outputs))


def solution(mesh):
    return jax.shard_map(
        on_device,
        mesh=mesh,
        in_specs=(
            P(None, "len", ("fib", "emg")),
            P("len", ("fib", "emg")),
            P(),
            P(),
            P(),
            P(),
            P(("fib", "emg"), None),
            P(("fib", "emg")),
            P(("fib", "emg")),
            P(),
            P("len", "fib", "emg"),
        ),
        out_specs=(
            P(None, "len", ("fib", "emg")),
            P("len", ("fib", "emg")),
            P(None, "len", "fib", "emg"),
        ),
        check_vma=False,
    )
```

```python
import math

import jax
import jax.numpy as jnp
import numpy as np
from jax import lax
from jax.experimental import pallas as pl
from jax.experimental.pallas import tpu as pltpu
from jax.sharding import PartitionSpec as P

STEPS = 2
SWEEPS = 4
NPC = 2

time_step = 0.5
conductance = 2000.0
amplitude = 200.0
band_half = 4
low_bound = 0.5
high_bound = 14.0

MESH = pl.DeviceIdType.MESH
HIGH = lax.Precision.HIGHEST
F32 = jnp.float32
BF16 = jnp.bfloat16

N_FIB, N_LEN, N_EMG = 8, 4, 4
GROUPS = N_FIB * N_EMG
STATES = 57
ROWS = 64
NODES = 64
FIB = 128
BINS = NODES // NPC
BY, BZ = 8, 128
SLOT_ROWS = 4
CAPACITY = 12
WIDE_ROWS = 304
Z_TILES = 24
WRAP = 48
VMEM_LIMIT = 24 << 20
UNROLL = 31


def cable_tables():
    total = NODES * N_LEN
    theta = math.acosh(1.0 + 0.5 / conductance)
    scale = conductance * math.sinh(theta) * math.sinh(total * theta)
    u = np.array([math.cosh((i + 0.5) * theta) for i in range(total)])
    v = np.array([math.cosh((total - 0.5 - i) * theta) / scale for i in range(total)])
    index = np.arange(NODES)
    local = np.zeros((N_LEN, NODES + 8, NODES))
    far = np.zeros((N_LEN, NODES, 8 * N_LEN))
    for shard in range(N_LEN):
        us, vs = u[shard * NODES :][:NODES], v[shard * NODES :][:NODES]
        low = index[:, None] <= index[None, :]
        local[shard, :NODES] = np.where(low, us[:, None] * vs[None, :], vs[:, None] * us[None, :])
        local[shard, NODES] = us
        local[shard, NODES + 1] = vs
        for other in range(N_LEN):
            if other < shard:
                far[shard, :, 8 * other] = vs
            if other > shard:
                far[shard, :, 8 * other + 1] = us
    return jnp.asarray(local, F32), jnp.asarray(far, F32)


def iota(shape, axis):
    return lax.broadcasted_iota(jnp.int32, shape, axis)


def split(values):
    high = values.astype(BF16)
    return high, (values - high.astype(F32)).astype(BF16)


def dot(a, b):
    return jnp.dot(a, b, preferred_element_type=F32)


def dot_high(a, b):
    return jnp.dot(a, b, preferred_element_type=F32, precision=HIGH)


def dot_t(a, b, precision=None):
    return lax.dot_general(
        a, b, (((1,), (1,)), ((), ())), preferred_element_type=F32, precision=precision
    )


def dot_tl(a, b, precision=None):
    return lax.dot_general(
        a, b, (((0,), (0,)), ((), ())), preferred_element_type=F32, precision=precision
    )


def kernel(
    states_hbm, volt_hbm, coup_hbm, decay_hbm, gain_hbm, wts_hbm, home_hbm, cell_hbm, mu_hbm,
    stim_hbm, tissue_hbm, local_hbm, far_hbm,
    states_out, volt_out, pot_out,
    volt_ref, coup_ref, decay_ref, gain_ref, wts_ref, home_ref, cell_ref, mu_ref,
    stim_ref, tissue_ref, local_ref, far_ref,
    s_in, s_work, s_new, lhs_ref, keep_ref, gain_b, wts_b, cur_ref, v1_ref, hot_ref, sel_ref,
    cell_send, cell_recv, row_send, row_recv, end_send, end_recv,
    own_ref, x_ref, r_ref, d_ref, t_ref, zr_ref, zd_ref, zt_ref, hz_ref,
    y_send, z_send, wide_recv, z_recv,
    in_sem, small_sem, a2a_send, a2a_recv, len_send, len_recv, halo_ssem, halo_rsem,
):
    fib, shard, emg = lax.axis_index("fib"), lax.axis_index("len"), lax.axis_index("emg")
    me = fib * N_EMG + emg

    quarter = NODES // 4
    smalls = [
        pltpu.make_async_copy(source, target, small_sem.at[number])
        for number, (source, target) in enumerate((
            (coup_hbm, coup_ref), (decay_hbm, decay_ref), (gain_hbm, gain_ref), (wts_hbm, wts_ref),
            (home_hbm, home_ref), (cell_hbm, cell_ref), (mu_hbm, mu_ref), (stim_hbm, stim_ref),
            (volt_hbm, volt_ref), (local_hbm, local_ref), (far_hbm, far_ref),
            (tissue_hbm, tissue_ref),
        ))
    ]
    for copy in smalls:
        copy.start()
    loads = []
    for part in range(4):
        window = pl.ds(part * quarter, quarter)
        copy = pltpu.make_async_copy(
            states_hbm.at[:, window, :], s_in.at[pl.ds(0, STATES), window, :], in_sem.at[part]
        )
        copy.start()
        loads.append(copy)

    barrier = pltpu.get_barrier_semaphore()

    def peer(step):
        other = lax.rem(me + step, GROUPS)
        return {"fib": other // N_EMG, "len": shard, "emg": lax.rem(other, N_EMG)}, other

    def towards(df, dl, de):
        return {
            "fib": lax.rem(fib + N_FIB + df, N_FIB),
            "len": lax.rem(shard + N_LEN + dl, N_LEN),
            "emg": lax.rem(emg + N_EMG + de, N_EMG),
        }

    def greet(step, _):
        device, _other = peer(step)
        pl.semaphore_signal(barrier, inc=1, device_id=device, device_id_type=MESH)
        return 0

    lax.fori_loop(1, GROUPS, greet, 0)
    for step in range(1, N_LEN):
        other = lax.rem(shard + step, N_LEN)
        pl.semaphore_signal(
            barrier, inc=1, device_id={"fib": fib, "len": other, "emg": emg}, device_id_type=MESH
        )

    for df in (-1, 0, 1):
        for de in (-1, 0, 1):
            for dl in (-1, 1):
                if (df, de) != (0, 0):
                    pl.semaphore_signal(
                        barrier, inc=1, device_id=towards(df, dl, de), device_id_type=MESH
                    )

    def column(row):
        wide = row.shape[1]
        picked = jnp.where(iota((ROWS, wide), 0) == iota((ROWS, wide), 1), row, 0.0)
        return dot_high(picked, jnp.ones((wide, FIB), F32))

    for copy in smalls[:8]:
        copy.wait()
    keep_ref[...] = 1.0 - time_step * column(decay_ref[...])
    gain_b[...] = column(gain_ref[...])
    wts_b[...] = column(wts_ref[...])
    spread = (iota((STATES, 3 * ROWS), 0) == lax.rem(iota((STATES, 3 * ROWS), 1), ROWS)).astype(F32)
    tiled = dot_high(coup_ref[...], spread)
    tiled = jnp.concatenate([tiled, jnp.zeros((ROWS - STATES, 3 * ROWS), F32)], axis=0)
    weights = dot_high(wts_ref[...], spread)
    tiled = jnp.where(iota((ROWS, 3 * ROWS), 0) == STATES, weights, tiled)
    high, low = split(tiled)
    lhs_ref[...] = jnp.where(iota((ROWS, 3 * ROWS), 1) < 2 * ROWS, high.astype(F32), low.astype(F32)).astype(BF16)

    unit_hot = (iota((FIB, FIB), 0) == mu_ref[...]).astype(F32)
    stim_row = jnp.concatenate(
        [stim_ref[...].astype(F32), jnp.zeros((1, FIB - stim_ref.shape[1]), F32)], axis=1
    )
    fire = dot(stim_row.astype(BF16), unit_hot.astype(BF16))

    home = home_ref[...]
    member = (iota((GROUPS, FIB), 0) == home).astype(F32)
    before = (iota((FIB, FIB), 0) < iota((FIB, FIB), 1)).astype(BF16)
    earlier = dot(member.astype(BF16), before)
    rank = jnp.sum(earlier * member, axis=0, keepdims=True).astype(jnp.int32)
    slot = home * CAPACITY + rank
    packed = GROUPS * SLOT_ROWS
    row_id = iota((packed, FIB), 0)
    in_brick = lax.rem(row_id, SLOT_ROWS)
    first_slot = (row_id // SLOT_ROWS) * CAPACITY + 4 * in_brick
    for q in range(4):
        chosen = (slot == first_slot + q) & (in_brick < CAPACITY // 4)
        sel_ref[:, q * FIB : (q + 1) * FIB] = chosen.astype(F32).astype(BF16)

    def pack(values):
        blank = jnp.zeros((BINS, FIB), BF16)
        total = None
        for part in split(values):
            block = jnp.concatenate(
                [
                    jnp.concatenate([part if q == row else blank for q in range(4)], axis=1)
                    for row in range(4)
                ],
                axis=0,
            )
            term = dot_t(sel_ref[...], block)
            total = term if total is None else total + term
        return total.reshape(GROUPS, SLOT_ROWS, FIB)

    def exchange(source, target, slot_index):
        def send(step, _):
            device, other = peer(step)
            pltpu.make_async_remote_copy(
                source.at[other], target.at[me], a2a_send.at[slot_index], a2a_recv.at[slot_index],
                device_id=device, device_id_type=MESH,
            ).start()
            return 0

        lax.fori_loop(1, GROUPS, send, 0, unroll=UNROLL)
        target[me] = source[me]

    def exchange_wait(target, slot_index):
        whole = target.at[pl.ds(0, GROUPS - 1)]
        pltpu.make_async_copy(whole, whole, a2a_recv.at[slot_index]).wait()

    def exchange_sent(source, slot_index):
        whole = source.at[pl.ds(0, GROUPS - 1)]
        pltpu.make_async_copy(whole, whole, a2a_send.at[slot_index]).wait()

    cell_row = jnp.broadcast_to(cell_ref[...].astype(F32), (BINS, FIB))
    cell_send[...] = pack(cell_row)

    for copy in smalls[8:]:
        copy.wait()

    s_flat = s_in.reshape(ROWS * NODES, FIB)
    s_in[pl.ds(STATES, ROWS - STATES)] = jnp.zeros((ROWS - STATES, NODES, FIB), F32)

    def stacked(values):
        high, low = split(values)
        return jnp.concatenate([high, low, high], axis=0)

    def twice(values):
        return jnp.concatenate([values, values], axis=1)

    def first_pair(pair, _):
        node = 2 * pair
        old = jnp.concatenate(
            [s_flat[pl.ds(node + k, ROWS, stride=NODES), :] for k in range(2)], axis=1
        )
        volts = jnp.concatenate([volt_ref[pl.ds(node + k, 1), :] for k in range(2)], axis=1)
        gain = twice(gain_b[...])
        drive = dot(lhs_ref[...], stacked(old)) + gain * volts
        new = twice(keep_ref[...]) * old + time_step * jnp.tanh(drive)
        after = dot(lhs_ref[...], stacked(new))
        for k in range(2):
            lanes = slice(k * FIB, (k + 1) * FIB)
            s_work[node + k] = new[:, lanes]
            s_new[node + k] = after[:, lanes]
            cur_ref[pl.ds(node + k, 1), :] = after[STATES : STATES + 1, lanes]
        return 0

    for part in range(4):
        loads[part].wait()
        lax.fori_loop(part * (quarter // 2), (part + 1) * (quarter // 2), first_pair, 0, unroll=8)

    pl.semaphore_wait(barrier, GROUPS - 1 + N_LEN - 1 + 16)
    node_id = shard * NODES + iota((NODES, FIB), 0)
    total_nodes = NODES * N_LEN
    band = (node_id >= total_nodes // 2 - band_half) & (node_id < total_nodes // 2 + band_half)

    def cable_begin(step, volts):
        active = (fire == float(step)).astype(F32)
        pulse = jnp.where(band, amplitude * active, 0.0)
        right = volts + time_step * (pulse - cur_ref[...])
        both = dot_high(local_ref[shard], right)
        end_send[step] = both[NODES:]
        for other_step in range(1, N_LEN):
            other = lax.rem(shard + other_step, N_LEN)
            pltpu.make_async_remote_copy(
                end_send.at[step], end_recv.at[step, shard], len_send.at[step], len_recv.at[step],
                device_id={"fib": fib, "len": other, "emg": emg}, device_id_type=MESH,
            ).start()
        end_recv[step, shard] = jnp.zeros((8, FIB), F32)
        return both[:NODES]

    def cable_end(step, local):
        whole = end_recv.at[step, pl.ds(0, N_LEN - 1)]
        pltpu.make_async_copy(whole, whole, len_recv.at[step]).wait()
        far = end_recv[step].reshape(8 * N_LEN, FIB)
        return local + dot_high(far_ref[shard], far)

    def binned():
        first = cur_ref[pl.ds(0, BINS, stride=2), :]
        second = cur_ref[pl.ds(1, BINS, stride=2), :]
        return first + second

    local = cable_begin(0, volt_ref[...])
    exchange(cell_send, cell_recv, 0)
    row_send[0] = pack(binned())
    exchange(row_send.at[0], row_recv.at[0], 1)

    middle = 0.5 * (high_bound + low_bound)
    spread_width = 0.5 * (high_bound - low_bound)
    ratio = middle / spread_width
    lane = iota((BY, BZ), 1)
    sub = iota((BY, BZ), 0)
    zlane = iota((8, WRAP * BY), 1)
    zsub = iota((8, WRAP * BY), 0)
    zrow = lax.rem(zlane, BY)

    def inside(condition):
        return jnp.where(condition, 1.0, 0.0).astype(F32)

    fib_up, fib_down = inside(fib < N_FIB - 1), inside(fib > 0)
    len_up, len_down = inside(shard < N_LEN - 1), inside(shard > 0)
    emg_up, emg_down = inside(emg < N_EMG - 1), inside(emg > 0)
    margin = jnp.where(sub < 4, fib_up, fib_down)
    zmask = jnp.where(zsub < 4, emg_up, emg_down)
    zmask = zmask * jnp.where(zlane < 256, 1.0, jnp.where(zlane < 320, len_up, len_down))
    zmasks = (zmask, zmask * jnp.where(zrow < 4, fib_up, fib_down))

    def spread_out(kind, own):
        flat = own.reshape(BINS * BY, BZ)
        pick = jnp.where(iota((8, BZ), 0) < 4, iota((8, BZ), 0), iota((8, BZ), 0) + BZ - 8)
        pick = (iota((8, BZ), 1) == pick).astype(F32)
        side = dot_t(pick, flat[...], HIGH)
        for half in range(2):
            for tile in range(2):
                z_send[kind, half, tile] = side[4 * half :][:4, tile * BZ :][:, :BZ]
        for y in range(3):
            y_send[kind, 0, y * BINS : (y + 1) * BINS, :] = flat[pl.ds(y, BINS, stride=BY), :]
            y_send[kind, 1, y * BINS : (y + 1) * BINS, :] = flat[pl.ds(BY - 3 + y, BINS, stride=BY), :]

        def post(source, target, sem, device):
            pltpu.make_async_remote_copy(
                source, target, halo_ssem.at[kind, sem], halo_rsem.at[kind, sem],
                device_id=device, device_id_type=MESH,
            ).start()

        wide, tiles = wide_recv.at[kind], z_recv.at[kind]
        for half, de in ((0, -1), (1, 1)):
            base = 12 * half
            for f, df in enumerate((-1, 1)):
                for x, dl in enumerate((-1, 1)):
                    post(
                        z_send.at[kind, half, pl.ds(x, 1)],
                        tiles.at[pl.ds(base + 8 + 2 * f + x, 1)], 1, towards(df, dl, de),
                    )
            for f, df in enumerate((-1, 1)):
                post(
                    z_send.at[kind, half], tiles.at[pl.ds(base + 4 + 2 * f, 2)], 1, towards(df, 0, de)
                )
            for x, dl in enumerate((-1, 1)):
                post(
                    z_send.at[kind, half, pl.ds(x, 1)], tiles.at[pl.ds(base + 2 + x, 1)], 1,
                    towards(0, dl, de),
                )
            post(z_send.at[kind, half], tiles.at[pl.ds(base, 2)], 1, towards(0, 0, de))
        for f, df in enumerate((-1, 1)):
            for x, dl in enumerate((-1, 1)):
                post(
                    flat.at[pl.ds(x * (BINS - 2) * BY, 2 * BY)],
                    wide.at[pl.ds(240 + 32 * f + 16 * x, 16)], 0, towards(df, dl, 0),
                )
        post(y_send.at[kind, 0], wide.at[pl.ds(96, 96)], 0, towards(-1, 0, 0))
        post(y_send.at[kind, 1], wide.at[pl.ds(0, 96)], 0, towards(1, 0, 0))
        post(flat.at[pl.ds(0, 24)], wide.at[pl.ds(216, 24)], 0, towards(0, -1, 0))
        post(flat.at[pl.ds((BINS - 3) * BY, 24)], wide.at[pl.ds(192, 24)], 0, towards(0, 1, 0))

    def assemble(kind, own, field, zfield, add):
        def plus(values):
            return values + add if add else values

        wide, tiles = wide_recv.at[kind], z_recv.at[kind]
        pltpu.make_async_copy(wide, wide, halo_rsem.at[kind, 0]).wait()
        pltpu.make_async_copy(tiles, tiles, halo_rsem.at[kind, 1]).wait()
        field[0, pl.ds(0, BINS)] = plus(own[...])
        for k in range(3):
            field[0, BINS + k] = plus(wide[216 + 8 * k : 224 + 8 * k, :] * len_up)
            field[0, WRAP - 3 + k] = plus(wide[192 + 8 * k : 200 + 8 * k, :] * len_down)
        beside = field.at[1].reshape(WRAP * BY, BZ)
        for y in range(3):
            beside[pl.ds(y, BINS, stride=BY), :] = plus(wide[96 + 32 * y : 128 + 32 * y, :] * fib_up)
            beside[pl.ds(BY - 3 + y, BINS, stride=BY), :] = plus(wide[32 * y : 32 * y + 32, :] * fib_down)
        for k in range(2):
            for x, (place, weight) in enumerate(((BINS, len_up), (WRAP - 2, len_down))):
                start = 240 + 16 * x + 8 * k
                up, down = wide[start : start + 8, :], wide[start + 32 : start + 40, :]
                edge = jnp.where(sub < 4, up * fib_up, down * fib_down)
                field[1, place + k] = plus(edge * weight)
        low = iota((4, BZ), 1) < BZ // 2
        near = lax.rem(iota((4, BZ), 1), BY) < 4
        for half, weight in ((0, emg_up), (1, emg_down)):
            base = 12 * half
            rows = slice(4 * half, 4 * half + 4)
            for tile in range(2):
                lanes = slice(tile * BZ, (tile + 1) * BZ)
                zfield[0, rows, lanes] = plus(tiles[base + tile] * weight)
                up, down = tiles[base + 4 + tile] * fib_up, tiles[base + 6 + tile] * fib_down
                zfield[1, rows, lanes] = plus(jnp.where(near, up, down) * weight)
            lanes = slice(2 * BZ, 3 * BZ)
            both = jnp.where(low, tiles[base + 2] * len_up, tiles[base + 3] * len_down)
            zfield[0, rows, lanes] = plus(both * weight)
            up = jnp.where(low, tiles[base + 8] * len_up, tiles[base + 9] * len_down)
            down = jnp.where(low, tiles[base + 10] * len_up, tiles[base + 11] * len_down)
            both = jnp.where(near, up * fib_up, down * fib_down)
            zfield[1, rows, lanes] = plus(both * weight)

    def scatter(step):
        exchange_wait(row_recv.at[step], 1 + step)
        rows = row_recv[step].reshape(packed, FIB)
        turned = rows.T
        wide = jnp.concatenate([turned[q * BINS : (q + 1) * BINS] for q in range(4)], axis=1)
        both = dot(jnp.concatenate(split(wide), axis=0), hot_ref[...])
        source = both[:BINS] + both[BINS:]
        flat = own_ref.at[step].reshape(BINS * BY, BZ)
        for y in range(BY):
            flat[pl.ds(y, BINS, stride=BY), :] = source[:, y * BZ : (y + 1) * BZ]

    weight = [1.0 / ratio]
    for _ in range(SWEEPS - 1):
        weight.append(1.0 / (2.0 * ratio - weight[-1]))

    def sweep(step, turn):
        first, last = turn == 0, turn == SWEEPS - 2
        keep = weight[turn + 1] * weight[turn]
        gain = 2.0 * weight[turn + 1] / spread_width
        scale = 1.0 / middle if first else 1.0
        field = r_ref.at[step] if first else d_ref.at[step]
        zfield = zr_ref.at[step] if first else zd_ref.at[step]
        inject = ((iota((8, BZ), 0) == BY - 1) & (iota((8, BZ), 1) == 0)).astype(F32)
        inject = inject + ((iota((8, BZ), 0) == 0) & (iota((8, BZ), 1) == BZ - 1)).astype(F32)
        ends = ((iota((8, BZ), 0) == 0) & (iota((8, BZ), 1) == BZ - 1)).astype(F32)
        ends = ends + ((iota((8, BZ), 0) == BY - 1) & (iota((8, BZ), 1) == 0)).astype(F32)
        count = BINS if last else WRAP
        for tile in range(1 if last else 2):
            injected = dot_tl(zfield[tile, :, : count * BY], inject, HIGH)
            hz_ref[tile, pl.ds(0, count)] = injected.reshape(count, BY, BZ)

        def advance(here, beside, diagonal, rest, push):
            if first:
                rest = here - scale * (diagonal * here - beside)
            else:
                rest = rest - (diagonal * here - beside)
            return rest, (keep * scale) * here + push * rest

        if not last:
            zs = [zfield[0], zfield[1]]
            edges = [dot_t(ends, field.at[t].reshape(WRAP * BY, BZ)[...], HIGH) for t in range(2)]
            up = [pltpu.roll(z, 1, 1) for z in zs]
            down = [pltpu.roll(z, WRAP * BY - 1, 1) for z in zs]
            up_far = [pltpu.roll(z, WRAP * BY - BY + 1, 1) for z in zs]
            down_far = [pltpu.roll(z, BY - 1, 1) for z in zs]
            for t in range(2):
                beside = pltpu.roll(zs[t], BY, 1) + pltpu.roll(zs[t], WRAP * BY - BY, 1)
                beside = beside + jnp.where(zrow == 0, up_far[1 - t], up[t])
                beside = beside + jnp.where(zrow == BY - 1, down_far[1 - t], down[t])
                beside = beside + jnp.where(zsub == 0, edges[t], pltpu.roll(zs[t], 1, 0))
                beside = beside + jnp.where(zsub == 7, edges[t], pltpu.roll(zs[t], 7, 0))
                rest, after = advance(
                    zs[t], beside, zt_ref[t], None if first else zr_ref[step, t], gain * zmasks[t]
                )
                zr_ref[step, t] = rest
                zd_ref[step, t] = after

        def slab(place, following, previous, push, own):
            here = (field[0, place], field[1, place])
            up = [pltpu.roll(h, 1, 0) for h in here]
            down = [pltpu.roll(h, BY - 1, 0) for h in here]
            for t in range(1 if last else 2):
                beside = previous[t] + field[t, following] + hz_ref[t, place]
                beside = beside + jnp.where(sub == 0, up[1 - t], up[t])
                beside = beside + jnp.where(sub == BY - 1, down[1 - t], down[t])
                beside = beside + jnp.where(lane == 0, 0.0, pltpu.roll(here[t], 1, 1))
                beside = beside + jnp.where(lane == BZ - 1, 0.0, pltpu.roll(here[t], BZ - 1, 1))
                rest, after = advance(
                    here[t], beside, t_ref[t, place], None if first else r_ref[step, t, place],
                    push if t == 0 else push * margin,
                )
                if not last:
                    r_ref[step, t, place] = rest
                    d_ref[step, t, place] = after
                if own and t == 0:
                    if last:
                        pot_out[step, place] = x_ref[step, place] + after
                    elif first:
                        x_ref[step, place] = scale * here[0] + after
                    else:
                        x_ref[step, place] = x_ref[step, place] + after
            return here

        reach = SWEEPS - 2 - turn
        start = (WRAP - 1 - reach) % WRAP
        previous = (field[0, start], field[1, start])
        for k in range(reach):
            place = start + 1 + k
            previous = slab(place, (place + 1) % WRAP, previous, gain * len_down, False)
        previous = lax.fori_loop(
            0, BINS, lambda x, before: slab(x, x + 1, before, gain, True), previous, unroll=8
        )
        for k in range(reach):
            previous = slab(BINS + k, BINS + k + 1, previous, gain * len_up, False)

    spread_out(STEPS, tissue_ref)
    r_ref[...] = jnp.zeros_like(r_ref)
    d_ref[...] = jnp.zeros_like(d_ref)
    t_ref[...] = jnp.zeros_like(t_ref)
    v1_ref[...] = cable_end(0, local)

    o_flat = states_out.reshape(STATES * NODES, FIB)

    def second(node, _):
        drive = s_new[node] + gain_b[...] * v1_ref[pl.ds(node, 1), :]
        new = keep_ref[...] * s_work[node] + time_step * jnp.tanh(drive)
        o_flat[pl.ds(node, STATES, stride=NODES), :] = new[:STATES]
        cur_ref[pl.ds(node, 1), :] = jnp.sum(wts_b[...] * new, axis=0, keepdims=True)
        return 0

    lax.fori_loop(0, NODES, second, 0, unroll=8)
    row_send[1] = pack(binned())
    exchange(row_send.at[1], row_recv.at[1], 2)
    local = cable_begin(1, v1_ref[...])

    exchange_wait(cell_recv, 0)
    cells = cell_recv[...].reshape(packed, FIB)
    for q in range(4):
        column_q = cells[:, q * BINS : q * BINS + 1].astype(jnp.int32)
        for y in range(BY):
            hot = (column_q == iota((packed, BZ), 1) + y * BZ).astype(F32).astype(BF16)
            hot_ref[q * packed : (q + 1) * packed, y * BZ : (y + 1) * BZ] = hot

    scatter(0)
    spread_out(0, own_ref.at[0])
    assemble(STEPS, tissue_ref, t_ref, zt_ref, 6.0)
    volt_out[...] = cable_end(1, local)
    scatter(1)
    spread_out(1, own_ref.at[1])
    for step in range(STEPS):
        assemble(step, own_ref.at[step], r_ref.at[step], zr_ref.at[step], 0.0)
        for turn in range(SWEEPS - 1):
            sweep(step, turn)

    exchange_sent(cell_send, 0)
    for step in range(STEPS):
        exchange_sent(row_send.at[step], 1 + step)
        whole = end_recv.at[step, pl.ds(0, N_LEN - 1)]
        pltpu.make_async_copy(whole, whole, len_send.at[step]).wait()
    for kind in range(STEPS + 1):
        for number, sent in enumerate((wide_recv.at[kind], z_recv.at[kind])):
            pltpu.make_async_copy(sent, sent, halo_ssem.at[kind, number]).wait()


def write_out(states, voltage, potential, states_out, voltage_out, potential_out, sem):
    cuts = (0, 15, 29, 43, STATES)
    copies = [
        pltpu.make_async_copy(
            states.at[pl.ds(cuts[k], cuts[k + 1] - cuts[k])],
            states_out.at[pl.ds(cuts[k], cuts[k + 1] - cuts[k])],
            sem.at[k],
        )
        for k in range(4)
    ]
    copies.append(pltpu.make_async_copy(potential, potential_out, sem.at[4]))
    copies.append(pltpu.make_async_copy(voltage, voltage_out, sem.at[5]))
    for copy in copies:
        copy.start()
    for copy in copies:
        copy.wait()


def on_device(
    states, voltage, coupling, decay_rates, volt_gain, current_weights,
    fibre_home, cross_cell, motor_unit, stim_step, tissue,
):
    local, far = cable_tables()
    vmem = pl.BlockSpec(memory_space=pltpu.VMEM)
    hbm = pl.BlockSpec(memory_space=pltpu.HBM)
    outputs = pl.pallas_call(
        kernel,
        out_shape=(
            jax.ShapeDtypeStruct(states.shape, F32),
            jax.ShapeDtypeStruct(voltage.shape, F32),
            jax.ShapeDtypeStruct((STEPS, *tissue.shape), F32),
        ),
        in_specs=[hbm] * 13,
        out_specs=(vmem, vmem, vmem),
        scratch_shapes=[
            pltpu.VMEM(voltage.shape, F32),
            pltpu.VMEM(coupling.shape, F32),
            pltpu.VMEM((1, STATES), F32),
            pltpu.VMEM((1, STATES), F32),
            pltpu.VMEM((1, STATES), F32),
            pltpu.VMEM((1, FIB), jnp.int32),
            pltpu.VMEM((1, FIB), jnp.int32),
            pltpu.VMEM((1, FIB), jnp.int32),
            pltpu.VMEM((1, stim_step.shape[0]), jnp.int32),
            pltpu.VMEM(tissue.shape, F32),
            pltpu.VMEM(local.shape, F32),
            pltpu.VMEM(far.shape, F32),
            pltpu.VMEM((ROWS, NODES, FIB), F32),
            pltpu.VMEM((NODES, ROWS, FIB), F32),
            pltpu.VMEM((NODES, ROWS, FIB), F32),
            pltpu.VMEM((ROWS, 3 * ROWS), BF16),
            pltpu.VMEM((ROWS, FIB), F32),
            pltpu.VMEM((ROWS, FIB), F32),
            pltpu.VMEM((ROWS, FIB), F32),
            pltpu.VMEM((NODES, FIB), F32),
            pltpu.VMEM((NODES, FIB), F32),
            pltpu.VMEM((4 * GROUPS * SLOT_ROWS, BY * BZ), BF16),
            pltpu.VMEM((GROUPS * SLOT_ROWS, 4 * FIB), BF16),
            pltpu.VMEM((GROUPS, SLOT_ROWS, FIB), F32),
            pltpu.VMEM((GROUPS, SLOT_ROWS, FIB), F32),
            pltpu.VMEM((STEPS, GROUPS, SLOT_ROWS, FIB), F32),
            pltpu.VMEM((STEPS, GROUPS, SLOT_ROWS, FIB), F32),
            pltpu.VMEM((STEPS, 8, FIB), F32),
            pltpu.VMEM((STEPS, N_LEN, 8, FIB), F32),
            pltpu.VMEM((STEPS, BINS, BY, BZ), F32),
            pltpu.VMEM((STEPS, BINS, BY, BZ), F32),
            pltpu.VMEM((STEPS, 2, WRAP, BY, BZ), F32),
            pltpu.VMEM((STEPS, 2, WRAP, BY, BZ), F32),
            pltpu.VMEM((2, WRAP, BY, BZ), F32),
            pltpu.VMEM((STEPS, 2, 8, WRAP * BY), F32),
            pltpu.VMEM((STEPS, 2, 8, WRAP * BY), F32),
            pltpu.VMEM((2, 8, WRAP * BY), F32),
            pltpu.VMEM((2, WRAP, BY, BZ), F32),
            pltpu.VMEM((STEPS + 1, 2, 3 * BINS, BZ), F32),
            pltpu.VMEM((STEPS + 1, 2, 2, 4, BZ), F32),
            pltpu.VMEM((STEPS + 1, WIDE_ROWS, BZ), F32),
            pltpu.VMEM((STEPS + 1, Z_TILES, 4, BZ), F32),
            pltpu.SemaphoreType.DMA((4,)),
            pltpu.SemaphoreType.DMA((12,)),
            pltpu.SemaphoreType.DMA((3,)),
            pltpu.SemaphoreType.DMA((3,)),
            pltpu.SemaphoreType.DMA((STEPS,)),
            pltpu.SemaphoreType.DMA((STEPS,)),
            pltpu.SemaphoreType.DMA((STEPS + 1, 2)),
            pltpu.SemaphoreType.DMA((STEPS + 1, 2)),
        ],
        compiler_params=pltpu.CompilerParams(collective_id=0, has_side_effects=True, vmem_limit_bytes=VMEM_LIMIT),
    )(*(pltpu.with_memory_space_constraint(array, pltpu.HBM) for array in (
        states, voltage, coupling, decay_rates.reshape(1, -1), volt_gain.reshape(1, -1),
        current_weights.reshape(1, -1), fibre_home.reshape(1, -1), cross_cell.reshape(1, -1),
        motor_unit.reshape(1, -1), stim_step.reshape(1, -1), tissue, local, far,
    )))
    return pl.pallas_call(
        write_out,
        out_shape=tuple(jax.ShapeDtypeStruct(array.shape, F32) for array in outputs),
        in_specs=[vmem] * 3,
        out_specs=(pl.BlockSpec(memory_space=pl.ANY),) * 3,
        scratch_shapes=[pltpu.SemaphoreType.DMA((6,))],
        compiler_params=pltpu.CompilerParams(vmem_limit_bytes=VMEM_LIMIT),
    )(*(pltpu.with_memory_space_constraint(array, pltpu.VMEM) for array in outputs))


def solution(mesh):
    return jax.shard_map(
        on_device,
        mesh=mesh,
        in_specs=(
            P(None, "len", ("fib", "emg")),
            P("len", ("fib", "emg")),
            P(),
            P(),
            P(),
            P(),
            P(("fib", "emg"), None),
            P(("fib", "emg")),
            P(("fib", "emg")),
            P(),
            P("len", "fib", "emg"),
        ),
        out_specs=(
            P(None, "len", ("fib", "emg")),
            P("len", ("fib", "emg")),
            P(None, "len", "fib", "emg"),
        ),
        check_vma=False,
    )
```

```python
import math

import jax
import jax.numpy as jnp
import numpy as np
from jax import lax
from jax.experimental import pallas as pl
from jax.experimental.pallas import tpu as pltpu
from jax.sharding import PartitionSpec as P

STEPS = 2
SWEEPS = 4
NPC = 2

time_step = 0.5
conductance = 2000.0
amplitude = 200.0
band_half = 4
low_bound = 0.5
high_bound = 14.0

MESH = pl.DeviceIdType.MESH
HIGH = lax.Precision.HIGHEST
F32 = jnp.float32
BF16 = jnp.bfloat16

N_FIB, N_LEN, N_EMG = 8, 4, 4
GROUPS = N_FIB * N_EMG
STATES = 57
ROWS = 64
NODES = 64
FIB = 128
BINS = NODES // NPC
BY, BZ = 8, 128
SLOT_ROWS = 4
CAPACITY = 12
WIDE_ROWS = 304
Z_TILES = 24
WRAP = 48
VMEM_LIMIT = 24 << 20
UNROLL = 31
WRITES = 12


def cable_tables():
    total = NODES * N_LEN
    theta = math.acosh(1.0 + 0.5 / conductance)
    scale = conductance * math.sinh(theta) * math.sinh(total * theta)
    u = np.array([math.cosh((i + 0.5) * theta) for i in range(total)])
    v = np.array([math.cosh((total - 0.5 - i) * theta) / scale for i in range(total)])
    index = np.arange(NODES)
    local = np.zeros((N_LEN, NODES + 8, NODES))
    far = np.zeros((N_LEN, NODES, 8 * N_LEN))
    for shard in range(N_LEN):
        us, vs = u[shard * NODES :][:NODES], v[shard * NODES :][:NODES]
        low = index[:, None] <= index[None, :]
        local[shard, :NODES] = np.where(low, us[:, None] * vs[None, :], vs[:, None] * us[None, :])
        local[shard, NODES] = us
        local[shard, NODES + 1] = vs
        for other in range(N_LEN):
            if other < shard:
                far[shard, :, 8 * other] = vs
            if other > shard:
                far[shard, :, 8 * other + 1] = us
    return jnp.asarray(local, F32), jnp.asarray(far, F32)


def iota(shape, axis):
    return lax.broadcasted_iota(jnp.int32, shape, axis)


def split(values):
    high = values.astype(BF16)
    return high, (values - high.astype(F32)).astype(BF16)


def dot(a, b):
    return jnp.dot(a, b, preferred_element_type=F32)


def dot_high(a, b):
    return jnp.dot(a, b, preferred_element_type=F32, precision=HIGH)


def dot_t(a, b, precision=None):
    return lax.dot_general(
        a, b, (((1,), (1,)), ((), ())), preferred_element_type=F32, precision=precision
    )


def dot_tl(a, b, precision=None):
    return lax.dot_general(
        a, b, (((0,), (0,)), ((), ())), preferred_element_type=F32, precision=precision
    )


def kernel(
    states_hbm, volt_hbm, coup_hbm, decay_hbm, gain_hbm, wts_hbm, home_hbm, cell_hbm, mu_hbm,
    stim_hbm, tissue_hbm, local_hbm, far_hbm,
    states_out, volt_out, pot_out,
    volt_ref, coup_ref, decay_ref, gain_ref, wts_ref, home_ref, cell_ref, mu_ref,
    stim_ref, tissue_ref, local_ref, far_ref,
    s_in, s_work, s_new, lhs_ref, keep_ref, gain_b, wts_b, cur_ref, v1_ref, hot_ref, sel_ref,
    cell_send, cell_recv, row_send, row_recv, end_send, end_recv,
    own_ref, x_ref, r_ref, d_ref, t_ref, zr_ref, zd_ref, zt_ref, hz_ref,
    y_send, z_send, wide_recv, z_recv,
    in_sem, out_sem, small_sem, a2a_send, a2a_recv, len_send, len_recv, halo_ssem, halo_rsem,
):
    fib, shard, emg = lax.axis_index("fib"), lax.axis_index("len"), lax.axis_index("emg")
    me = fib * N_EMG + emg

    smalls = [
        pltpu.make_async_copy(source, target, small_sem.at[number])
        for number, (source, target) in enumerate((
            (coup_hbm, coup_ref), (decay_hbm, decay_ref), (gain_hbm, gain_ref), (wts_hbm, wts_ref),
            (home_hbm, home_ref), (cell_hbm, cell_ref), (mu_hbm, mu_ref), (stim_hbm, stim_ref),
            (volt_hbm, volt_ref), (local_hbm, local_ref), (far_hbm, far_ref),
            (tissue_hbm, tissue_ref),
        ))
    ]
    for copy in smalls[:4] + smalls[8:9]:
        copy.start()
    barrier = pltpu.get_barrier_semaphore()

    def peer(step):
        other = lax.rem(me + step, GROUPS)
        return {"fib": other // N_EMG, "len": shard, "emg": lax.rem(other, N_EMG)}, other

    def towards(df, dl, de):
        return {
            "fib": lax.rem(fib + N_FIB + df, N_FIB),
            "len": lax.rem(shard + N_LEN + dl, N_LEN),
            "emg": lax.rem(emg + N_EMG + de, N_EMG),
        }

    def greet(step, _):
        device, _other = peer(step)
        pl.semaphore_signal(barrier, inc=1, device_id=device, device_id_type=MESH)
        return 0

    lax.fori_loop(1, GROUPS, greet, 0, unroll=UNROLL)
    for step in range(1, N_LEN):
        other = lax.rem(shard + step, N_LEN)
        pl.semaphore_signal(
            barrier, inc=1, device_id={"fib": fib, "len": other, "emg": emg}, device_id_type=MESH
        )

    for df in (-1, 0, 1):
        for de in (-1, 0, 1):
            for dl in (-1, 1):
                if (df, de) != (0, 0):
                    pl.semaphore_signal(
                        barrier, inc=1, device_id=towards(df, dl, de), device_id_type=MESH
                    )

    s_in[:, pl.ds(STATES, ROWS - STATES), :] = jnp.zeros((NODES, ROWS - STATES, FIB), F32)
    quarter = NODES // 4
    for part in range(4):

        def take(node, _, part=part):
            pltpu.make_async_copy(
                states_hbm.at[:, node, :], s_in.at[node, pl.ds(0, STATES), :], in_sem.at[part]
            ).start()
            return 0

        lax.fori_loop(part * quarter, (part + 1) * quarter, take, 0, unroll=16)
    for copy in smalls[4:8] + smalls[9:]:
        copy.start()

    def column(row):
        wide = row.shape[1]
        picked = jnp.where(iota((ROWS, wide), 0) == iota((ROWS, wide), 1), row, 0.0)
        return dot_high(picked, jnp.ones((wide, FIB), F32))

    for copy in smalls[:4]:
        copy.wait()
    keep_ref[...] = 1.0 - time_step * column(decay_ref[...])
    gain_b[...] = column(gain_ref[...])
    wts_b[...] = column(wts_ref[...])
    spread = (iota((STATES, 3 * ROWS), 0) == lax.rem(iota((STATES, 3 * ROWS), 1), ROWS)).astype(F32)
    tiled = dot_high(coup_ref[...], spread)
    tiled = jnp.concatenate([tiled, jnp.zeros((ROWS - STATES, 3 * ROWS), F32)], axis=0)
    high, low = split(tiled)
    lhs_ref[...] = jnp.where(iota((ROWS, 3 * ROWS), 1) < 2 * ROWS, high.astype(F32), low.astype(F32)).astype(BF16)


    def stacked(values):
        high, low = split(values)
        return jnp.concatenate([high, low, high], axis=0)

    def twice(values):
        return jnp.concatenate([values, values], axis=1)

    def first_pair(pair, _):
        node = 2 * pair
        old = jnp.concatenate([s_in[node], s_in[node + 1]], axis=1)
        volts = jnp.concatenate([volt_ref[pl.ds(node + k, 1), :] for k in range(2)], axis=1)
        gain = twice(gain_b[...])
        drive = dot(lhs_ref[...], stacked(old)) + gain * volts
        new = twice(keep_ref[...]) * old + time_step * jnp.tanh(drive)
        for k in range(2):
            part = new[:, k * FIB : (k + 1) * FIB]
            s_work[node + k] = part
            cur_ref[pl.ds(node + k, 1), :] = jnp.sum(wts_b[...] * part, axis=0, keepdims=True)
        return 0

    def next_pair(pair, _):
        node = 2 * pair
        new = jnp.concatenate([s_work[node], s_work[node + 1]], axis=1)
        after = dot(lhs_ref[...], stacked(new))
        for k in range(2):
            s_new[node + k] = after[:, k * FIB : (k + 1) * FIB]
        return 0

    smalls[8].wait()

    for part in range(4):
        block = s_in.at[pl.ds(part * quarter, quarter), pl.ds(0, STATES), :]
        pltpu.make_async_copy(block, block, in_sem.at[part]).wait()
        lax.fori_loop(part * (quarter // 2), (part + 1) * (quarter // 2), first_pair, 0, unroll=8)

    for copy in smalls[4:8] + smalls[9:]:
        copy.wait()
    unit_hot = (iota((FIB, FIB), 0) == mu_ref[...]).astype(F32)
    stim_row = jnp.concatenate(
        [stim_ref[...].astype(F32), jnp.zeros((1, FIB - stim_ref.shape[1]), F32)], axis=1
    )
    fire = dot(stim_row.astype(BF16), unit_hot.astype(BF16))

    pl.semaphore_wait(barrier, GROUPS - 1 + N_LEN - 1 + 16)
    node_id = shard * NODES + iota((NODES, FIB), 0)
    total_nodes = NODES * N_LEN
    band = (node_id >= total_nodes // 2 - band_half) & (node_id < total_nodes // 2 + band_half)

    def cable_begin(step, volts):
        active = (fire == float(step)).astype(F32)
        pulse = jnp.where(band, amplitude * active, 0.0)
        right = volts + time_step * (pulse - cur_ref[...])
        both = dot_high(local_ref[shard], right)
        end_send[step] = both[NODES:]
        for other_step in range(1, N_LEN):
            other = lax.rem(shard + other_step, N_LEN)
            pltpu.make_async_remote_copy(
                end_send.at[step], end_recv.at[step, shard], len_send.at[step], len_recv.at[step],
                device_id={"fib": fib, "len": other, "emg": emg}, device_id_type=MESH,
            ).start()
        end_recv[step, shard] = jnp.zeros((8, FIB), F32)
        return both[:NODES]

    def cable_end(step, local):
        whole = end_recv.at[step, pl.ds(0, N_LEN - 1)]
        pltpu.make_async_copy(whole, whole, len_recv.at[step]).wait()
        far = end_recv[step].reshape(8 * N_LEN, FIB)
        return local + dot_high(far_ref[shard], far)

    def binned():
        first = cur_ref[pl.ds(0, BINS, stride=2), :]
        second = cur_ref[pl.ds(1, BINS, stride=2), :]
        return first + second

    local = cable_begin(0, volt_ref[...])
    home = home_ref[...]
    member = (iota((GROUPS, FIB), 0) == home).astype(F32)
    before = (iota((FIB, FIB), 0) < iota((FIB, FIB), 1)).astype(BF16)
    earlier = dot(member.astype(BF16), before)
    rank = jnp.sum(earlier * member, axis=0, keepdims=True).astype(jnp.int32)
    slot = home * CAPACITY + rank
    packed = GROUPS * SLOT_ROWS
    row_id = iota((packed, FIB), 0)
    in_brick = lax.rem(row_id, SLOT_ROWS)
    first_slot = (row_id // SLOT_ROWS) * CAPACITY + 4 * in_brick
    for q in range(4):
        chosen = (slot == first_slot + q) & (in_brick < CAPACITY // 4)
        sel_ref[:, q * FIB : (q + 1) * FIB] = chosen.astype(F32).astype(BF16)

    def pack(values):
        blank = jnp.zeros((BINS, FIB), BF16)
        total = None
        for part in split(values):
            block = jnp.concatenate(
                [
                    jnp.concatenate([part if q == row else blank for q in range(4)], axis=1)
                    for row in range(4)
                ],
                axis=0,
            )
            term = dot_t(sel_ref[...], block)
            total = term if total is None else total + term
        return total.reshape(GROUPS, SLOT_ROWS, FIB)

    def exchange(source, target, slot_index):
        def send(step, _):
            device, other = peer(step)
            pltpu.make_async_remote_copy(
                source.at[other], target.at[me], a2a_send.at[slot_index], a2a_recv.at[slot_index],
                device_id=device, device_id_type=MESH,
            ).start()
            return 0

        lax.fori_loop(1, GROUPS, send, 0, unroll=UNROLL)
        target[me] = source[me]

    def exchange_wait(target, slot_index):
        whole = target.at[pl.ds(0, GROUPS - 1)]
        pltpu.make_async_copy(whole, whole, a2a_recv.at[slot_index]).wait()

    def exchange_sent(source, slot_index):
        whole = source.at[pl.ds(0, GROUPS - 1)]
        pltpu.make_async_copy(whole, whole, a2a_send.at[slot_index]).wait()

    cell_row = jnp.broadcast_to(cell_ref[...].astype(F32), (BINS, FIB))
    cell_send[...] = pack(cell_row)

    exchange(cell_send, cell_recv, 0)
    row_send[0] = pack(binned())
    exchange(row_send.at[0], row_recv.at[0], 1)

    middle = 0.5 * (high_bound + low_bound)
    spread_width = 0.5 * (high_bound - low_bound)
    ratio = middle / spread_width
    lane = iota((BY, BZ), 1)
    sub = iota((BY, BZ), 0)
    zlane = iota((8, WRAP * BY), 1)
    zsub = iota((8, WRAP * BY), 0)
    zrow = lax.rem(zlane, BY)

    def inside(condition):
        return jnp.where(condition, 1.0, 0.0).astype(F32)

    fib_up, fib_down = inside(fib < N_FIB - 1), inside(fib > 0)
    len_up, len_down = inside(shard < N_LEN - 1), inside(shard > 0)
    emg_up, emg_down = inside(emg < N_EMG - 1), inside(emg > 0)
    margin = jnp.where(sub < 4, fib_up, fib_down)
    zmask = jnp.where(zsub < 4, emg_up, emg_down)
    zmask = zmask * jnp.where(zlane < 256, 1.0, jnp.where(zlane < 320, len_up, len_down))
    zmasks = (zmask, zmask * jnp.where(zrow < 4, fib_up, fib_down))

    def spread_out(kind, own):
        flat = own.reshape(BINS * BY, BZ)
        for tile in range(2):
            turned = flat[tile * BZ : (tile + 1) * BZ, :].T
            z_send[kind, 0, tile] = turned[:4]
            z_send[kind, 1, tile] = turned[BZ - 4 :]
        for y in range(3):
            y_send[kind, 0, y * BINS : (y + 1) * BINS, :] = flat[pl.ds(y, BINS, stride=BY), :]
            y_send[kind, 1, y * BINS : (y + 1) * BINS, :] = flat[pl.ds(BY - 3 + y, BINS, stride=BY), :]

        def post(source, target, sem, device):
            pltpu.make_async_remote_copy(
                source, target, halo_ssem.at[kind, sem], halo_rsem.at[kind, sem],
                device_id=device, device_id_type=MESH,
            ).start()

        wide, tiles = wide_recv.at[kind], z_recv.at[kind]
        for half, de in ((0, -1), (1, 1)):
            base = 12 * half
            for f, df in enumerate((-1, 1)):
                for x, dl in enumerate((-1, 1)):
                    post(
                        z_send.at[kind, half, pl.ds(x, 1)],
                        tiles.at[pl.ds(base + 8 + 2 * f + x, 1)], 1, towards(df, dl, de),
                    )
            for f, df in enumerate((-1, 1)):
                post(
                    z_send.at[kind, half], tiles.at[pl.ds(base + 4 + 2 * f, 2)], 1, towards(df, 0, de)
                )
            for x, dl in enumerate((-1, 1)):
                post(
                    z_send.at[kind, half, pl.ds(x, 1)], tiles.at[pl.ds(base + 2 + x, 1)], 1,
                    towards(0, dl, de),
                )
            post(z_send.at[kind, half], tiles.at[pl.ds(base, 2)], 1, towards(0, 0, de))
        for f, df in enumerate((-1, 1)):
            for x, dl in enumerate((-1, 1)):
                post(
                    flat.at[pl.ds(x * (BINS - 2) * BY, 2 * BY)],
                    wide.at[pl.ds(240 + 32 * f + 16 * x, 16)], 0, towards(df, dl, 0),
                )
        post(y_send.at[kind, 0], wide.at[pl.ds(96, 96)], 0, towards(-1, 0, 0))
        post(y_send.at[kind, 1], wide.at[pl.ds(0, 96)], 0, towards(1, 0, 0))
        post(flat.at[pl.ds(0, 24)], wide.at[pl.ds(216, 24)], 0, towards(0, -1, 0))
        post(flat.at[pl.ds((BINS - 3) * BY, 24)], wide.at[pl.ds(192, 24)], 0, towards(0, 1, 0))

    def assemble(kind, own, field, zfield, add):
        def plus(values):
            return values + add if add else values

        wide, tiles = wide_recv.at[kind], z_recv.at[kind]
        pltpu.make_async_copy(wide, wide, halo_rsem.at[kind, 0]).wait()
        pltpu.make_async_copy(tiles, tiles, halo_rsem.at[kind, 1]).wait()
        field[0, pl.ds(0, BINS)] = plus(own[...])
        for k in range(3):
            field[0, BINS + k] = plus(wide[216 + 8 * k : 224 + 8 * k, :] * len_up)
            field[0, WRAP - 3 + k] = plus(wide[192 + 8 * k : 200 + 8 * k, :] * len_down)
        beside = field.at[1].reshape(WRAP * BY, BZ)
        for y in range(3):
            beside[pl.ds(y, BINS, stride=BY), :] = plus(wide[96 + 32 * y : 128 + 32 * y, :] * fib_up)
            beside[pl.ds(BY - 3 + y, BINS, stride=BY), :] = plus(wide[32 * y : 32 * y + 32, :] * fib_down)
        for k in range(2):
            for x, (place, weight) in enumerate(((BINS, len_up), (WRAP - 2, len_down))):
                start = 240 + 16 * x + 8 * k
                up, down = wide[start : start + 8, :], wide[start + 32 : start + 40, :]
                edge = jnp.where(sub < 4, up * fib_up, down * fib_down)
                field[1, place + k] = plus(edge * weight)
        low = iota((4, BZ), 1) < BZ // 2
        near = lax.rem(iota((4, BZ), 1), BY) < 4
        for half, weight in ((0, emg_up), (1, emg_down)):
            base = 12 * half
            rows = slice(4 * half, 4 * half + 4)
            for tile in range(2):
                lanes = slice(tile * BZ, (tile + 1) * BZ)
                zfield[0, rows, lanes] = plus(tiles[base + tile] * weight)
                up, down = tiles[base + 4 + tile] * fib_up, tiles[base + 6 + tile] * fib_down
                zfield[1, rows, lanes] = plus(jnp.where(near, up, down) * weight)
            lanes = slice(2 * BZ, 3 * BZ)
            both = jnp.where(low, tiles[base + 2] * len_up, tiles[base + 3] * len_down)
            zfield[0, rows, lanes] = plus(both * weight)
            up = jnp.where(low, tiles[base + 8] * len_up, tiles[base + 9] * len_down)
            down = jnp.where(low, tiles[base + 10] * len_up, tiles[base + 11] * len_down)
            both = jnp.where(near, up * fib_up, down * fib_down)
            zfield[1, rows, lanes] = plus(both * weight)

    def scatter(step):
        exchange_wait(row_recv.at[step], 1 + step)
        rows = row_recv[step].reshape(packed, FIB)
        turned = rows.T
        wide = jnp.concatenate([turned[q * BINS : (q + 1) * BINS] for q in range(4)], axis=1)
        both = dot(jnp.concatenate(split(wide), axis=0), hot_ref[...])
        source = both[:BINS] + both[BINS:]
        flat = own_ref.at[step].reshape(BINS * BY, BZ)
        for y in range(BY):
            flat[pl.ds(y, BINS, stride=BY), :] = source[:, y * BZ : (y + 1) * BZ]

    weight = [1.0 / ratio]
    for _ in range(SWEEPS - 1):
        weight.append(1.0 / (2.0 * ratio - weight[-1]))

    def sweep(step, turn):
        first, last = turn == 0, turn == SWEEPS - 2
        keep = weight[turn + 1] * weight[turn]
        gain = 2.0 * weight[turn + 1] / spread_width
        scale = 1.0 / middle if first else 1.0
        field = r_ref.at[step] if first else d_ref.at[step]
        zfield = zr_ref.at[step] if first else zd_ref.at[step]
        blank = jnp.zeros((BZ - 16, BZ), F32)
        for tile in range(1 if last else 2):
            for block in range(2 if last else 3):
                z = zfield[tile, :, block * BZ : (block + 1) * BZ]
                first_lane = jnp.where(sub == 0, pltpu.roll(z, 1, 0), 0.0)
                last_lane = jnp.where(sub == 7, pltpu.roll(z, 7, 0), 0.0)
                turned = jnp.concatenate([first_lane, blank, last_lane], axis=0).T
                hz_ref[tile, pl.ds(16 * block, 16)] = turned.reshape(16, BY, BZ)

        def advance(here, beside, diagonal, rest, push):
            if first:
                rest = here - scale * (diagonal * here - beside)
            else:
                rest = rest - (diagonal * here - beside)
            return rest, (keep * scale) * here + push * rest

        if not last:
            zs = [zfield[0], zfield[1]]
            edges = []
            for t in range(2):
                parts = []
                for block in range(3):
                    turned = field[t, pl.ds(16 * block, 16)].reshape(BZ, BZ).T
                    ends = jnp.where(
                        sub == 0, pltpu.roll(turned[BZ - 8 :], 1, 0), pltpu.roll(turned[:8], 7, 0)
                    )
                    parts.append(ends)
                edges.append(jnp.concatenate(parts, axis=1))
            up = [pltpu.roll(z, 1, 1) for z in zs]
            down = [pltpu.roll(z, WRAP * BY - 1, 1) for z in zs]
            up_far = [pltpu.roll(z, WRAP * BY - BY + 1, 1) for z in zs]
            down_far = [pltpu.roll(z, BY - 1, 1) for z in zs]
            for t in range(2):
                beside = pltpu.roll(zs[t], BY, 1) + pltpu.roll(zs[t], WRAP * BY - BY, 1)
                beside = beside + jnp.where(zrow == 0, up_far[1 - t], up[t])
                beside = beside + jnp.where(zrow == BY - 1, down_far[1 - t], down[t])
                beside = beside + jnp.where(zsub == 0, edges[t], pltpu.roll(zs[t], 1, 0))
                beside = beside + jnp.where(zsub == 7, edges[t], pltpu.roll(zs[t], 7, 0))
                rest, after = advance(
                    zs[t], beside, zt_ref[t], None if first else zr_ref[step, t], gain * zmasks[t]
                )
                zr_ref[step, t] = rest
                zd_ref[step, t] = after

        def slab(place, following, previous, push, own):
            here = (field[0, place], field[1, place])
            up = [pltpu.roll(h, 1, 0) for h in here]
            down = [pltpu.roll(h, BY - 1, 0) for h in here]
            for t in range(1 if last else 2):
                beside = previous[t] + field[t, following] + hz_ref[t, place]
                beside = beside + jnp.where(sub == 0, up[1 - t], up[t])
                beside = beside + jnp.where(sub == BY - 1, down[1 - t], down[t])
                beside = beside + jnp.where(lane == 0, 0.0, pltpu.roll(here[t], 1, 1))
                beside = beside + jnp.where(lane == BZ - 1, 0.0, pltpu.roll(here[t], BZ - 1, 1))
                rest, after = advance(
                    here[t], beside, t_ref[t, place], None if first else r_ref[step, t, place],
                    push if t == 0 else push * margin,
                )
                if not last:
                    r_ref[step, t, place] = rest
                    d_ref[step, t, place] = after
                if own and t == 0:
                    if last:
                        pot_out[step, place] = x_ref[step, place] + after
                    elif first:
                        x_ref[step, place] = scale * here[0] + after
                    else:
                        x_ref[step, place] = x_ref[step, place] + after
            return here

        reach = SWEEPS - 2 - turn
        start = (WRAP - 1 - reach) % WRAP
        previous = (field[0, start], field[1, start])
        for k in range(reach):
            place = start + 1 + k
            previous = slab(place, (place + 1) % WRAP, previous, gain * len_down, False)
        previous = lax.fori_loop(
            0, BINS, lambda x, before: slab(x, x + 1, before, gain, True), previous, unroll=32
        )
        for k in range(reach):
            previous = slab(BINS + k, BINS + k + 1, previous, gain * len_up, False)

    spread_out(STEPS, tissue_ref)
    r_ref[...] = jnp.zeros_like(r_ref)
    d_ref[...] = jnp.zeros_like(d_ref)
    t_ref[...] = jnp.zeros_like(t_ref)
    lax.fori_loop(0, NODES // 2, next_pair, 0, unroll=8)
    v1_ref[...] = cable_end(0, local)

    def second(node, _):
        drive = s_new[node] + gain_b[...] * v1_ref[pl.ds(node, 1), :]
        new = keep_ref[...] * s_work[node] + time_step * jnp.tanh(drive)
        s_in[node] = new
        cur_ref[pl.ds(node, 1), :] = jnp.sum(wts_b[...] * new, axis=0, keepdims=True)
        return 0

    lax.fori_loop(0, NODES, second, 0, unroll=8)
    row_send[1] = pack(binned())
    exchange(row_send.at[1], row_recv.at[1], 2)
    local = cable_begin(1, v1_ref[...])

    exchange_wait(cell_recv, 0)
    cells = cell_recv[...].reshape(packed, FIB)
    for q in range(4):
        column_q = cells[:, q * BINS : q * BINS + 1].astype(jnp.int32)
        for y in range(BY):
            hot = (column_q == iota((packed, BZ), 1) + y * BZ).astype(F32).astype(BF16)
            hot_ref[q * packed : (q + 1) * packed, y * BZ : (y + 1) * BZ] = hot

    scatter(0)
    spread_out(0, own_ref.at[0])
    def put(node, _):
        pltpu.make_async_copy(
            s_in.at[node, pl.ds(0, STATES), :], states_out.at[:, node, :], out_sem.at[0]
        ).start()
        return 0

    lax.fori_loop(0, NODES, put, 0, unroll=16)
    assemble(STEPS, tissue_ref, t_ref, zt_ref, 6.0)
    volt_out[...] = cable_end(1, local)
    scatter(1)
    spread_out(1, own_ref.at[1])
    for step in range(STEPS):
        assemble(step, own_ref.at[step], r_ref.at[step], zr_ref.at[step], 0.0)
        for turn in range(SWEEPS - 1):
            sweep(step, turn)

    pltpu.make_async_copy(states_out, states_out, out_sem.at[0]).wait()
    exchange_sent(cell_send, 0)
    for step in range(STEPS):
        exchange_sent(row_send.at[step], 1 + step)
        whole = end_recv.at[step, pl.ds(0, N_LEN - 1)]
        pltpu.make_async_copy(whole, whole, len_send.at[step]).wait()
    for kind in range(STEPS + 1):
        for number, sent in enumerate((wide_recv.at[kind], z_recv.at[kind])):
            pltpu.make_async_copy(sent, sent, halo_ssem.at[kind, number]).wait()


def write_out(states, voltage, potential, states_out, voltage_out, potential_out, sem):
    cuts = [STATES * k // WRITES for k in range(WRITES + 1)]
    copies = [
        pltpu.make_async_copy(
            states.at[pl.ds(cuts[k], cuts[k + 1] - cuts[k])],
            states_out.at[pl.ds(cuts[k], cuts[k + 1] - cuts[k])],
            sem.at[k],
        )
        for k in range(WRITES)
    ]
    copies.append(pltpu.make_async_copy(potential, potential_out, sem.at[WRITES]))
    copies.append(pltpu.make_async_copy(voltage, voltage_out, sem.at[WRITES + 1]))
    for copy in copies:
        copy.start()
    for copy in copies:
        copy.wait()


def on_device(
    states, voltage, coupling, decay_rates, volt_gain, current_weights,
    fibre_home, cross_cell, motor_unit, stim_step, tissue,
):
    local, far = cable_tables()
    vmem = pl.BlockSpec(memory_space=pltpu.VMEM)
    hbm = pl.BlockSpec(memory_space=pltpu.HBM)
    outputs = pl.pallas_call(
        kernel,
        out_shape=(
            jax.ShapeDtypeStruct(states.shape, F32),
            jax.ShapeDtypeStruct(voltage.shape, F32),
            jax.ShapeDtypeStruct((STEPS, *tissue.shape), F32),
        ),
        in_specs=[hbm] * 13,
        out_specs=(vmem, vmem, vmem),
        scratch_shapes=[
            pltpu.VMEM(voltage.shape, F32),
            pltpu.VMEM(coupling.shape, F32),
            pltpu.VMEM((1, STATES), F32),
            pltpu.VMEM((1, STATES), F32),
            pltpu.VMEM((1, STATES), F32),
            pltpu.VMEM((1, FIB), jnp.int32),
            pltpu.VMEM((1, FIB), jnp.int32),
            pltpu.VMEM((1, FIB), jnp.int32),
            pltpu.VMEM((1, stim_step.shape[0]), jnp.int32),
            pltpu.VMEM(tissue.shape, F32),
            pltpu.VMEM(local.shape, F32),
            pltpu.VMEM(far.shape, F32),
            pltpu.VMEM((NODES, ROWS, FIB), F32),
            pltpu.VMEM((NODES, ROWS, FIB), F32),
            pltpu.VMEM((NODES, ROWS, FIB), F32),
            pltpu.VMEM((ROWS, 3 * ROWS), BF16),
            pltpu.VMEM((ROWS, FIB), F32),
            pltpu.VMEM((ROWS, FIB), F32),
            pltpu.VMEM((ROWS, FIB), F32),
            pltpu.VMEM((NODES, FIB), F32),
            pltpu.VMEM((NODES, FIB), F32),
            pltpu.VMEM((4 * GROUPS * SLOT_ROWS, BY * BZ), BF16),
            pltpu.VMEM((GROUPS * SLOT_ROWS, 4 * FIB), BF16),
            pltpu.VMEM((GROUPS, SLOT_ROWS, FIB), F32),
            pltpu.VMEM((GROUPS, SLOT_ROWS, FIB), F32),
            pltpu.VMEM((STEPS, GROUPS, SLOT_ROWS, FIB), F32),
            pltpu.VMEM((STEPS, GROUPS, SLOT_ROWS, FIB), F32),
            pltpu.VMEM((STEPS, 8, FIB), F32),
            pltpu.VMEM((STEPS, N_LEN, 8, FIB), F32),
            pltpu.VMEM((STEPS, BINS, BY, BZ), F32),
            pltpu.VMEM((STEPS, BINS, BY, BZ), F32),
            pltpu.VMEM((STEPS, 2, WRAP, BY, BZ), F32),
            pltpu.VMEM((STEPS, 2, WRAP, BY, BZ), F32),
            pltpu.VMEM((2, WRAP, BY, BZ), F32),
            pltpu.VMEM((STEPS, 2, 8, WRAP * BY), F32),
            pltpu.VMEM((STEPS, 2, 8, WRAP * BY), F32),
            pltpu.VMEM((2, 8, WRAP * BY), F32),
            pltpu.VMEM((2, WRAP, BY, BZ), F32),
            pltpu.VMEM((STEPS + 1, 2, 3 * BINS, BZ), F32),
            pltpu.VMEM((STEPS + 1, 2, 2, 4, BZ), F32),
            pltpu.VMEM((STEPS + 1, WIDE_ROWS, BZ), F32),
            pltpu.VMEM((STEPS + 1, Z_TILES, 4, BZ), F32),
            pltpu.SemaphoreType.DMA((4,)),
            pltpu.SemaphoreType.DMA((1,)),
            pltpu.SemaphoreType.DMA((12,)),
            pltpu.SemaphoreType.DMA((3,)),
            pltpu.SemaphoreType.DMA((3,)),
            pltpu.SemaphoreType.DMA((STEPS,)),
            pltpu.SemaphoreType.DMA((STEPS,)),
            pltpu.SemaphoreType.DMA((STEPS + 1, 2)),
            pltpu.SemaphoreType.DMA((STEPS + 1, 2)),
        ],
        compiler_params=pltpu.CompilerParams(collective_id=0, has_side_effects=True, vmem_limit_bytes=VMEM_LIMIT),
    )(*(pltpu.with_memory_space_constraint(array, pltpu.HBM) for array in (
        states, voltage, coupling, decay_rates.reshape(1, -1), volt_gain.reshape(1, -1),
        current_weights.reshape(1, -1), fibre_home.reshape(1, -1), cross_cell.reshape(1, -1),
        motor_unit.reshape(1, -1), stim_step.reshape(1, -1), tissue, local, far,
    )))
    return pl.pallas_call(
        write_out,
        out_shape=tuple(jax.ShapeDtypeStruct(array.shape, F32) for array in outputs),
        in_specs=[vmem] * 3,
        out_specs=(pl.BlockSpec(memory_space=pl.ANY),) * 3,
        scratch_shapes=[pltpu.SemaphoreType.DMA((WRITES + 2,))],
        compiler_params=pltpu.CompilerParams(vmem_limit_bytes=VMEM_LIMIT),
    )(*(pltpu.with_memory_space_constraint(array, pltpu.VMEM) for array in outputs))


def solution(mesh):
    return jax.shard_map(
        on_device,
        mesh=mesh,
        in_specs=(
            P(None, "len", ("fib", "emg")),
            P("len", ("fib", "emg")),
            P(),
            P(),
            P(),
            P(),
            P(("fib", "emg"), None),
            P(("fib", "emg")),
            P(("fib", "emg")),
            P(),
            P("len", "fib", "emg"),
        ),
        out_specs=(
            P(None, "len", ("fib", "emg")),
            P("len", ("fib", "emg")),
            P(None, "len", "fib", "emg"),
        ),
        check_vma=False,
    )
```

```python
import itertools
import math

import jax
import jax.numpy as jnp
import numpy as np
from jax import lax
from jax.experimental import pallas as pl
from jax.experimental.pallas import tpu as pltpu
from jax.sharding import PartitionSpec as P

STEPS = 2
SWEEPS = 4
NPC = 2

time_step = 0.5
conductance = 2000.0
amplitude = 200.0
band_half = 4
low_bound = 0.5
high_bound = 14.0

MESH = pl.DeviceIdType.MESH
HIGH = lax.Precision.HIGHEST
F32 = jnp.float32
BF16 = jnp.bfloat16

N_FIB, N_LEN, N_EMG = 8, 4, 4
GROUPS = N_FIB * N_EMG
STATES = 57
ROWS = 64
NODES = 64
FIB = 128
BINS = NODES // NPC
BY, BZ = 8, 128
SLOT_ROWS = 4
CAPACITY = 12
WIDE_ROWS = 240
TILES = 28
WRAP = 48
VMEM_LIMIT = 24 << 20
WRITES = 4


def hops(df, dl, de):
    rows = df % N_FIB
    return min(rows, N_FIB - rows) / 2 + min(dl % N_LEN, -dl % N_LEN) + min(de % N_EMG, -de % N_EMG)


WAYS = [(df, dl, de) for df in (-1, 0, 1) for dl in (-1, 0, 1) for de in (-1, 0, 1)]
WAYS = sorted((way for way in WAYS if any(way)), key=lambda way: -sum(map(abs, way)))


def way_tiles(df, dl, de):
    if de or (df and dl):
        return 1 if dl else 2
    return 24 if df else 6


PEERS = sorted(
    ((df, de) for df in range(N_FIB) for de in range(N_EMG) if (df, de) != (0, 0)),
    key=lambda peer: -hops(peer[0], 0, peer[1]),
)
AROUND = sorted(
    [(0, 2, 0)] + [(df, dl, de) for df in (-1, 0, 1) for dl in (-1, 1) for de in (-1, 0, 1)],
    key=lambda peer: -hops(*peer),
)


def cable_tables():
    total = NODES * N_LEN
    theta = math.acosh(1.0 + 0.5 / conductance)
    scale = conductance * math.sinh(theta) * math.sinh(total * theta)
    u = np.array([math.cosh((i + 0.5) * theta) for i in range(total)])
    v = np.array([math.cosh((total - 0.5 - i) * theta) / scale for i in range(total)])
    index = np.arange(NODES)
    local = np.zeros((N_LEN, NODES + 8, NODES))
    far = np.zeros((N_LEN, NODES, 8 * N_LEN))
    for shard in range(N_LEN):
        us, vs = u[shard * NODES :][:NODES], v[shard * NODES :][:NODES]
        low = index[:, None] <= index[None, :]
        local[shard, :NODES] = np.where(low, us[:, None] * vs[None, :], vs[:, None] * us[None, :])
        local[shard, NODES] = us
        local[shard, NODES + 1] = vs
        for other in range(N_LEN):
            if other < shard:
                far[shard, :, 8 * other] = vs
            if other > shard:
                far[shard, :, 8 * other + 1] = us
    return jnp.asarray(local, F32), jnp.asarray(far, F32)


def iota(shape, axis):
    return lax.broadcasted_iota(jnp.int32, shape, axis)


def split(values):
    high = values.astype(BF16)
    return high, (values - high.astype(F32)).astype(BF16)


def dot(a, b):
    return jnp.dot(a, b, preferred_element_type=F32)


def dot_high(a, b):
    return jnp.dot(a, b, preferred_element_type=F32, precision=HIGH)


def dot_t(a, b, precision=None):
    return lax.dot_general(
        a, b, (((1,), (1,)), ((), ())), preferred_element_type=F32, precision=precision
    )


def dot_tl(a, b, precision=None):
    return lax.dot_general(
        a, b, (((0,), (0,)), ((), ())), preferred_element_type=F32, precision=precision
    )


def kernel(
    states_hbm, volt_hbm, coup_hbm, decay_hbm, gain_hbm, wts_hbm, home_hbm, cell_hbm, mu_hbm,
    stim_hbm, tissue_hbm, local_hbm, far_hbm,
    states_out, volt_out, pot_out,
    volt_ref, coup_ref, decay_ref, gain_ref, wts_ref, home_ref, cell_ref, mu_ref,
    stim_ref, tissue_ref, local_ref, far_ref,
    s_in, s_work, s_new, lhs_ref, keep_ref, gain_b, wts_b, cur_ref, v1_ref, hot_ref, sel_ref,
    cell_send, cell_recv, row_send, row_recv, end_send, end_recv,
    own_ref, x_ref, r_ref, d_ref, t_ref, zr_ref, zd_ref, zt_ref, hz_ref,
    y_send, z_send, e_send, wide_recv, z_recv, count_ref,
    in_sem, out_sem, small_sem, a2a_send, a2a_recv, len_send, len_recv, halo_ssem, halo_rsem,
):
    fib, shard, emg = lax.axis_index("fib"), lax.axis_index("len"), lax.axis_index("emg")
    me = fib * N_EMG + emg

    smalls = [
        pltpu.make_async_copy(source, target, small_sem.at[number])
        for number, (source, target) in enumerate((
            (coup_hbm, coup_ref), (decay_hbm, decay_ref), (gain_hbm, gain_ref), (wts_hbm, wts_ref),
            (home_hbm, home_ref), (cell_hbm, cell_ref), (mu_hbm, mu_ref), (stim_hbm, stim_ref),
            (volt_hbm, volt_ref), (local_hbm, local_ref), (far_hbm, far_ref),
            (tissue_hbm, tissue_ref),
        ))
    ]
    for copy in smalls[:4] + smalls[8:9]:
        copy.start()
    barrier = pltpu.get_barrier_semaphore()

    def exists(df, dl, de):
        steps = ((fib + df, N_FIB), (shard + dl, N_LEN), (emg + de, N_EMG))
        inside = [(place >= 0) & (place < size) for place, size in steps]
        return inside[0] & inside[1] & inside[2]

    def towards(df, dl, de):
        return {
            "fib": lax.rem(fib + N_FIB + df, N_FIB),
            "len": lax.rem(shard + N_LEN + dl, N_LEN),
            "emg": lax.rem(emg + N_EMG + de, N_EMG),
        }

    for df, de in PEERS:
        pl.semaphore_signal(barrier, inc=1, device_id=towards(df, 0, de), device_id_type=MESH)
    for df, dl, de in AROUND:
        pl.semaphore_signal(barrier, inc=1, device_id=towards(df, dl, de), device_id_type=MESH)

    s_in[:, pl.ds(STATES, ROWS - STATES), :] = jnp.zeros((NODES, ROWS - STATES, FIB), F32)
    quarter = NODES // 4
    for part in range(4):

        def take(node, _, part=part):
            pltpu.make_async_copy(
                states_hbm.at[:, node, :], s_in.at[node, pl.ds(0, STATES), :], in_sem.at[part]
            ).start()
            return 0

        lax.fori_loop(part * quarter, (part + 1) * quarter, take, 0, unroll=16)
    for copy in smalls[4:8] + smalls[9:]:
        copy.start()

    def column(row):
        wide = row.shape[1]
        picked = jnp.where(iota((ROWS, wide), 0) == iota((ROWS, wide), 1), row, 0.0)
        return dot_high(picked, jnp.ones((wide, FIB), F32))

    for copy in smalls[:4]:
        copy.wait()
    keep_ref[...] = 1.0 - time_step * column(decay_ref[...])
    gain_b[...] = column(gain_ref[...])
    wts_b[...] = column(wts_ref[...])
    spread = (iota((STATES, 3 * ROWS), 0) == lax.rem(iota((STATES, 3 * ROWS), 1), ROWS)).astype(F32)
    tiled = dot_high(coup_ref[...], spread)
    tiled = jnp.concatenate([tiled, jnp.zeros((ROWS - STATES, 3 * ROWS), F32)], axis=0)
    high, low = split(tiled)
    lhs_ref[...] = jnp.where(iota((ROWS, 3 * ROWS), 1) < 2 * ROWS, high.astype(F32), low.astype(F32)).astype(BF16)


    def stacked(values):
        high, low = split(values)
        return jnp.concatenate([high, low, high], axis=0)

    def twice(values):
        return jnp.concatenate([values, values], axis=1)

    def first_pair(pair, _):
        node = 2 * pair
        old = jnp.concatenate([s_in[node], s_in[node + 1]], axis=1)
        volts = jnp.concatenate([volt_ref[pl.ds(node + k, 1), :] for k in range(2)], axis=1)
        gain = twice(gain_b[...])
        drive = dot(lhs_ref[...], stacked(old)) + gain * volts
        new = twice(keep_ref[...]) * old + time_step * jnp.tanh(drive)
        for k in range(2):
            part = new[:, k * FIB : (k + 1) * FIB]
            s_work[node + k] = part
            cur_ref[pl.ds(node + k, 1), :] = jnp.sum(wts_b[...] * part, axis=0, keepdims=True)
        return 0

    def next_pair(pair, _):
        node = 2 * pair
        new = jnp.concatenate([s_work[node], s_work[node + 1]], axis=1)
        after = dot(lhs_ref[...], stacked(new))
        for k in range(2):
            s_new[node + k] = after[:, k * FIB : (k + 1) * FIB]
        return 0

    smalls[8].wait()

    for part in range(4):
        block = s_in.at[pl.ds(part * quarter, quarter), pl.ds(0, STATES), :]
        pltpu.make_async_copy(block, block, in_sem.at[part]).wait()
        lax.fori_loop(part * (quarter // 2), (part + 1) * (quarter // 2), first_pair, 0, unroll=8)

    for copy in smalls[4:8] + smalls[9:]:
        copy.wait()
    unit_hot = (iota((FIB, FIB), 0) == mu_ref[...]).astype(F32)
    stim_row = jnp.concatenate(
        [stim_ref[...].astype(F32), jnp.zeros((1, FIB - stim_ref.shape[1]), F32)], axis=1
    )
    fire = dot(stim_row.astype(BF16), unit_hot.astype(BF16))

    pl.semaphore_wait(barrier, len(PEERS) + len(AROUND))
    node_id = shard * NODES + iota((NODES, FIB), 0)
    total_nodes = NODES * N_LEN
    band = (node_id >= total_nodes // 2 - band_half) & (node_id < total_nodes // 2 + band_half)

    def cable_begin(step, volts):
        active = (fire == float(step)).astype(F32)
        pulse = jnp.where(band, amplitude * active, 0.0)
        right = volts + time_step * (pulse - cur_ref[...])
        both = dot_high(local_ref[shard], right)
        end_send[step] = both[NODES:]
        for other_step in range(1, N_LEN):
            other = lax.rem(shard + other_step, N_LEN)
            pltpu.make_async_remote_copy(
                end_send.at[step], end_recv.at[step, shard], len_send.at[step], len_recv.at[step],
                device_id={"fib": fib, "len": other, "emg": emg}, device_id_type=MESH,
            ).start()
        end_recv[step, shard] = jnp.zeros((8, FIB), F32)
        return both[:NODES]

    def cable_end(step, local):
        whole = end_recv.at[step, pl.ds(0, N_LEN - 1)]
        pltpu.make_async_copy(whole, whole, len_recv.at[step]).wait()
        far = end_recv[step].reshape(8 * N_LEN, FIB)
        return local + dot_high(far_ref[shard], far)

    def binned():
        first = cur_ref[pl.ds(0, BINS, stride=2), :]
        second = cur_ref[pl.ds(1, BINS, stride=2), :]
        return first + second

    local = cable_begin(0, volt_ref[...])
    home = home_ref[...]
    member = (iota((GROUPS, FIB), 0) == home).astype(F32)
    before = (iota((FIB, FIB), 0) < iota((FIB, FIB), 1)).astype(BF16)
    earlier = dot(member.astype(BF16), before)
    rank = jnp.sum(earlier * member, axis=0, keepdims=True).astype(jnp.int32)
    slot = home * CAPACITY + rank
    packed = GROUPS * SLOT_ROWS
    row_id = iota((packed, FIB), 0)
    in_brick = lax.rem(row_id, SLOT_ROWS)
    first_slot = (row_id // SLOT_ROWS) * CAPACITY + 4 * in_brick
    for q in range(4):
        chosen = (slot == first_slot + q) & (in_brick < CAPACITY // 4)
        sel_ref[:, q * FIB : (q + 1) * FIB] = chosen.astype(F32).astype(BF16)

    def pack(values):
        blank = jnp.zeros((BINS, FIB), BF16)
        total = None
        for part in split(values):
            block = jnp.concatenate(
                [
                    jnp.concatenate([part if q == row else blank for q in range(4)], axis=1)
                    for row in range(4)
                ],
                axis=0,
            )
            term = dot_t(sel_ref[...], block)
            total = term if total is None else total + term
        return total.reshape(GROUPS, SLOT_ROWS, FIB)

    def exchange(source, target, slot_index):
        for df, de in PEERS:
            device = towards(df, 0, de)
            other = device["fib"] * N_EMG + device["emg"]
            pltpu.make_async_remote_copy(
                source.at[other], target.at[me], a2a_send.at[slot_index], a2a_recv.at[slot_index],
                device_id=device, device_id_type=MESH,
            ).start()
        target[me] = source[me]

    def exchange_wait(target, slot_index):
        whole = target.at[pl.ds(0, GROUPS - 1)]
        pltpu.make_async_copy(whole, whole, a2a_recv.at[slot_index]).wait()

    def exchange_sent(source, slot_index):
        whole = source.at[pl.ds(0, GROUPS - 1)]
        pltpu.make_async_copy(whole, whole, a2a_send.at[slot_index]).wait()

    cell_row = jnp.broadcast_to(cell_ref[...].astype(F32), (BINS, FIB))
    cell_send[...] = pack(cell_row)

    exchange(cell_send, cell_recv, 0)
    row_send[0] = pack(binned())
    exchange(row_send.at[0], row_recv.at[0], 1)

    middle = 0.5 * (high_bound + low_bound)
    spread_width = 0.5 * (high_bound - low_bound)
    ratio = middle / spread_width
    lane = iota((BY, BZ), 1)
    sub = iota((BY, BZ), 0)
    zlane = iota((8, WRAP * BY), 1)
    zsub = iota((8, WRAP * BY), 0)
    zrow = lax.rem(zlane, BY)

    def inside(condition):
        return jnp.where(condition, 1.0, 0.0).astype(F32)

    has_fib_up, has_fib_down = fib < N_FIB - 1, fib > 0
    has_len_up, has_len_down = shard < N_LEN - 1, shard > 0
    has_emg_up, has_emg_down = emg < N_EMG - 1, emg > 0
    fib_up, fib_down = inside(has_fib_up), inside(has_fib_down)
    len_up, len_down = inside(has_len_up), inside(has_len_down)
    emg_up, emg_down = inside(has_emg_up), inside(has_emg_down)
    margin = jnp.where(sub < 4, fib_up, fib_down)
    zmask = jnp.where(zsub < 4, emg_up, emg_down)
    zmask = zmask * jnp.where(zlane < 256, 1.0, jnp.where(zlane < 320, len_up, len_down))
    zmasks = (zmask, zmask * jnp.where(zrow < 4, fib_up, fib_down))

    def spread_out(kind, own):
        flat = own.reshape(BINS * BY, BZ)
        for tile in range(2):
            turned = flat[tile * BZ : (tile + 1) * BZ, :].T
            z_send[kind, 0, tile] = turned[:4]
            z_send[kind, 1, tile] = turned[BZ - 4 :]
        for f in range(2):
            for x in range(2):
                for k in range(2):
                    rows = own[x * (BINS - 2) + k, f * (BY - 2) : f * (BY - 2) + 2, :]
                    e_send[kind, f, x, 2 * k : 2 * k + 2, :] = rows
        for y in range(3):
            y_send[kind, 0, y * BINS : (y + 1) * BINS, :] = flat[pl.ds(y, BINS, stride=BY), :]
            y_send[kind, 1, y * BINS : (y + 1) * BINS, :] = flat[pl.ds(BY - 3 + y, BINS, stride=BY), :]

        for way in WAYS:
            source = margin_source(kind, flat, way)
            target = margin_target(kind, tuple(-step for step in way))
            copy = pltpu.make_async_remote_copy(
                source, target, halo_ssem.at[kind], halo_rsem.at[kind],
                device_id=towards(*way), device_id_type=MESH,
            )
            pl.when(exists(*way))(copy.start)

    def margin_source(kind, flat, way):
        df, dl, de = way
        if de:
            half = z_send.at[kind, max(de, 0)]
            return half.at[pl.ds(max(dl, 0), 1)] if dl else half
        if df and dl:
            return e_send.at[kind, max(df, 0), pl.ds(max(dl, 0), 1)]
        if df:
            return y_send.at[kind, max(df, 0)]
        return flat.at[pl.ds(0 if dl < 0 else (BINS - 3) * BY, 24)]

    def margin_target(kind, way):
        df, dl, de = way
        f, x = int(df < 0), int(dl < 0)
        if de:
            base = 12 * int(de < 0)
            if df and dl:
                return z_recv.at[kind, pl.ds(base + 8 + 2 * f + x, 1)]
            if dl:
                return z_recv.at[kind, pl.ds(base + 2 + x, 1)]
            return z_recv.at[kind, pl.ds(base + (4 + 2 * f if df else 0), 2)]
        if df and dl:
            return z_recv.at[kind, pl.ds(24 + 2 * f + x, 1)]
        if df:
            return wide_recv.at[kind, pl.ds(0 if df < 0 else 96, 96)]
        return wide_recv.at[kind, pl.ds(192 if dl < 0 else 216, 24)]

    at_edge = [
        (place == 0) | (place == size - 1)
        for place, size in ((fib, N_FIB), (shard, N_LEN), (emg, N_EMG))
    ]

    def margins_wait(kind, sem):
        for edges in itertools.product((False, True), repeat=3):
            ways = [
                way for way in WAYS
                if not any(edge and step < 0 for edge, step in zip(edges, way))
            ]
            tiles = sum(way_tiles(*way) for way in ways)
            here = [at == edge for at, edge in zip(at_edge, edges)]
            whole = count_ref.at[pl.ds(0, tiles)]
            copy = pltpu.make_async_copy(whole, whole, sem.at[kind])
            pl.when(here[0] & here[1] & here[2])(copy.wait)

    def assemble(kind, own, field, zfield, add):
        def only(condition, values):
            return jnp.where(condition, values, 0.0)

        def plus(values):
            return values + add if add else values

        wide, tiles = wide_recv.at[kind], z_recv.at[kind]
        margins_wait(kind, halo_rsem)
        field[0, pl.ds(0, BINS)] = plus(own[...])
        for k in range(3):
            field[0, BINS + k] = plus(only(has_len_up, wide[216 + 8 * k : 224 + 8 * k, :]))
            field[0, WRAP - 3 + k] = plus(only(has_len_down, wide[192 + 8 * k : 200 + 8 * k, :]))
        beside = field.at[1].reshape(WRAP * BY, BZ)
        for y in range(3):
            beside[pl.ds(y, BINS, stride=BY), :] = plus(only(has_fib_up, wide[96 + 32 * y : 128 + 32 * y, :]))
            beside[pl.ds(BY - 3 + y, BINS, stride=BY), :] = plus(only(has_fib_down, wide[32 * y : 32 * y + 32, :]))
        for f, along in enumerate((has_fib_up, has_fib_down)):
            for x, (place, weight) in enumerate(((BINS, has_len_up), (WRAP - 2, has_len_down))):
                for k in range(2):
                    rows = tiles[24 + 2 * f + x, 2 * k : 2 * k + 2, :]
                    field[1, place + k, f * (BY - 2) : f * (BY - 2) + 2, :] = plus(
                        only(along & weight, rows)
                    )
        low = iota((4, BZ), 1) < BZ // 2
        near = lax.rem(iota((4, BZ), 1), BY) < 4
        for half, weight in ((0, has_emg_up), (1, has_emg_down)):
            base = 12 * half
            rows = slice(4 * half, 4 * half + 4)
            for tile in range(2):
                lanes = slice(tile * BZ, (tile + 1) * BZ)
                zfield[0, rows, lanes] = plus(only(weight, tiles[base + tile]))
                up = only(has_fib_up, tiles[base + 4 + tile])
                down = only(has_fib_down, tiles[base + 6 + tile])
                zfield[1, rows, lanes] = plus(only(weight, jnp.where(near, up, down)))
            lanes = slice(2 * BZ, 3 * BZ)
            both = jnp.where(low, only(has_len_up, tiles[base + 2]), only(has_len_down, tiles[base + 3]))
            zfield[0, rows, lanes] = plus(only(weight, both))
            up = jnp.where(low, only(has_len_up, tiles[base + 8]), only(has_len_down, tiles[base + 9]))
            down = jnp.where(low, only(has_len_up, tiles[base + 10]), only(has_len_down, tiles[base + 11]))
            both = jnp.where(near, only(has_fib_up, up), only(has_fib_down, down))
            zfield[1, rows, lanes] = plus(only(weight, both))

    def scatter(step):
        exchange_wait(row_recv.at[step], 1 + step)
        rows = row_recv[step].reshape(packed, FIB)
        turned = rows.T
        wide = jnp.concatenate([turned[q * BINS : (q + 1) * BINS] for q in range(4)], axis=1)
        both = dot(jnp.concatenate(split(wide), axis=0), hot_ref[...])
        source = both[:BINS] + both[BINS:]
        flat = own_ref.at[step].reshape(BINS * BY, BZ)
        for y in range(BY):
            flat[pl.ds(y, BINS, stride=BY), :] = source[:, y * BZ : (y + 1) * BZ]

    weight = [1.0 / ratio]
    for _ in range(SWEEPS - 1):
        weight.append(1.0 / (2.0 * ratio - weight[-1]))

    def sweep(step, turn):
        first, last = turn == 0, turn == SWEEPS - 2
        keep = weight[turn + 1] * weight[turn]
        gain = 2.0 * weight[turn + 1] / spread_width
        scale = 1.0 / middle if first else 1.0
        field = r_ref.at[step] if first else d_ref.at[step]
        zfield = zr_ref.at[step] if first else zd_ref.at[step]
        blank = jnp.zeros((BZ - 16, BZ), F32)
        for tile in range(1 if last else 2):
            for block in range(2 if last or (turn and tile) else 3):
                z = zfield[tile, :, block * BZ : (block + 1) * BZ]
                first_lane = jnp.where(sub == 0, pltpu.roll(z, 1, 0), 0.0)
                last_lane = jnp.where(sub == 7, pltpu.roll(z, 7, 0), 0.0)
                turned = jnp.concatenate([first_lane, blank, last_lane], axis=0).T
                hz_ref[tile, pl.ds(16 * block, 16)] = turned.reshape(16, BY, BZ)

        def advance(here, beside, diagonal, rest, push):
            if first:
                rest = here - scale * (diagonal * here - beside)
            else:
                rest = rest - (diagonal * here - beside)
            return rest, (keep * scale) * here + push * rest

        if not last:
            zs = [zfield[0], zfield[1]]
            up = [pltpu.roll(z, 1, 1) for z in zs]
            down = [pltpu.roll(z, WRAP * BY - 1, 1) for z in zs]
            up_far = [pltpu.roll(z, WRAP * BY - BY + 1, 1) for z in zs]
            down_far = [pltpu.roll(z, BY - 1, 1) for z in zs]
            for t in range(1 if turn else 2):
                blocks = 2 if turn or t else 3
                width = blocks * BZ
                ends = []
                for block in range(blocks):
                    turned = field[t, pl.ds(16 * block, 16)].reshape(BZ, BZ).T
                    ends.append(
                        jnp.where(
                            sub == 0, pltpu.roll(turned[BZ - 8 :], 1, 0), pltpu.roll(turned[:8], 7, 0)
                        )
                    )
                edges = jnp.concatenate(ends, axis=1)
                beside = pltpu.roll(zs[t], BY, 1) + pltpu.roll(zs[t], WRAP * BY - BY, 1)
                beside = beside + jnp.where(zrow == 0, up_far[1 - t], up[t])
                beside = beside + jnp.where(zrow == BY - 1, down_far[1 - t], down[t])
                row, beside = zsub[:, :width], beside[:, :width]
                z = zs[t][:, :width]
                beside = beside + jnp.where(row == 0, edges, pltpu.roll(z, 1, 0))
                beside = beside + jnp.where(row == 7, edges, pltpu.roll(z, 7, 0))
                rest, after = advance(
                    z, beside, zt_ref[t, :, :width], None if first else zr_ref[step, t, :, :width],
                    gain * zmasks[t][:, :width],
                )
                zr_ref[step, t, :, :width] = rest
                zd_ref[step, t, :, :width] = after

        def slab(place, following, previous, push, own, tiles=2):
            here = (field[0, place], field[1, place])
            up = [pltpu.roll(h, 1, 0) for h in here]
            down = [pltpu.roll(h, BY - 1, 0) for h in here]
            for t in range(1 if last else tiles):
                beside = previous[t] + field[t, following] + hz_ref[t, place]
                beside = beside + jnp.where(sub == 0, up[1 - t], up[t])
                beside = beside + jnp.where(sub == BY - 1, down[1 - t], down[t])
                beside = beside + jnp.where(lane == 0, 0.0, pltpu.roll(here[t], 1, 1))
                beside = beside + jnp.where(lane == BZ - 1, 0.0, pltpu.roll(here[t], BZ - 1, 1))
                rest, after = advance(
                    here[t], beside, t_ref[t, place], None if first else r_ref[step, t, place],
                    push if t == 0 else push * margin,
                )
                if not last:
                    r_ref[step, t, place] = rest
                    d_ref[step, t, place] = after
                if own and t == 0:
                    if last:
                        pot_out[step, place] = x_ref[step, place] + after
                    elif first:
                        x_ref[step, place] = scale * here[0] + after
                    else:
                        x_ref[step, place] = x_ref[step, place] + after
            return here

        reach = SWEEPS - 2 - turn
        start = (WRAP - 1 - reach) % WRAP
        previous = (field[0, start], field[1, start])
        for k in range(reach):
            place = start + 1 + k
            tiles = 2 if k else 1
            previous = slab(place, (place + 1) % WRAP, previous, gain * len_down, False, tiles)
        previous = lax.fori_loop(
            0, BINS, lambda x, before: slab(x, x + 1, before, gain, True), previous, unroll=32
        )
        for k in range(reach):
            tiles = 2 if k + 1 < reach else 1
            previous = slab(BINS + k, BINS + k + 1, previous, gain * len_up, False, tiles)

    spread_out(STEPS, tissue_ref)
    r_ref[...] = jnp.zeros_like(r_ref)
    d_ref[...] = jnp.zeros_like(d_ref)
    t_ref[...] = jnp.zeros_like(t_ref)
    lax.fori_loop(0, NODES // 2, next_pair, 0, unroll=8)
    v1_ref[...] = cable_end(0, local)

    def second(node, _):
        drive = s_new[node] + gain_b[...] * v1_ref[pl.ds(node, 1), :]
        new = keep_ref[...] * s_work[node] + time_step * jnp.tanh(drive)
        s_in[node] = new
        cur_ref[pl.ds(node, 1), :] = jnp.sum(wts_b[...] * new, axis=0, keepdims=True)
        return 0

    lax.fori_loop(0, NODES, second, 0, unroll=8)
    row_send[1] = pack(binned())
    exchange(row_send.at[1], row_recv.at[1], 2)
    local = cable_begin(1, v1_ref[...])

    exchange_wait(cell_recv, 0)
    cells = cell_recv[...].reshape(packed, FIB)
    for q in range(4):
        column_q = cells[:, q * BINS : q * BINS + 1].astype(jnp.int32)
        for y in range(BY):
            hot = (column_q == iota((packed, BZ), 1) + y * BZ).astype(F32).astype(BF16)
            hot_ref[q * packed : (q + 1) * packed, y * BZ : (y + 1) * BZ] = hot

    scatter(0)
    spread_out(0, own_ref.at[0])
    def put(node, _):
        pltpu.make_async_copy(
            s_in.at[node, pl.ds(0, STATES), :], states_out.at[:, node, :], out_sem.at[0]
        ).start()
        return 0

    lax.fori_loop(0, NODES, put, 0, unroll=16)
    assemble(STEPS, tissue_ref, t_ref, zt_ref, 6.0)
    exchange_sent(cell_send, 0)
    margins_wait(STEPS, halo_ssem)
    volt_out[...] = cable_end(1, local)
    scatter(1)
    spread_out(1, own_ref.at[1])
    def sent(step):
        exchange_sent(row_send.at[step], 1 + step)
        whole = end_recv.at[step, pl.ds(0, N_LEN - 1)]
        pltpu.make_async_copy(whole, whole, len_send.at[step]).wait()
        margins_wait(step, halo_ssem)

    for step in range(STEPS):
        if step:
            pltpu.make_async_copy(states_out, states_out, out_sem.at[0]).wait()
            sent(0)
            sent(1)
        assemble(step, own_ref.at[step], r_ref.at[step], zr_ref.at[step], 0.0)
        for turn in range(SWEEPS - 1):
            sweep(step, turn)


def write_out(states, voltage, potential, states_out, voltage_out, potential_out, sem):
    cuts = [STATES * k // WRITES for k in range(WRITES + 1)]
    copies = [
        pltpu.make_async_copy(
            states.at[pl.ds(cuts[k], cuts[k + 1] - cuts[k])],
            states_out.at[pl.ds(cuts[k], cuts[k + 1] - cuts[k])],
            sem.at[k],
        )
        for k in range(WRITES)
    ]
    copies.append(pltpu.make_async_copy(potential, potential_out, sem.at[WRITES]))
    copies.append(pltpu.make_async_copy(voltage, voltage_out, sem.at[WRITES + 1]))
    for copy in copies:
        copy.start()
    for copy in copies:
        copy.wait()


def on_device(
    states, voltage, coupling, decay_rates, volt_gain, current_weights,
    fibre_home, cross_cell, motor_unit, stim_step, tissue,
):
    local, far = cable_tables()
    vmem = pl.BlockSpec(memory_space=pltpu.VMEM)
    hbm = pl.BlockSpec(memory_space=pltpu.HBM)
    outputs = pl.pallas_call(
        kernel,
        out_shape=(
            jax.ShapeDtypeStruct(states.shape, F32),
            jax.ShapeDtypeStruct(voltage.shape, F32),
            jax.ShapeDtypeStruct((STEPS, *tissue.shape), F32),
        ),
        in_specs=[hbm] * 13,
        out_specs=(vmem, vmem, vmem),
        scratch_shapes=[
            pltpu.VMEM(voltage.shape, F32),
            pltpu.VMEM(coupling.shape, F32),
            pltpu.VMEM((1, STATES), F32),
            pltpu.VMEM((1, STATES), F32),
            pltpu.VMEM((1, STATES), F32),
            pltpu.VMEM((1, FIB), jnp.int32),
            pltpu.VMEM((1, FIB), jnp.int32),
            pltpu.VMEM((1, FIB), jnp.int32),
            pltpu.VMEM((1, stim_step.shape[0]), jnp.int32),
            pltpu.VMEM(tissue.shape, F32),
            pltpu.VMEM(local.shape, F32),
            pltpu.VMEM(far.shape, F32),
            pltpu.VMEM((NODES, ROWS, FIB), F32),
            pltpu.VMEM((NODES, ROWS, FIB), F32),
            pltpu.VMEM((NODES, ROWS, FIB), F32),
            pltpu.VMEM((ROWS, 3 * ROWS), BF16),
            pltpu.VMEM((ROWS, FIB), F32),
            pltpu.VMEM((ROWS, FIB), F32),
            pltpu.VMEM((ROWS, FIB), F32),
            pltpu.VMEM((NODES, FIB), F32),
            pltpu.VMEM((NODES, FIB), F32),
            pltpu.VMEM((4 * GROUPS * SLOT_ROWS, BY * BZ), BF16),
            pltpu.VMEM((GROUPS * SLOT_ROWS, 4 * FIB), BF16),
            pltpu.VMEM((GROUPS, SLOT_ROWS, FIB), F32),
            pltpu.VMEM((GROUPS, SLOT_ROWS, FIB), F32),
            pltpu.VMEM((STEPS, GROUPS, SLOT_ROWS, FIB), F32),
            pltpu.VMEM((STEPS, GROUPS, SLOT_ROWS, FIB), F32),
            pltpu.VMEM((STEPS, 8, FIB), F32),
            pltpu.VMEM((STEPS, N_LEN, 8, FIB), F32),
            pltpu.VMEM((STEPS, BINS, BY, BZ), F32),
            pltpu.VMEM((STEPS, BINS, BY, BZ), F32),
            pltpu.VMEM((STEPS, 2, WRAP, BY, BZ), F32),
            pltpu.VMEM((STEPS, 2, WRAP, BY, BZ), F32),
            pltpu.VMEM((2, WRAP, BY, BZ), F32),
            pltpu.VMEM((STEPS, 2, 8, WRAP * BY), F32),
            pltpu.VMEM((STEPS, 2, 8, WRAP * BY), F32),
            pltpu.VMEM((2, 8, WRAP * BY), F32),
            pltpu.VMEM((2, WRAP, BY, BZ), F32),
            pltpu.VMEM((STEPS + 1, 2, 3 * BINS, BZ), F32),
            pltpu.VMEM((STEPS + 1, 2, 2, 4, BZ), F32),
            pltpu.VMEM((STEPS + 1, 2, 2, 4, BZ), F32),
            pltpu.VMEM((STEPS + 1, WIDE_ROWS, BZ), F32),
            pltpu.VMEM((STEPS + 1, TILES, 4, BZ), F32),
            pltpu.VMEM((WIDE_ROWS // 4 + TILES, 4, BZ), F32),
            pltpu.SemaphoreType.DMA((4,)),
            pltpu.SemaphoreType.DMA((1,)),
            pltpu.SemaphoreType.DMA((12,)),
            pltpu.SemaphoreType.DMA((3,)),
            pltpu.SemaphoreType.DMA((3,)),
            pltpu.SemaphoreType.DMA((STEPS,)),
            pltpu.SemaphoreType.DMA((STEPS,)),
            pltpu.SemaphoreType.DMA((STEPS + 1,)),
            pltpu.SemaphoreType.DMA((STEPS + 1,)),
        ],
        compiler_params=pltpu.CompilerParams(collective_id=0, has_side_effects=True, vmem_limit_bytes=VMEM_LIMIT),
    )(*(pltpu.with_memory_space_constraint(array, pltpu.HBM) for array in (
        states, voltage, coupling, decay_rates.reshape(1, -1), volt_gain.reshape(1, -1),
        current_weights.reshape(1, -1), fibre_home.reshape(1, -1), cross_cell.reshape(1, -1),
        motor_unit.reshape(1, -1), stim_step.reshape(1, -1), tissue, local, far,
    )))
    return pl.pallas_call(
        write_out,
        out_shape=tuple(jax.ShapeDtypeStruct(array.shape, F32) for array in outputs),
        in_specs=[vmem] * 3,
        out_specs=(pl.BlockSpec(memory_space=pl.ANY),) * 3,
        scratch_shapes=[pltpu.SemaphoreType.DMA((WRITES + 2,))],
        compiler_params=pltpu.CompilerParams(vmem_limit_bytes=VMEM_LIMIT),
    )(*(pltpu.with_memory_space_constraint(array, pltpu.VMEM) for array in outputs))


def solution(mesh):
    return jax.shard_map(
        on_device,
        mesh=mesh,
        in_specs=(
            P(None, "len", ("fib", "emg")),
            P("len", ("fib", "emg")),
            P(),
            P(),
            P(),
            P(),
            P(("fib", "emg"), None),
            P(("fib", "emg")),
            P(("fib", "emg")),
            P(),
            P("len", "fib", "emg"),
        ),
        out_specs=(
            P(None, "len", ("fib", "emg")),
            P("len", ("fib", "emg")),
            P(None, "len", "fib", "emg"),
        ),
        check_vma=False,
    )
```

```python
import itertools
import math

import jax
import jax.numpy as jnp
import numpy as np
from jax import lax
from jax.experimental import pallas as pl
from jax.experimental.pallas import tpu as pltpu
from jax.sharding import PartitionSpec as P

STEPS = 2
SWEEPS = 4
NPC = 2

time_step = 0.5
conductance = 2000.0
amplitude = 200.0
band_half = 4
low_bound = 0.5
high_bound = 14.0

MESH = pl.DeviceIdType.MESH
HIGH = lax.Precision.HIGHEST
F32 = jnp.float32
BF16 = jnp.bfloat16

N_FIB, N_LEN, N_EMG = 8, 4, 4
GROUPS = N_FIB * N_EMG
STATES = 57
ROWS = 64
NODES = 64
FIB = 128
BINS = NODES // NPC
BY, BZ = 8, 128
SLOT_ROWS = 4
CAPACITY = 12
WIDE_ROWS = 240
TILES = 28
WRAP = 48
VMEM_LIMIT = 24 << 20
WRITES = 4


def hops(df, dl, de):
    rows = df % N_FIB
    return min(rows, N_FIB - rows) / 2 + min(dl % N_LEN, -dl % N_LEN) + min(de % N_EMG, -de % N_EMG)


WAYS = [(df, dl, de) for df in (-1, 0, 1) for dl in (-1, 0, 1) for de in (-1, 0, 1)]
WAYS = sorted((way for way in WAYS if any(way)), key=lambda way: -sum(map(abs, way)))


def way_tiles(df, dl, de):
    if de or (df and dl):
        return 1 if dl else 2
    return 24 if df else 6


PEERS = sorted(
    ((df, de) for df in range(N_FIB) for de in range(N_EMG) if (df, de) != (0, 0)),
    key=lambda peer: -hops(peer[0], 0, peer[1]),
)
AXIS_PEERS = sorted(
    [(step, 0, 0) for step in range(1, N_FIB)]
    + [(0, step, 0) for step in range(1, N_LEN)]
    + [(0, 0, step) for step in range(1, N_EMG)],
    key=lambda peer: -hops(*peer),
)


def cable_tables():
    total = NODES * N_LEN
    theta = math.acosh(1.0 + 0.5 / conductance)
    scale = conductance * math.sinh(theta) * math.sinh(total * theta)
    u = np.array([math.cosh((i + 0.5) * theta) for i in range(total)])
    v = np.array([math.cosh((total - 0.5 - i) * theta) / scale for i in range(total)])
    index = np.arange(NODES)
    local = np.zeros((N_LEN, NODES, NODES))
    ends = np.zeros((N_LEN, 2, NODES, FIB))
    for shard in range(N_LEN):
        us, vs = u[shard * NODES :][:NODES], v[shard * NODES :][:NODES]
        low = index[:, None] <= index[None, :]
        local[shard] = np.where(low, us[:, None] * vs[None, :], vs[:, None] * us[None, :])
        ends[shard] = np.stack([us, vs])[:, :, None]
    return jnp.asarray(local, F32), jnp.asarray(ends, F32)


def iota(shape, axis):
    return lax.broadcasted_iota(jnp.int32, shape, axis)


def split(values):
    high = values.astype(BF16)
    return high, (values - high.astype(F32)).astype(BF16)


def dot(a, b):
    return jnp.dot(a, b, preferred_element_type=F32)


def dot_high(a, b):
    return jnp.dot(a, b, preferred_element_type=F32, precision=HIGH)


def dot_t(a, b, precision=None):
    return lax.dot_general(
        a, b, (((1,), (1,)), ((), ())), preferred_element_type=F32, precision=precision
    )


def dot_tl(a, b, precision=None):
    return lax.dot_general(
        a, b, (((0,), (0,)), ((), ())), preferred_element_type=F32, precision=precision
    )


def kernel(
    states_hbm, volt_hbm, coup_hbm, decay_hbm, gain_hbm, wts_hbm, home_hbm, cell_hbm, mu_hbm,
    stim_hbm, tissue_hbm, local_hbm, far_hbm,
    states_out, volt_out, pot_out,
    volt_ref, coup_ref, decay_ref, gain_ref, wts_ref, home_ref, cell_ref, mu_ref,
    stim_ref, tissue_ref, local_ref, far_ref,
    s_in, s_work, s_new, lhs_ref, keep_ref, gain_b, wts_b, cur_ref, v1_ref, hot_ref, sel_ref,
    cell_send, cell_recv, row_send, row_recv, ends_out, ends_in,
    own_ref, x_ref, r_ref, d_ref, t_ref, zr_ref, zd_ref, zt_ref, hz_ref,
    y_send, z_send, e_send, wide_recv, z_recv, count_ref,
    in_sem, out_sem, small_sem, a2a_send, a2a_recv, len_send, len_recv, halo_ssem, halo_rsem, entered,
):
    fib, shard, emg = lax.axis_index("fib"), lax.axis_index("len"), lax.axis_index("emg")
    me = fib * N_EMG + emg

    smalls = [
        pltpu.make_async_copy(source, target, small_sem.at[number])
        for number, (source, target) in enumerate((
            (coup_hbm, coup_ref), (decay_hbm, decay_ref), (gain_hbm, gain_ref), (wts_hbm, wts_ref),
            (home_hbm, home_ref), (cell_hbm, cell_ref), (mu_hbm, mu_ref), (stim_hbm, stim_ref),
            (volt_hbm, volt_ref), (local_hbm.at[shard], local_ref), (far_hbm.at[shard], far_ref),
            (tissue_hbm, tissue_ref),
        ))
    ]
    for copy in smalls[:4] + smalls[8:9]:
        copy.start()
    barrier = pltpu.get_barrier_semaphore()

    def exists(df, dl, de):
        steps = ((fib + df, N_FIB), (shard + dl, N_LEN), (emg + de, N_EMG))
        inside = [(place >= 0) & (place < size) for place, size in steps]
        return inside[0] & inside[1] & inside[2]

    def towards(df, dl, de):
        return {
            "fib": lax.rem(fib + N_FIB + df, N_FIB),
            "len": lax.rem(shard + N_LEN + dl, N_LEN),
            "emg": lax.rem(emg + N_EMG + de, N_EMG),
        }

    for way in AXIS_PEERS:
        pl.semaphore_signal(barrier, inc=1, device_id=towards(*way), device_id_type=MESH)

    s_in[:, pl.ds(STATES, ROWS - STATES), :] = jnp.zeros((NODES, ROWS - STATES, FIB), F32)
    quarter = NODES // 4
    for part in range(4):

        def take(node, _, part=part):
            pltpu.make_async_copy(
                states_hbm.at[:, node, :], s_in.at[node, pl.ds(0, STATES), :], in_sem.at[part]
            ).start()
            return 0

        lax.fori_loop(part * quarter, (part + 1) * quarter, take, 0, unroll=16)
    for copy in smalls[4:8] + smalls[9:]:
        copy.start()

    def column(row):
        wide = row.shape[1]
        picked = jnp.where(iota((ROWS, wide), 0) == iota((ROWS, wide), 1), row, 0.0)
        return dot_high(picked, jnp.ones((wide, FIB), F32))

    for copy in smalls[:4]:
        copy.wait()
    keep_ref[...] = 1.0 - time_step * column(decay_ref[...])
    gain_b[...] = column(gain_ref[...])
    wts_b[...] = column(wts_ref[...])
    spread = (iota((STATES, 3 * ROWS), 0) == lax.rem(iota((STATES, 3 * ROWS), 1), ROWS)).astype(F32)
    tiled = dot_high(coup_ref[...], spread)
    tiled = jnp.concatenate([tiled, jnp.zeros((ROWS - STATES, 3 * ROWS), F32)], axis=0)
    high, low = split(tiled)
    lhs_ref[...] = jnp.where(iota((ROWS, 3 * ROWS), 1) < 2 * ROWS, high.astype(F32), low.astype(F32)).astype(BF16)


    def stacked(values):
        high, low = split(values)
        return jnp.concatenate([high, low, high], axis=0)

    def twice(values):
        return jnp.concatenate([values, values], axis=1)

    def first_pair(pair, _):
        node = 2 * pair
        old = jnp.concatenate([s_in[node], s_in[node + 1]], axis=1)
        volts = jnp.concatenate([volt_ref[pl.ds(node + k, 1), :] for k in range(2)], axis=1)
        gain = twice(gain_b[...])
        drive = dot(lhs_ref[...], stacked(old)) + gain * volts
        new = twice(keep_ref[...]) * old + time_step * jnp.tanh(drive)
        for k in range(2):
            part = new[:, k * FIB : (k + 1) * FIB]
            s_work[node + k] = part
            cur_ref[pl.ds(node + k, 1), :] = jnp.sum(wts_b[...] * part, axis=0, keepdims=True)
        return 0

    def next_pair(pair, _):
        node = 2 * pair
        new = jnp.concatenate([s_work[node], s_work[node + 1]], axis=1)
        after = dot(lhs_ref[...], stacked(new))
        for k in range(2):
            s_new[node + k] = after[:, k * FIB : (k + 1) * FIB]
        return 0

    smalls[8].wait()

    for part in range(4):
        block = s_in.at[pl.ds(part * quarter, quarter), pl.ds(0, STATES), :]
        pltpu.make_async_copy(block, block, in_sem.at[part]).wait()
        lax.fori_loop(part * (quarter // 2), (part + 1) * (quarter // 2), first_pair, 0, unroll=8)

    for copy in smalls[4:8] + smalls[9:]:
        copy.wait()
    unit_hot = (iota((FIB, FIB), 0) == mu_ref[...]).astype(F32)
    stim_row = jnp.concatenate(
        [stim_ref[...].astype(F32), jnp.zeros((1, FIB - stim_ref.shape[1]), F32)], axis=1
    )
    fire = dot(stim_row.astype(BF16), unit_hot.astype(BF16))

    pl.semaphore_wait(barrier, len(AXIS_PEERS))
    node_id = shard * NODES + iota((NODES, FIB), 0)
    total_nodes = NODES * N_LEN
    band = (node_id >= total_nodes // 2 - band_half) & (node_id < total_nodes // 2 + band_half)

    def cable_begin(step, volts):
        active = (fire == float(step)).astype(F32)
        pulse = jnp.where(band, amplitude * active, 0.0)
        right = volts + time_step * (pulse - cur_ref[...])
        ends_out[step, 0:1, :] = jnp.sum(far_ref[0] * right, axis=0, keepdims=True)
        ends_out[step, 1:2, :] = jnp.sum(far_ref[1] * right, axis=0, keepdims=True)
        for other_step in range(1, N_LEN):
            other = lax.rem(shard + other_step, N_LEN)
            pltpu.make_async_remote_copy(
                ends_out.at[step], ends_in.at[step, shard], len_send.at[step], len_recv.at[step],
                device_id={"fib": fib, "len": other, "emg": emg}, device_id_type=MESH,
            ).start()
        return dot_high(local_ref[...], right)

    def cable_end(step, local):
        whole = ends_in.at[step, pl.ds(0, N_LEN - 1)]
        pltpu.make_async_copy(whole, whole, len_recv.at[step]).wait()
        below = above = jnp.zeros((1, FIB), F32)
        for other in range(N_LEN):
            below = below + jnp.where(other < shard, ends_in[step, other, 0:1, :], 0.0)
            above = above + jnp.where(other > shard, ends_in[step, other, 1:2, :], 0.0)
        return local + far_ref[1] * below + far_ref[0] * above

    def binned():
        first = cur_ref[pl.ds(0, BINS, stride=2), :]
        second = cur_ref[pl.ds(1, BINS, stride=2), :]
        return first + second

    local = cable_begin(0, volt_ref[...])
    for df in range(1, N_FIB):
        pl.semaphore_signal(entered, inc=1, device_id=towards(df, 0, 0), device_id_type=MESH)
    home = home_ref[...]
    member = (iota((GROUPS, FIB), 0) == home).astype(F32)
    before = (iota((FIB, FIB), 0) < iota((FIB, FIB), 1)).astype(BF16)
    earlier = dot(member.astype(BF16), before)
    rank = jnp.sum(earlier * member, axis=0, keepdims=True).astype(jnp.int32)
    slot = home * CAPACITY + rank
    packed = GROUPS * SLOT_ROWS
    row_id = iota((packed, FIB), 0)
    in_brick = lax.rem(row_id, SLOT_ROWS)
    first_slot = (row_id // SLOT_ROWS) * CAPACITY + 4 * in_brick
    for q in range(4):
        chosen = (slot == first_slot + q) & (in_brick < CAPACITY // 4)
        sel_ref[:, q * FIB : (q + 1) * FIB] = chosen.astype(F32).astype(BF16)

    def pack(values):
        blank = jnp.zeros((BINS, FIB), BF16)
        total = None
        for part in split(values):
            block = jnp.concatenate(
                [
                    jnp.concatenate([part if q == row else blank for q in range(4)], axis=1)
                    for row in range(4)
                ],
                axis=0,
            )
            term = dot_t(sel_ref[...], block)
            total = term if total is None else total + term
        return total.reshape(GROUPS, SLOT_ROWS, FIB)

    def exchange(source, target, slot_index):
        for df, de in PEERS:
            device = towards(df, 0, de)
            other = device["fib"] * N_EMG + device["emg"]
            pltpu.make_async_remote_copy(
                source.at[other], target.at[me], a2a_send.at[slot_index], a2a_recv.at[slot_index],
                device_id=device, device_id_type=MESH,
            ).start()
        target[me] = source[me]

    def exchange_wait(target, slot_index):
        whole = target.at[pl.ds(0, GROUPS - 1)]
        pltpu.make_async_copy(whole, whole, a2a_recv.at[slot_index]).wait()

    def exchange_sent(source, slot_index):
        whole = source.at[pl.ds(0, GROUPS - 1)]
        pltpu.make_async_copy(whole, whole, a2a_send.at[slot_index]).wait()

    cell_row = jnp.broadcast_to(cell_ref[...].astype(F32), (BINS, FIB))
    cell_send[...] = pack(cell_row)

    row_send[0] = pack(binned())

    middle = 0.5 * (high_bound + low_bound)
    spread_width = 0.5 * (high_bound - low_bound)
    ratio = middle / spread_width
    lane = iota((BY, BZ), 1)
    sub = iota((BY, BZ), 0)
    zlane = iota((8, WRAP * BY), 1)
    zsub = iota((8, WRAP * BY), 0)
    zrow = lax.rem(zlane, BY)

    def inside(condition):
        return jnp.where(condition, 1.0, 0.0).astype(F32)

    has_fib_up, has_fib_down = fib < N_FIB - 1, fib > 0
    has_len_up, has_len_down = shard < N_LEN - 1, shard > 0
    has_emg_up, has_emg_down = emg < N_EMG - 1, emg > 0
    fib_up, fib_down = inside(has_fib_up), inside(has_fib_down)
    len_up, len_down = inside(has_len_up), inside(has_len_down)
    emg_up, emg_down = inside(has_emg_up), inside(has_emg_down)
    margin = jnp.where(sub < 4, fib_up, fib_down)
    zmask = jnp.where(zsub < 4, emg_up, emg_down)
    zmask = zmask * jnp.where(zlane < 256, 1.0, jnp.where(zlane < 320, len_up, len_down))
    zmasks = (zmask, zmask * jnp.where(zrow < 4, fib_up, fib_down))

    def spread_out(kind, own):
        flat = own.reshape(BINS * BY, BZ)
        for tile in range(2):
            turned = flat[tile * BZ : (tile + 1) * BZ, :].T
            z_send[kind, 0, tile] = turned[:4]
            z_send[kind, 1, tile] = turned[BZ - 4 :]
        for f in range(2):
            for x in range(2):
                for k in range(2):
                    rows = own[x * (BINS - 2) + k, f * (BY - 2) : f * (BY - 2) + 2, :]
                    e_send[kind, f, x, 2 * k : 2 * k + 2, :] = rows
        for y in range(3):
            y_send[kind, 0, y * BINS : (y + 1) * BINS, :] = flat[pl.ds(y, BINS, stride=BY), :]
            y_send[kind, 1, y * BINS : (y + 1) * BINS, :] = flat[pl.ds(BY - 3 + y, BINS, stride=BY), :]

        for way in WAYS:
            source = margin_source(kind, flat, way)
            target = margin_target(kind, tuple(-step for step in way))
            copy = pltpu.make_async_remote_copy(
                source, target, halo_ssem.at[kind], halo_rsem.at[kind],
                device_id=towards(*way), device_id_type=MESH,
            )
            pl.when(exists(*way))(copy.start)

    def margin_source(kind, flat, way):
        df, dl, de = way
        if de:
            half = z_send.at[kind, max(de, 0)]
            return half.at[pl.ds(max(dl, 0), 1)] if dl else half
        if df and dl:
            return e_send.at[kind, max(df, 0), pl.ds(max(dl, 0), 1)]
        if df:
            return y_send.at[kind, max(df, 0)]
        return flat.at[pl.ds(0 if dl < 0 else (BINS - 3) * BY, 24)]

    def margin_target(kind, way):
        df, dl, de = way
        f, x = int(df < 0), int(dl < 0)
        if de:
            base = 12 * int(de < 0)
            if df and dl:
                return z_recv.at[kind, pl.ds(base + 8 + 2 * f + x, 1)]
            if dl:
                return z_recv.at[kind, pl.ds(base + 2 + x, 1)]
            return z_recv.at[kind, pl.ds(base + (4 + 2 * f if df else 0), 2)]
        if df and dl:
            return z_recv.at[kind, pl.ds(24 + 2 * f + x, 1)]
        if df:
            return wide_recv.at[kind, pl.ds(0 if df < 0 else 96, 96)]
        return wide_recv.at[kind, pl.ds(192 if dl < 0 else 216, 24)]

    at_edge = [
        (place == 0) | (place == size - 1)
        for place, size in ((fib, N_FIB), (shard, N_LEN), (emg, N_EMG))
    ]

    def margins_wait(kind, sem):
        for edges in itertools.product((False, True), repeat=3):
            ways = [
                way for way in WAYS
                if not any(edge and step < 0 for edge, step in zip(edges, way))
            ]
            tiles = sum(way_tiles(*way) for way in ways)
            here = [at == edge for at, edge in zip(at_edge, edges)]
            whole = count_ref.at[pl.ds(0, tiles)]
            copy = pltpu.make_async_copy(whole, whole, sem.at[kind])
            pl.when(here[0] & here[1] & here[2])(copy.wait)

    def assemble(kind, own, field, zfield, add):
        def only(condition, values):
            return jnp.where(condition, values, 0.0)

        def plus(values):
            return values + add if add else values

        wide, tiles = wide_recv.at[kind], z_recv.at[kind]
        margins_wait(kind, halo_rsem)
        field[0, pl.ds(0, BINS)] = plus(own[...])
        for k in range(3):
            field[0, BINS + k] = plus(only(has_len_up, wide[216 + 8 * k : 224 + 8 * k, :]))
            field[0, WRAP - 3 + k] = plus(only(has_len_down, wide[192 + 8 * k : 200 + 8 * k, :]))
        beside = field.at[1].reshape(WRAP * BY, BZ)
        for y in range(3):
            beside[pl.ds(y, BINS, stride=BY), :] = plus(only(has_fib_up, wide[96 + 32 * y : 128 + 32 * y, :]))
            beside[pl.ds(BY - 3 + y, BINS, stride=BY), :] = plus(only(has_fib_down, wide[32 * y : 32 * y + 32, :]))
        for f, along in enumerate((has_fib_up, has_fib_down)):
            for x, (place, weight) in enumerate(((BINS, has_len_up), (WRAP - 2, has_len_down))):
                for k in range(2):
                    rows = tiles[24 + 2 * f + x, 2 * k : 2 * k + 2, :]
                    field[1, place + k, f * (BY - 2) : f * (BY - 2) + 2, :] = plus(
                        only(along & weight, rows)
                    )
        low = iota((4, BZ), 1) < BZ // 2
        near = lax.rem(iota((4, BZ), 1), BY) < 4
        for half, weight in ((0, has_emg_up), (1, has_emg_down)):
            base = 12 * half
            rows = slice(4 * half, 4 * half + 4)
            for tile in range(2):
                lanes = slice(tile * BZ, (tile + 1) * BZ)
                zfield[0, rows, lanes] = plus(only(weight, tiles[base + tile]))
                up = only(has_fib_up, tiles[base + 4 + tile])
                down = only(has_fib_down, tiles[base + 6 + tile])
                zfield[1, rows, lanes] = plus(only(weight, jnp.where(near, up, down)))
            lanes = slice(2 * BZ, 3 * BZ)
            both = jnp.where(low, only(has_len_up, tiles[base + 2]), only(has_len_down, tiles[base + 3]))
            zfield[0, rows, lanes] = plus(only(weight, both))
            up = jnp.where(low, only(has_len_up, tiles[base + 8]), only(has_len_down, tiles[base + 9]))
            down = jnp.where(low, only(has_len_up, tiles[base + 10]), only(has_len_down, tiles[base + 11]))
            both = jnp.where(near, only(has_fib_up, up), only(has_fib_down, down))
            zfield[1, rows, lanes] = plus(only(weight, both))

    def scatter(step):
        exchange_wait(row_recv.at[step], 1 + step)
        rows = row_recv[step].reshape(packed, FIB)
        turned = rows.T
        wide = jnp.concatenate([turned[q * BINS : (q + 1) * BINS] for q in range(4)], axis=1)
        both = dot(jnp.concatenate(split(wide), axis=0), hot_ref[...])
        source = both[:BINS] + both[BINS:]
        flat = own_ref.at[step].reshape(BINS * BY, BZ)
        for y in range(BY):
            flat[pl.ds(y, BINS, stride=BY), :] = source[:, y * BZ : (y + 1) * BZ]

    weight = [1.0 / ratio]
    for _ in range(SWEEPS - 1):
        weight.append(1.0 / (2.0 * ratio - weight[-1]))

    def sweep(step, turn):
        first, last = turn == 0, turn == SWEEPS - 2
        keep = weight[turn + 1] * weight[turn]
        gain = 2.0 * weight[turn + 1] / spread_width
        scale = 1.0 / middle if first else 1.0
        field = r_ref.at[step] if first else d_ref.at[step]
        zfield = zr_ref.at[step] if first else zd_ref.at[step]
        blank = jnp.zeros((BZ - 16, BZ), F32)
        for tile in range(1 if last else 2):
            for block in range(2 if last or (turn and tile) else 3):
                z = zfield[tile, :, block * BZ : (block + 1) * BZ]
                first_lane = jnp.where(sub == 0, pltpu.roll(z, 1, 0), 0.0)
                last_lane = jnp.where(sub == 7, pltpu.roll(z, 7, 0), 0.0)
                turned = jnp.concatenate([first_lane, blank, last_lane], axis=0).T
                hz_ref[tile, pl.ds(16 * block, 16)] = turned.reshape(16, BY, BZ)

        def advance(here, beside, diagonal, rest, push):
            if first:
                rest = here - scale * (diagonal * here - beside)
            else:
                rest = rest - (diagonal * here - beside)
            return rest, (keep * scale) * here + push * rest

        if not last:
            zs = [zfield[0], zfield[1]]
            up = [pltpu.roll(z, 1, 1) for z in zs]
            down = [pltpu.roll(z, WRAP * BY - 1, 1) for z in zs]
            up_far = [pltpu.roll(z, WRAP * BY - BY + 1, 1) for z in zs]
            down_far = [pltpu.roll(z, BY - 1, 1) for z in zs]
            for t in range(1 if turn else 2):
                blocks = 2 if turn or t else 3
                width = blocks * BZ
                ends = []
                for block in range(blocks):
                    turned = field[t, pl.ds(16 * block, 16)].reshape(BZ, BZ).T
                    ends.append(
                        jnp.where(
                            sub == 0, pltpu.roll(turned[BZ - 8 :], 1, 0), pltpu.roll(turned[:8], 7, 0)
                        )
                    )
                edges = jnp.concatenate(ends, axis=1)
                beside = pltpu.roll(zs[t], BY, 1) + pltpu.roll(zs[t], WRAP * BY - BY, 1)
                beside = beside + jnp.where(zrow == 0, up_far[1 - t], up[t])
                beside = beside + jnp.where(zrow == BY - 1, down_far[1 - t], down[t])
                row, beside = zsub[:, :width], beside[:, :width]
                z = zs[t][:, :width]
                beside = beside + jnp.where(row == 0, edges, pltpu.roll(z, 1, 0))
                beside = beside + jnp.where(row == 7, edges, pltpu.roll(z, 7, 0))
                rest, after = advance(
                    z, beside, zt_ref[t, :, :width], None if first else zr_ref[step, t, :, :width],
                    gain * zmasks[t][:, :width],
                )
                zr_ref[step, t, :, :width] = rest
                zd_ref[step, t, :, :width] = after

        def slab(place, following, previous, push, own, tiles=2):
            here = (field[0, place], field[1, place])
            up = [pltpu.roll(h, 1, 0) for h in here]
            down = [pltpu.roll(h, BY - 1, 0) for h in here]
            for t in range(1 if last else tiles):
                beside = previous[t] + field[t, following] + hz_ref[t, place]
                beside = beside + jnp.where(sub == 0, up[1 - t], up[t])
                beside = beside + jnp.where(sub == BY - 1, down[1 - t], down[t])
                beside = beside + jnp.where(lane == 0, 0.0, pltpu.roll(here[t], 1, 1))
                beside = beside + jnp.where(lane == BZ - 1, 0.0, pltpu.roll(here[t], BZ - 1, 1))
                rest, after = advance(
                    here[t], beside, t_ref[t, place], None if first else r_ref[step, t, place],
                    push if t == 0 else push * margin,
                )
                if not last:
                    r_ref[step, t, place] = rest
                    d_ref[step, t, place] = after
                if own and t == 0:
                    if last:
                        pot_out[step, place] = x_ref[step, place] + after
                    elif first:
                        x_ref[step, place] = scale * here[0] + after
                    else:
                        x_ref[step, place] = x_ref[step, place] + after
            return here

        reach = SWEEPS - 2 - turn
        start = (WRAP - 1 - reach) % WRAP
        previous = (field[0, start], field[1, start])
        for k in range(reach):
            place = start + 1 + k
            tiles = 2 if k else 1
            previous = slab(place, (place + 1) % WRAP, previous, gain * len_down, False, tiles)
        previous = lax.fori_loop(
            0, BINS, lambda x, before: slab(x, x + 1, before, gain, True), previous, unroll=32
        )
        for k in range(reach):
            tiles = 2 if k + 1 < reach else 1
            previous = slab(BINS + k, BINS + k + 1, previous, gain * len_up, False, tiles)

    r_ref[...] = jnp.zeros_like(r_ref)
    d_ref[...] = jnp.zeros_like(d_ref)
    t_ref[...] = jnp.zeros_like(t_ref)
    lax.fori_loop(0, NODES // 2, next_pair, 0, unroll=8)
    pl.semaphore_wait(entered, N_FIB - 1)
    exchange(cell_send, cell_recv, 0)
    exchange(row_send.at[0], row_recv.at[0], 1)
    v1_ref[...] = cable_end(0, local)

    def second(node, _):
        drive = s_new[node] + gain_b[...] * v1_ref[pl.ds(node, 1), :]
        new = keep_ref[...] * s_work[node] + time_step * jnp.tanh(drive)
        s_in[node] = new
        cur_ref[pl.ds(node, 1), :] = jnp.sum(wts_b[...] * new, axis=0, keepdims=True)
        return 0

    lax.fori_loop(0, NODES, second, 0, unroll=8)
    row_send[1] = pack(binned())
    exchange(row_send.at[1], row_recv.at[1], 2)
    local = cable_begin(1, v1_ref[...])

    def put(node, _):
        pltpu.make_async_copy(
            s_in.at[node, pl.ds(0, STATES), :], states_out.at[:, node, :], out_sem.at[0]
        ).start()
        return 0

    lax.fori_loop(0, NODES, put, 0, unroll=16)

    exchange_wait(cell_recv, 0)
    cells = cell_recv[...].reshape(packed, FIB)
    for q in range(4):
        column_q = cells[:, q * BINS : q * BINS + 1].astype(jnp.int32)
        for y in range(BY):
            hot = (column_q == iota((packed, BZ), 1) + y * BZ).astype(F32).astype(BF16)
            hot_ref[q * packed : (q + 1) * packed, y * BZ : (y + 1) * BZ] = hot

    scatter(0)
    spread_out(0, own_ref.at[0])
    spread_out(STEPS, tissue_ref)
    exchange_sent(cell_send, 0)
    volt_out[...] = cable_end(1, local)
    scatter(1)
    spread_out(1, own_ref.at[1])
    def sent(step):
        exchange_sent(row_send.at[step], 1 + step)
        whole = ends_in.at[step, pl.ds(0, N_LEN - 1)]
        pltpu.make_async_copy(whole, whole, len_send.at[step]).wait()
        margins_wait(step, halo_ssem)

    for step in range(STEPS):
        if step == 0:
            assemble(STEPS, tissue_ref, t_ref, zt_ref, 6.0)
            margins_wait(STEPS, halo_ssem)
        else:
            pltpu.make_async_copy(states_out, states_out, out_sem.at[0]).wait()
            sent(0)
            sent(1)
        assemble(step, own_ref.at[step], r_ref.at[step], zr_ref.at[step], 0.0)
        for turn in range(SWEEPS - 1):
            sweep(step, turn)


def write_out(states, voltage, potential, states_out, voltage_out, potential_out, sem):
    cuts = [STATES * k // WRITES for k in range(WRITES + 1)]
    copies = [
        pltpu.make_async_copy(
            states.at[pl.ds(cuts[k], cuts[k + 1] - cuts[k])],
            states_out.at[pl.ds(cuts[k], cuts[k + 1] - cuts[k])],
            sem.at[k],
        )
        for k in range(WRITES)
    ]
    copies.append(pltpu.make_async_copy(potential, potential_out, sem.at[WRITES]))
    copies.append(pltpu.make_async_copy(voltage, voltage_out, sem.at[WRITES + 1]))
    for copy in copies:
        copy.start()
    for copy in copies:
        copy.wait()


def on_device(
    states, voltage, coupling, decay_rates, volt_gain, current_weights,
    fibre_home, cross_cell, motor_unit, stim_step, tissue,
):
    local, far = cable_tables()
    vmem = pl.BlockSpec(memory_space=pltpu.VMEM)
    hbm = pl.BlockSpec(memory_space=pltpu.HBM)
    outputs = pl.pallas_call(
        kernel,
        out_shape=(
            jax.ShapeDtypeStruct(states.shape, F32),
            jax.ShapeDtypeStruct(voltage.shape, F32),
            jax.ShapeDtypeStruct((STEPS, *tissue.shape), F32),
        ),
        in_specs=[hbm] * 13,
        out_specs=(vmem, vmem, vmem),
        scratch_shapes=[
            pltpu.VMEM(voltage.shape, F32),
            pltpu.VMEM(coupling.shape, F32),
            pltpu.VMEM((1, STATES), F32),
            pltpu.VMEM((1, STATES), F32),
            pltpu.VMEM((1, STATES), F32),
            pltpu.VMEM((1, FIB), jnp.int32),
            pltpu.VMEM((1, FIB), jnp.int32),
            pltpu.VMEM((1, FIB), jnp.int32),
            pltpu.VMEM((1, stim_step.shape[0]), jnp.int32),
            pltpu.VMEM(tissue.shape, F32),
            pltpu.VMEM(local.shape[1:], F32),
            pltpu.VMEM(far.shape[1:], F32),
            pltpu.VMEM((NODES, ROWS, FIB), F32),
            pltpu.VMEM((NODES, ROWS, FIB), F32),
            pltpu.VMEM((NODES, ROWS, FIB), F32),
            pltpu.VMEM((ROWS, 3 * ROWS), BF16),
            pltpu.VMEM((ROWS, FIB), F32),
            pltpu.VMEM((ROWS, FIB), F32),
            pltpu.VMEM((ROWS, FIB), F32),
            pltpu.VMEM((NODES, FIB), F32),
            pltpu.VMEM((NODES, FIB), F32),
            pltpu.VMEM((4 * GROUPS * SLOT_ROWS, BY * BZ), BF16),
            pltpu.VMEM((GROUPS * SLOT_ROWS, 4 * FIB), BF16),
            pltpu.VMEM((GROUPS, SLOT_ROWS, FIB), F32),
            pltpu.VMEM((GROUPS, SLOT_ROWS, FIB), F32),
            pltpu.VMEM((STEPS, GROUPS, SLOT_ROWS, FIB), F32),
            pltpu.VMEM((STEPS, GROUPS, SLOT_ROWS, FIB), F32),
            pltpu.VMEM((STEPS, 2, FIB), F32),
            pltpu.VMEM((STEPS, N_LEN, 2, FIB), F32),
            pltpu.VMEM((STEPS, BINS, BY, BZ), F32),
            pltpu.VMEM((STEPS, BINS, BY, BZ), F32),
            pltpu.VMEM((STEPS, 2, WRAP, BY, BZ), F32),
            pltpu.VMEM((STEPS, 2, WRAP, BY, BZ), F32),
            pltpu.VMEM((2, WRAP, BY, BZ), F32),
            pltpu.VMEM((STEPS, 2, 8, WRAP * BY), F32),
            pltpu.VMEM((STEPS, 2, 8, WRAP * BY), F32),
            pltpu.VMEM((2, 8, WRAP * BY), F32),
            pltpu.VMEM((2, WRAP, BY, BZ), F32),
            pltpu.VMEM((STEPS + 1, 2, 3 * BINS, BZ), F32),
            pltpu.VMEM((STEPS + 1, 2, 2, 4, BZ), F32),
            pltpu.VMEM((STEPS + 1, 2, 2, 4, BZ), F32),
            pltpu.VMEM((STEPS + 1, WIDE_ROWS, BZ), F32),
            pltpu.VMEM((STEPS + 1, TILES, 4, BZ), F32),
            pltpu.VMEM((WIDE_ROWS // 4 + TILES, 4, BZ), F32),
            pltpu.SemaphoreType.DMA((4,)),
            pltpu.SemaphoreType.DMA((1,)),
            pltpu.SemaphoreType.DMA((12,)),
            pltpu.SemaphoreType.DMA((3,)),
            pltpu.SemaphoreType.DMA((3,)),
            pltpu.SemaphoreType.DMA((STEPS,)),
            pltpu.SemaphoreType.DMA((STEPS,)),
            pltpu.SemaphoreType.DMA((STEPS + 1,)),
            pltpu.SemaphoreType.DMA((STEPS + 1,)),
            pltpu.SemaphoreType.REGULAR,
        ],
        compiler_params=pltpu.CompilerParams(collective_id=0, has_side_effects=True, vmem_limit_bytes=VMEM_LIMIT),
    )(*(pltpu.with_memory_space_constraint(array, pltpu.HBM) for array in (
        states, voltage, coupling, decay_rates.reshape(1, -1), volt_gain.reshape(1, -1),
        current_weights.reshape(1, -1), fibre_home.reshape(1, -1), cross_cell.reshape(1, -1),
        motor_unit.reshape(1, -1), stim_step.reshape(1, -1), tissue, local, far,
    )))
    return pl.pallas_call(
        write_out,
        out_shape=tuple(jax.ShapeDtypeStruct(array.shape, F32) for array in outputs),
        in_specs=[vmem] * 3,
        out_specs=(pl.BlockSpec(memory_space=pl.ANY),) * 3,
        scratch_shapes=[pltpu.SemaphoreType.DMA((WRITES + 2,))],
        compiler_params=pltpu.CompilerParams(vmem_limit_bytes=VMEM_LIMIT),
    )(*(pltpu.with_memory_space_constraint(array, pltpu.VMEM) for array in outputs))


def solution(mesh):
    return jax.shard_map(
        on_device,
        mesh=mesh,
        in_specs=(
            P(None, "len", ("fib", "emg")),
            P("len", ("fib", "emg")),
            P(),
            P(),
            P(),
            P(),
            P(("fib", "emg"), None),
            P(("fib", "emg")),
            P(("fib", "emg")),
            P(),
            P("len", "fib", "emg"),
        ),
        out_specs=(
            P(None, "len", ("fib", "emg")),
            P("len", ("fib", "emg")),
            P(None, "len", "fib", "emg"),
        ),
        check_vma=False,
    )
```

```python
import itertools
import math

import jax
import jax.numpy as jnp
import numpy as np
from jax import lax
from jax.experimental import pallas as pl
from jax.experimental.pallas import tpu as pltpu
from jax.sharding import PartitionSpec as P

STEPS = 2
SWEEPS = 4
NPC = 2

time_step = 0.5
conductance = 2000.0
amplitude = 200.0
band_half = 4
low_bound = 0.5
high_bound = 14.0

MESH = pl.DeviceIdType.MESH
HIGH = lax.Precision.HIGHEST
F32 = jnp.float32
BF16 = jnp.bfloat16

N_FIB, N_LEN, N_EMG = 8, 4, 4
GROUPS = N_FIB * N_EMG
STATES = 57
ROWS = 64
NODES = 64
FIB = 128
BINS = NODES // NPC
BY, BZ = 8, 128
SLOT_ROWS = 4
CAPACITY = 12
WIDE_ROWS = 240
TILES = 28
WRAP = 48
VMEM_LIMIT = 24 << 20
WRITES = 4


def hops(df, dl, de):
    rows = df % N_FIB
    return min(rows, N_FIB - rows) / 2 + min(dl % N_LEN, -dl % N_LEN) + min(de % N_EMG, -de % N_EMG)


WAYS = [(df, dl, de) for df in (-1, 0, 1) for dl in (-1, 0, 1) for de in (-1, 0, 1)]
WAYS = sorted((way for way in WAYS if any(way)), key=lambda way: -sum(map(abs, way)))


def way_tiles(df, dl, de):
    if de or (df and dl):
        return 1 if dl else 2
    return 24 if df else 6


PEERS = sorted(
    ((df, de) for df in range(N_FIB) for de in range(N_EMG) if (df, de) != (0, 0)),
    key=lambda peer: -hops(peer[0], 0, peer[1]),
)
AXIS_PEERS = sorted(
    [(step, 0, 0) for step in range(1, N_FIB)]
    + [(0, step, 0) for step in range(1, N_LEN)]
    + [(0, 0, step) for step in range(1, N_EMG)],
    key=lambda peer: -hops(*peer),
)


def cable_tables():
    total = NODES * N_LEN
    theta = math.acosh(1.0 + 0.5 / conductance)
    scale = conductance * math.sinh(theta) * math.sinh(total * theta)
    u = np.array([math.cosh((i + 0.5) * theta) for i in range(total)])
    v = np.array([math.cosh((total - 0.5 - i) * theta) / scale for i in range(total)])
    index = np.arange(NODES)
    local = np.zeros((N_LEN, NODES, NODES))
    ends = np.zeros((N_LEN, 2, NODES, FIB))
    for shard in range(N_LEN):
        us, vs = u[shard * NODES :][:NODES], v[shard * NODES :][:NODES]
        low = index[:, None] <= index[None, :]
        local[shard] = np.where(low, us[:, None] * vs[None, :], vs[:, None] * us[None, :])
        ends[shard] = np.stack([us, vs])[:, :, None]
    return jnp.asarray(local, F32), jnp.asarray(ends, F32)


def iota(shape, axis):
    return lax.broadcasted_iota(jnp.int32, shape, axis)


def split(values):
    high = values.astype(BF16)
    return high, (values - high.astype(F32)).astype(BF16)


def dot(a, b):
    return jnp.dot(a, b, preferred_element_type=F32)


def dot_high(a, b):
    return jnp.dot(a, b, preferred_element_type=F32, precision=HIGH)


def dot_t(a, b, precision=None):
    return lax.dot_general(
        a, b, (((1,), (1,)), ((), ())), preferred_element_type=F32, precision=precision
    )


def dot_tl(a, b, precision=None):
    return lax.dot_general(
        a, b, (((0,), (0,)), ((), ())), preferred_element_type=F32, precision=precision
    )


def kernel(
    states_hbm, volt_hbm, coup_hbm, decay_hbm, gain_hbm, wts_hbm, home_hbm, cell_hbm, mu_hbm,
    stim_hbm, tissue_hbm, local_hbm, far_hbm,
    states_out, volt_out, pot_out,
    volt_ref, coup_ref, decay_ref, gain_ref, wts_ref, home_ref, cell_ref, mu_ref,
    stim_ref, tissue_ref, local_ref, far_ref,
    s_in, s_work, s_new, lhs_ref, keep_ref, gain_b, wts_b, cur_ref, v1_ref, hot_ref, sel_ref,
    both_send, both_recv, row_send, row_recv, ends_out, ends_in,
    own_ref, x_ref, r_ref, d_ref, t_ref, zr_ref, zd_ref, zt_ref, hz_ref,
    y_send, z_send, e_send, wide_recv, z_recv, count_ref,
    in_sem, out_sem, small_sem, a2a_send, a2a_recv, len_send, len_recv, halo_ssem, halo_rsem, entered,
):
    fib, shard, emg = lax.axis_index("fib"), lax.axis_index("len"), lax.axis_index("emg")
    me = fib * N_EMG + emg

    smalls = [
        pltpu.make_async_copy(source, target, small_sem.at[number])
        for number, (source, target) in enumerate((
            (coup_hbm, coup_ref), (decay_hbm, decay_ref), (gain_hbm, gain_ref), (wts_hbm, wts_ref),
            (home_hbm, home_ref), (cell_hbm, cell_ref), (mu_hbm, mu_ref), (stim_hbm, stim_ref),
            (volt_hbm, volt_ref), (local_hbm.at[shard], local_ref), (far_hbm.at[shard], far_ref),
            (tissue_hbm, tissue_ref),
        ))
    ]
    for copy in smalls[:4] + smalls[8:9]:
        copy.start()
    barrier = pltpu.get_barrier_semaphore()

    def exists(df, dl, de):
        steps = ((fib + df, N_FIB), (shard + dl, N_LEN), (emg + de, N_EMG))
        inside = [(place >= 0) & (place < size) for place, size in steps]
        return inside[0] & inside[1] & inside[2]

    def towards(df, dl, de):
        return {
            "fib": lax.rem(fib + N_FIB + df, N_FIB),
            "len": lax.rem(shard + N_LEN + dl, N_LEN),
            "emg": lax.rem(emg + N_EMG + de, N_EMG),
        }

    for way in AXIS_PEERS:
        pl.semaphore_signal(barrier, inc=1, device_id=towards(*way), device_id_type=MESH)

    s_in[:, pl.ds(STATES, ROWS - STATES), :] = jnp.zeros((NODES, ROWS - STATES, FIB), F32)
    quarter = NODES // 4
    for part in range(4):

        def take(node, _, part=part):
            pltpu.make_async_copy(
                states_hbm.at[:, node, :], s_in.at[node, pl.ds(0, STATES), :], in_sem.at[part]
            ).start()
            return 0

        lax.fori_loop(part * quarter, (part + 1) * quarter, take, 0, unroll=16)
    for copy in smalls[4:8] + smalls[9:]:
        copy.start()

    def column(row):
        wide = row.shape[1]
        picked = jnp.where(iota((ROWS, wide), 0) == iota((ROWS, wide), 1), row, 0.0)
        return dot_high(picked, jnp.ones((wide, FIB), F32))

    for copy in smalls[:4]:
        copy.wait()
    keep_ref[...] = 1.0 - time_step * column(decay_ref[...])
    gain_b[...] = column(gain_ref[...])
    wts_b[...] = column(wts_ref[...])
    spread = (iota((STATES, 3 * ROWS), 0) == lax.rem(iota((STATES, 3 * ROWS), 1), ROWS)).astype(F32)
    tiled = dot_high(coup_ref[...], spread)
    tiled = jnp.concatenate([tiled, jnp.zeros((ROWS - STATES, 3 * ROWS), F32)], axis=0)
    high, low = split(tiled)
    lhs_ref[...] = jnp.where(iota((ROWS, 3 * ROWS), 1) < 2 * ROWS, high.astype(F32), low.astype(F32)).astype(BF16)


    def stacked(values):
        high, low = split(values)
        return jnp.concatenate([high, low, high], axis=0)

    def twice(values):
        return jnp.concatenate([values, values], axis=1)

    def first_pair(pair, _):
        node = 2 * pair
        old = jnp.concatenate([s_in[node], s_in[node + 1]], axis=1)
        volts = jnp.concatenate([volt_ref[pl.ds(node + k, 1), :] for k in range(2)], axis=1)
        gain = twice(gain_b[...])
        drive = dot(lhs_ref[...], stacked(old)) + gain * volts
        new = twice(keep_ref[...]) * old + time_step * jnp.tanh(drive)
        for k in range(2):
            part = new[:, k * FIB : (k + 1) * FIB]
            s_work[node + k] = part
            cur_ref[pl.ds(node + k, 1), :] = jnp.sum(wts_b[...] * part, axis=0, keepdims=True)
        return 0

    def next_pair(pair, _):
        node = 2 * pair
        new = jnp.concatenate([s_work[node], s_work[node + 1]], axis=1)
        after = dot(lhs_ref[...], stacked(new))
        for k in range(2):
            s_new[node + k] = after[:, k * FIB : (k + 1) * FIB]
        return 0

    smalls[8].wait()

    for part in range(4):
        block = s_in.at[pl.ds(part * quarter, quarter), pl.ds(0, STATES), :]
        pltpu.make_async_copy(block, block, in_sem.at[part]).wait()
        lax.fori_loop(part * (quarter // 2), (part + 1) * (quarter // 2), first_pair, 0, unroll=8)

    for copy in smalls[4:8] + smalls[9:]:
        copy.wait()
    unit_hot = (iota((FIB, FIB), 0) == mu_ref[...]).astype(F32)
    stim_row = jnp.concatenate(
        [stim_ref[...].astype(F32), jnp.zeros((1, FIB - stim_ref.shape[1]), F32)], axis=1
    )
    fire = dot(stim_row.astype(BF16), unit_hot.astype(BF16))

    pl.semaphore_wait(barrier, len(AXIS_PEERS))
    node_id = shard * NODES + iota((NODES, FIB), 0)
    total_nodes = NODES * N_LEN
    band = (node_id >= total_nodes // 2 - band_half) & (node_id < total_nodes // 2 + band_half)

    def cable_begin(step, volts):
        active = (fire == float(step)).astype(F32)
        pulse = jnp.where(band, amplitude * active, 0.0)
        right = volts + time_step * (pulse - cur_ref[...])
        ends_out[step, 0:1, :] = jnp.sum(far_ref[0] * right, axis=0, keepdims=True)
        ends_out[step, 1:2, :] = jnp.sum(far_ref[1] * right, axis=0, keepdims=True)
        for other_step in range(1, N_LEN):
            other = lax.rem(shard + other_step, N_LEN)
            pltpu.make_async_remote_copy(
                ends_out.at[step], ends_in.at[step, shard], len_send.at[step], len_recv.at[step],
                device_id={"fib": fib, "len": other, "emg": emg}, device_id_type=MESH,
            ).start()
        return dot_high(local_ref[...], right)

    def cable_end(step, local):
        whole = ends_in.at[step, pl.ds(0, N_LEN - 1)]
        pltpu.make_async_copy(whole, whole, len_recv.at[step]).wait()
        below = above = jnp.zeros((1, FIB), F32)
        for other in range(N_LEN):
            below = below + jnp.where(other < shard, ends_in[step, other, 0:1, :], 0.0)
            above = above + jnp.where(other > shard, ends_in[step, other, 1:2, :], 0.0)
        return local + far_ref[1] * below + far_ref[0] * above

    def binned():
        first = cur_ref[pl.ds(0, BINS, stride=2), :]
        second = cur_ref[pl.ds(1, BINS, stride=2), :]
        return first + second

    local = cable_begin(0, volt_ref[...])
    for df in range(1, N_FIB):
        pl.semaphore_signal(entered, inc=1, device_id=towards(df, 0, 0), device_id_type=MESH)
    home = home_ref[...]
    member = (iota((GROUPS, FIB), 0) == home).astype(F32)
    before = (iota((FIB, FIB), 0) < iota((FIB, FIB), 1)).astype(BF16)
    earlier = dot(member.astype(BF16), before)
    rank = jnp.sum(earlier * member, axis=0, keepdims=True).astype(jnp.int32)
    slot = home * CAPACITY + rank
    packed = GROUPS * SLOT_ROWS
    row_id = iota((packed, FIB), 0)
    in_brick = lax.rem(row_id, SLOT_ROWS)
    first_slot = (row_id // SLOT_ROWS) * CAPACITY + 4 * in_brick
    for q in range(4):
        chosen = (slot == first_slot + q) & (in_brick < CAPACITY // 4)
        sel_ref[:, q * FIB : (q + 1) * FIB] = chosen.astype(F32).astype(BF16)

    def pack(values):
        blank = jnp.zeros((BINS, FIB), BF16)
        total = None
        for part in split(values):
            block = jnp.concatenate(
                [
                    jnp.concatenate([part if q == row else blank for q in range(4)], axis=1)
                    for row in range(4)
                ],
                axis=0,
            )
            term = dot_t(sel_ref[...], block)
            total = term if total is None else total + term
        return total.reshape(GROUPS, SLOT_ROWS, FIB)

    def exchange(source, target, slot_index):
        for df, de in PEERS:
            device = towards(df, 0, de)
            other = device["fib"] * N_EMG + device["emg"]
            pltpu.make_async_remote_copy(
                source.at[other], target.at[me], a2a_send.at[slot_index], a2a_recv.at[slot_index],
                device_id=device, device_id_type=MESH,
            ).start()
        target[me] = source[me]

    def exchange_wait(target, slot_index):
        whole = target.at[pl.ds(0, GROUPS - 1)]
        pltpu.make_async_copy(whole, whole, a2a_recv.at[slot_index]).wait()

    def exchange_sent(source, slot_index):
        whole = source.at[pl.ds(0, GROUPS - 1)]
        pltpu.make_async_copy(whole, whole, a2a_send.at[slot_index]).wait()

    cell_row = jnp.broadcast_to(cell_ref[...].astype(F32), (BINS, FIB))
    both_send[:, SLOT_ROWS:, :] = pack(cell_row)

    both_send[:, :SLOT_ROWS, :] = pack(binned())

    middle = 0.5 * (high_bound + low_bound)
    spread_width = 0.5 * (high_bound - low_bound)
    ratio = middle / spread_width
    lane = iota((BY, BZ), 1)
    sub = iota((BY, BZ), 0)
    zlane = iota((8, WRAP * BY), 1)
    zsub = iota((8, WRAP * BY), 0)
    zrow = lax.rem(zlane, BY)

    def inside(condition):
        return jnp.where(condition, 1.0, 0.0).astype(F32)

    has_fib_up, has_fib_down = fib < N_FIB - 1, fib > 0
    has_len_up, has_len_down = shard < N_LEN - 1, shard > 0
    has_emg_up, has_emg_down = emg < N_EMG - 1, emg > 0
    fib_up, fib_down = inside(has_fib_up), inside(has_fib_down)
    len_up, len_down = inside(has_len_up), inside(has_len_down)
    emg_up, emg_down = inside(has_emg_up), inside(has_emg_down)
    margin = jnp.where(sub < 4, fib_up, fib_down)
    zmask = jnp.where(zsub < 4, emg_up, emg_down)
    zmask = zmask * jnp.where(zlane < 256, 1.0, jnp.where(zlane < 320, len_up, len_down))
    zmasks = (zmask, zmask * jnp.where(zrow < 4, fib_up, fib_down))

    def spread_out(kind, own):
        flat = own.reshape(BINS * BY, BZ)
        for tile in range(2):
            turned = flat[tile * BZ : (tile + 1) * BZ, :].T
            z_send[kind, 0, tile] = turned[:4]
            z_send[kind, 1, tile] = turned[BZ - 4 :]
        for f in range(2):
            for x in range(2):
                for k in range(2):
                    rows = own[x * (BINS - 2) + k, f * (BY - 2) : f * (BY - 2) + 2, :]
                    e_send[kind, f, x, 2 * k : 2 * k + 2, :] = rows
        for y in range(3):
            y_send[kind, 0, y * BINS : (y + 1) * BINS, :] = flat[pl.ds(y, BINS, stride=BY), :]
            y_send[kind, 1, y * BINS : (y + 1) * BINS, :] = flat[pl.ds(BY - 3 + y, BINS, stride=BY), :]

        for way in WAYS:
            source = margin_source(kind, flat, way)
            target = margin_target(kind, tuple(-step for step in way))
            copy = pltpu.make_async_remote_copy(
                source, target, halo_ssem.at[kind], halo_rsem.at[kind],
                device_id=towards(*way), device_id_type=MESH,
            )
            pl.when(exists(*way))(copy.start)

    def margin_source(kind, flat, way):
        df, dl, de = way
        if de:
            half = z_send.at[kind, max(de, 0)]
            return half.at[pl.ds(max(dl, 0), 1)] if dl else half
        if df and dl:
            return e_send.at[kind, max(df, 0), pl.ds(max(dl, 0), 1)]
        if df:
            return y_send.at[kind, max(df, 0)]
        return flat.at[pl.ds(0 if dl < 0 else (BINS - 3) * BY, 24)]

    def margin_target(kind, way):
        df, dl, de = way
        f, x = int(df < 0), int(dl < 0)
        if de:
            base = 12 * int(de < 0)
            if df and dl:
                return z_recv.at[kind, pl.ds(base + 8 + 2 * f + x, 1)]
            if dl:
                return z_recv.at[kind, pl.ds(base + 2 + x, 1)]
            return z_recv.at[kind, pl.ds(base + (4 + 2 * f if df else 0), 2)]
        if df and dl:
            return z_recv.at[kind, pl.ds(24 + 2 * f + x, 1)]
        if df:
            return wide_recv.at[kind, pl.ds(0 if df < 0 else 96, 96)]
        return wide_recv.at[kind, pl.ds(192 if dl < 0 else 216, 24)]

    at_edge = [
        (place == 0) | (place == size - 1)
        for place, size in ((fib, N_FIB), (shard, N_LEN), (emg, N_EMG))
    ]

    def margins_wait(kind, sem):
        for edges in itertools.product((False, True), repeat=3):
            ways = [
                way for way in WAYS
                if not any(edge and step < 0 for edge, step in zip(edges, way))
            ]
            tiles = sum(way_tiles(*way) for way in ways)
            here = [at == edge for at, edge in zip(at_edge, edges)]
            whole = count_ref.at[pl.ds(0, tiles)]
            copy = pltpu.make_async_copy(whole, whole, sem.at[kind])
            pl.when(here[0] & here[1] & here[2])(copy.wait)

    def assemble(kind, own, field, zfield, add):
        def only(condition, values):
            return jnp.where(condition, values, 0.0)

        def plus(values):
            return values + add if add else values

        wide, tiles = wide_recv.at[kind], z_recv.at[kind]
        margins_wait(kind, halo_rsem)
        field[0, pl.ds(0, BINS)] = plus(own[...])
        for k in range(3):
            field[0, BINS + k] = plus(only(has_len_up, wide[216 + 8 * k : 224 + 8 * k, :]))
            field[0, WRAP - 3 + k] = plus(only(has_len_down, wide[192 + 8 * k : 200 + 8 * k, :]))
        beside = field.at[1].reshape(WRAP * BY, BZ)
        for y in range(3):
            beside[pl.ds(y, BINS, stride=BY), :] = plus(only(has_fib_up, wide[96 + 32 * y : 128 + 32 * y, :]))
            beside[pl.ds(BY - 3 + y, BINS, stride=BY), :] = plus(only(has_fib_down, wide[32 * y : 32 * y + 32, :]))
        for f, along in enumerate((has_fib_up, has_fib_down)):
            for x, (place, weight) in enumerate(((BINS, has_len_up), (WRAP - 2, has_len_down))):
                for k in range(2):
                    rows = tiles[24 + 2 * f + x, 2 * k : 2 * k + 2, :]
                    field[1, place + k, f * (BY - 2) : f * (BY - 2) + 2, :] = plus(
                        only(along & weight, rows)
                    )
        low = iota((4, BZ), 1) < BZ // 2
        near = lax.rem(iota((4, BZ), 1), BY) < 4
        for half, weight in ((0, has_emg_up), (1, has_emg_down)):
            base = 12 * half
            rows = slice(4 * half, 4 * half + 4)
            for tile in range(2):
                lanes = slice(tile * BZ, (tile + 1) * BZ)
                zfield[0, rows, lanes] = plus(only(weight, tiles[base + tile]))
                up = only(has_fib_up, tiles[base + 4 + tile])
                down = only(has_fib_down, tiles[base + 6 + tile])
                zfield[1, rows, lanes] = plus(only(weight, jnp.where(near, up, down)))
            lanes = slice(2 * BZ, 3 * BZ)
            both = jnp.where(low, only(has_len_up, tiles[base + 2]), only(has_len_down, tiles[base + 3]))
            zfield[0, rows, lanes] = plus(only(weight, both))
            up = jnp.where(low, only(has_len_up, tiles[base + 8]), only(has_len_down, tiles[base + 9]))
            down = jnp.where(low, only(has_len_up, tiles[base + 10]), only(has_len_down, tiles[base + 11]))
            both = jnp.where(near, only(has_fib_up, up), only(has_fib_down, down))
            zfield[1, rows, lanes] = plus(only(weight, both))

    def scatter(step):
        if step:
            exchange_wait(row_recv, 1)
        rows = row_recv[...] if step else both_recv[:, :SLOT_ROWS, :]
        rows = rows.reshape(packed, FIB)
        turned = rows.T
        wide = jnp.concatenate([turned[q * BINS : (q + 1) * BINS] for q in range(4)], axis=1)
        both = dot(jnp.concatenate(split(wide), axis=0), hot_ref[...])
        source = both[:BINS] + both[BINS:]
        flat = own_ref.at[step].reshape(BINS * BY, BZ)
        for y in range(BY):
            flat[pl.ds(y, BINS, stride=BY), :] = source[:, y * BZ : (y + 1) * BZ]

    weight = [1.0 / ratio]
    for _ in range(SWEEPS - 1):
        weight.append(1.0 / (2.0 * ratio - weight[-1]))

    def sweep(step, turn):
        first, last = turn == 0, turn == SWEEPS - 2
        keep = weight[turn + 1] * weight[turn]
        gain = 2.0 * weight[turn + 1] / spread_width
        scale = 1.0 / middle if first else 1.0
        field = r_ref.at[step] if first else d_ref.at[step]
        zfield = zr_ref.at[step] if first else zd_ref.at[step]
        blank = jnp.zeros((BZ - 16, BZ), F32)
        for tile in range(1 if last else 2):
            for block in range(2 if last or (turn and tile) else 3):
                z = zfield[tile, :, block * BZ : (block + 1) * BZ]
                first_lane = jnp.where(sub == 0, pltpu.roll(z, 1, 0), 0.0)
                last_lane = jnp.where(sub == 7, pltpu.roll(z, 7, 0), 0.0)
                turned = jnp.concatenate([first_lane, blank, last_lane], axis=0).T
                hz_ref[tile, pl.ds(16 * block, 16)] = turned.reshape(16, BY, BZ)

        def advance(here, beside, diagonal, rest, push):
            if first:
                rest = here - scale * (diagonal * here - beside)
            else:
                rest = rest - (diagonal * here - beside)
            return rest, (keep * scale) * here + push * rest

        if not last:
            zs = [zfield[0], zfield[1]]
            up = [pltpu.roll(z, 1, 1) for z in zs]
            down = [pltpu.roll(z, WRAP * BY - 1, 1) for z in zs]
            up_far = [pltpu.roll(z, WRAP * BY - BY + 1, 1) for z in zs]
            down_far = [pltpu.roll(z, BY - 1, 1) for z in zs]
            for t in range(1 if turn else 2):
                blocks = 2 if turn or t else 3
                width = blocks * BZ
                ends = []
                for block in range(blocks):
                    turned = field[t, pl.ds(16 * block, 16)].reshape(BZ, BZ).T
                    ends.append(
                        jnp.where(
                            sub == 0, pltpu.roll(turned[BZ - 8 :], 1, 0), pltpu.roll(turned[:8], 7, 0)
                        )
                    )
                edges = jnp.concatenate(ends, axis=1)
                beside = pltpu.roll(zs[t], BY, 1) + pltpu.roll(zs[t], WRAP * BY - BY, 1)
                beside = beside + jnp.where(zrow == 0, up_far[1 - t], up[t])
                beside = beside + jnp.where(zrow == BY - 1, down_far[1 - t], down[t])
                row, beside = zsub[:, :width], beside[:, :width]
                z = zs[t][:, :width]
                beside = beside + jnp.where(row == 0, edges, pltpu.roll(z, 1, 0))
                beside = beside + jnp.where(row == 7, edges, pltpu.roll(z, 7, 0))
                rest, after = advance(
                    z, beside, zt_ref[t, :, :width], None if first else zr_ref[step, t, :, :width],
                    gain * zmasks[t][:, :width],
                )
                zr_ref[step, t, :, :width] = rest
                zd_ref[step, t, :, :width] = after

        def slab(place, following, previous, push, own, tiles=2):
            here = (field[0, place], field[1, place])
            up = [pltpu.roll(h, 1, 0) for h in here]
            down = [pltpu.roll(h, BY - 1, 0) for h in here]
            for t in range(1 if last else tiles):
                beside = previous[t] + field[t, following] + hz_ref[t, place]
                beside = beside + jnp.where(sub == 0, up[1 - t], up[t])
                beside = beside + jnp.where(sub == BY - 1, down[1 - t], down[t])
                beside = beside + jnp.where(lane == 0, 0.0, pltpu.roll(here[t], 1, 1))
                beside = beside + jnp.where(lane == BZ - 1, 0.0, pltpu.roll(here[t], BZ - 1, 1))
                rest, after = advance(
                    here[t], beside, t_ref[t, place], None if first else r_ref[step, t, place],
                    push if t == 0 else push * margin,
                )
                if not last:
                    r_ref[step, t, place] = rest
                    d_ref[step, t, place] = after
                if own and t == 0:
                    if last:
                        pot_out[step, place] = x_ref[step, place] + after
                    elif first:
                        x_ref[step, place] = scale * here[0] + after
                    else:
                        x_ref[step, place] = x_ref[step, place] + after
            return here

        reach = SWEEPS - 2 - turn
        start = (WRAP - 1 - reach) % WRAP
        previous = (field[0, start], field[1, start])
        for k in range(reach):
            place = start + 1 + k
            tiles = 2 if k else 1
            previous = slab(place, (place + 1) % WRAP, previous, gain * len_down, False, tiles)
        previous = lax.fori_loop(
            0, BINS, lambda x, before: slab(x, x + 1, before, gain, True), previous, unroll=32
        )
        for k in range(reach):
            tiles = 2 if k + 1 < reach else 1
            previous = slab(BINS + k, BINS + k + 1, previous, gain * len_up, False, tiles)

    r_ref[...] = jnp.zeros_like(r_ref)
    d_ref[...] = jnp.zeros_like(d_ref)
    t_ref[...] = jnp.zeros_like(t_ref)
    lax.fori_loop(0, NODES // 2, next_pair, 0, unroll=8)
    pl.semaphore_wait(entered, N_FIB - 1)
    exchange(both_send, both_recv, 0)
    v1_ref[...] = cable_end(0, local)

    def second(node, _):
        drive = s_new[node] + gain_b[...] * v1_ref[pl.ds(node, 1), :]
        new = keep_ref[...] * s_work[node] + time_step * jnp.tanh(drive)
        s_in[node] = new
        cur_ref[pl.ds(node, 1), :] = jnp.sum(wts_b[...] * new, axis=0, keepdims=True)
        return 0

    lax.fori_loop(0, NODES, second, 0, unroll=8)
    row_send[...] = pack(binned())
    exchange(row_send, row_recv, 1)
    local = cable_begin(1, v1_ref[...])

    def put(node, _):
        pltpu.make_async_copy(
            s_in.at[node, pl.ds(0, STATES), :], states_out.at[:, node, :], out_sem.at[0]
        ).start()
        return 0

    lax.fori_loop(0, NODES, put, 0, unroll=16)

    exchange_wait(both_recv, 0)
    cells = both_recv[:, SLOT_ROWS:, :].reshape(packed, FIB)
    for q in range(4):
        column_q = cells[:, q * BINS : q * BINS + 1].astype(jnp.int32)
        for y in range(BY):
            hot = (column_q == iota((packed, BZ), 1) + y * BZ).astype(F32).astype(BF16)
            hot_ref[q * packed : (q + 1) * packed, y * BZ : (y + 1) * BZ] = hot

    scatter(0)
    spread_out(0, own_ref.at[0])
    spread_out(STEPS, tissue_ref)
    volt_out[...] = cable_end(1, local)
    scatter(1)
    spread_out(1, own_ref.at[1])
    def sent(step):
        exchange_sent(row_send if step else both_send, step)
        whole = ends_in.at[step, pl.ds(0, N_LEN - 1)]
        pltpu.make_async_copy(whole, whole, len_send.at[step]).wait()
        margins_wait(step, halo_ssem)

    for step in range(STEPS):
        if step == 0:
            assemble(STEPS, tissue_ref, t_ref, zt_ref, 6.0)
            margins_wait(STEPS, halo_ssem)
        else:
            pltpu.make_async_copy(states_out, states_out, out_sem.at[0]).wait()
            sent(0)
            sent(1)
        assemble(step, own_ref.at[step], r_ref.at[step], zr_ref.at[step], 0.0)
        for turn in range(SWEEPS - 1):
            sweep(step, turn)


def write_out(states, voltage, potential, states_out, voltage_out, potential_out, sem):
    cuts = [STATES * k // WRITES for k in range(WRITES + 1)]
    copies = [
        pltpu.make_async_copy(
            states.at[pl.ds(cuts[k], cuts[k + 1] - cuts[k])],
            states_out.at[pl.ds(cuts[k], cuts[k + 1] - cuts[k])],
            sem.at[k],
        )
        for k in range(WRITES)
    ]
    copies.append(pltpu.make_async_copy(potential, potential_out, sem.at[WRITES]))
    copies.append(pltpu.make_async_copy(voltage, voltage_out, sem.at[WRITES + 1]))
    for copy in copies:
        copy.start()
    for copy in copies:
        copy.wait()


def on_device(
    states, voltage, coupling, decay_rates, volt_gain, current_weights,
    fibre_home, cross_cell, motor_unit, stim_step, tissue,
):
    local, far = cable_tables()
    vmem = pl.BlockSpec(memory_space=pltpu.VMEM)
    hbm = pl.BlockSpec(memory_space=pltpu.HBM)
    outputs = pl.pallas_call(
        kernel,
        out_shape=(
            jax.ShapeDtypeStruct(states.shape, F32),
            jax.ShapeDtypeStruct(voltage.shape, F32),
            jax.ShapeDtypeStruct((STEPS, *tissue.shape), F32),
        ),
        in_specs=[hbm] * 13,
        out_specs=(vmem, vmem, vmem),
        scratch_shapes=[
            pltpu.VMEM(voltage.shape, F32),
            pltpu.VMEM(coupling.shape, F32),
            pltpu.VMEM((1, STATES), F32),
            pltpu.VMEM((1, STATES), F32),
            pltpu.VMEM((1, STATES), F32),
            pltpu.VMEM((1, FIB), jnp.int32),
            pltpu.VMEM((1, FIB), jnp.int32),
            pltpu.VMEM((1, FIB), jnp.int32),
            pltpu.VMEM((1, stim_step.shape[0]), jnp.int32),
            pltpu.VMEM(tissue.shape, F32),
            pltpu.VMEM(local.shape[1:], F32),
            pltpu.VMEM(far.shape[1:], F32),
            pltpu.VMEM((NODES, ROWS, FIB), F32),
            pltpu.VMEM((NODES, ROWS, FIB), F32),
            pltpu.VMEM((NODES, ROWS, FIB), F32),
            pltpu.VMEM((ROWS, 3 * ROWS), BF16),
            pltpu.VMEM((ROWS, FIB), F32),
            pltpu.VMEM((ROWS, FIB), F32),
            pltpu.VMEM((ROWS, FIB), F32),
            pltpu.VMEM((NODES, FIB), F32),
            pltpu.VMEM((NODES, FIB), F32),
            pltpu.VMEM((4 * GROUPS * SLOT_ROWS, BY * BZ), BF16),
            pltpu.VMEM((GROUPS * SLOT_ROWS, 4 * FIB), BF16),
            pltpu.VMEM((GROUPS, 2 * SLOT_ROWS, FIB), F32),
            pltpu.VMEM((GROUPS, 2 * SLOT_ROWS, FIB), F32),
            pltpu.VMEM((GROUPS, SLOT_ROWS, FIB), F32),
            pltpu.VMEM((GROUPS, SLOT_ROWS, FIB), F32),
            pltpu.VMEM((STEPS, 2, FIB), F32),
            pltpu.VMEM((STEPS, N_LEN, 2, FIB), F32),
            pltpu.VMEM((STEPS, BINS, BY, BZ), F32),
            pltpu.VMEM((STEPS, BINS, BY, BZ), F32),
            pltpu.VMEM((STEPS, 2, WRAP, BY, BZ), F32),
            pltpu.VMEM((STEPS, 2, WRAP, BY, BZ), F32),
            pltpu.VMEM((2, WRAP, BY, BZ), F32),
            pltpu.VMEM((STEPS, 2, 8, WRAP * BY), F32),
            pltpu.VMEM((STEPS, 2, 8, WRAP * BY), F32),
            pltpu.VMEM((2, 8, WRAP * BY), F32),
            pltpu.VMEM((2, WRAP, BY, BZ), F32),
            pltpu.VMEM((STEPS + 1, 2, 3 * BINS, BZ), F32),
            pltpu.VMEM((STEPS + 1, 2, 2, 4, BZ), F32),
            pltpu.VMEM((STEPS + 1, 2, 2, 4, BZ), F32),
            pltpu.VMEM((STEPS + 1, WIDE_ROWS, BZ), F32),
            pltpu.VMEM((STEPS + 1, TILES, 4, BZ), F32),
            pltpu.VMEM((WIDE_ROWS // 4 + TILES, 4, BZ), F32),
            pltpu.SemaphoreType.DMA((4,)),
            pltpu.SemaphoreType.DMA((1,)),
            pltpu.SemaphoreType.DMA((12,)),
            pltpu.SemaphoreType.DMA((STEPS,)),
            pltpu.SemaphoreType.DMA((STEPS,)),
            pltpu.SemaphoreType.DMA((STEPS,)),
            pltpu.SemaphoreType.DMA((STEPS,)),
            pltpu.SemaphoreType.DMA((STEPS + 1,)),
            pltpu.SemaphoreType.DMA((STEPS + 1,)),
            pltpu.SemaphoreType.REGULAR,
        ],
        compiler_params=pltpu.CompilerParams(collective_id=0, has_side_effects=True, vmem_limit_bytes=VMEM_LIMIT),
    )(*(pltpu.with_memory_space_constraint(array, pltpu.HBM) for array in (
        states, voltage, coupling, decay_rates.reshape(1, -1), volt_gain.reshape(1, -1),
        current_weights.reshape(1, -1), fibre_home.reshape(1, -1), cross_cell.reshape(1, -1),
        motor_unit.reshape(1, -1), stim_step.reshape(1, -1), tissue, local, far,
    )))
    return pl.pallas_call(
        write_out,
        out_shape=tuple(jax.ShapeDtypeStruct(array.shape, F32) for array in outputs),
        in_specs=[vmem] * 3,
        out_specs=(pl.BlockSpec(memory_space=pl.ANY),) * 3,
        scratch_shapes=[pltpu.SemaphoreType.DMA((WRITES + 2,))],
        compiler_params=pltpu.CompilerParams(vmem_limit_bytes=VMEM_LIMIT),
    )(*(pltpu.with_memory_space_constraint(array, pltpu.VMEM) for array in outputs))


def solution(mesh):
    return jax.shard_map(
        on_device,
        mesh=mesh,
        in_specs=(
            P(None, "len", ("fib", "emg")),
            P("len", ("fib", "emg")),
            P(),
            P(),
            P(),
            P(),
            P(("fib", "emg"), None),
            P(("fib", "emg")),
            P(("fib", "emg")),
            P(),
            P("len", "fib", "emg"),
        ),
        out_specs=(
            P(None, "len", ("fib", "emg")),
            P("len", ("fib", "emg")),
            P(None, "len", "fib", "emg"),
        ),
        check_vma=False,
    )
```
